128 devices in a mesh: gx: 8 (over x_hi, z), gy: 4 (over x_lo, core), gz: 4 (over y).
Axes of the slice: x: 4 (x_hi: 2, x_lo: 2; x = x_hi * 2 + x_lo), y: 4, z: 4, core: 2. Of those that a mesh axis runs over, the one named last changes fastest.
Arguments:
- panel: float32 [128, 524288], P(None, ('gx', 'gy', 'gz')), may hold values from -3000 to 3000
- trailing: float32 [64, 524288], P(None, ('gx', 'gy', 'gz')), may hold values from -6 to 6
Outputs:
- basis: float32 [128, 524288], P(None, ('gx', 'gy', 'gz'))
- upper: float32 [128, 128], replicated
- coupling: float32 [128, 64], replicated
- updated: float32 [64, 524288], P(None, ('gx', 'gy', 'gz'))
The draws below stay inside these ranges and needn't reach their ends.
All inputs are finite; a program needn't handle non-finite values.
Results may differ from the reference program's by a relative error of at most 0.0033.
Values sent between devices are 32-bit elements; how exact they have to be, the bound alone decides.
No kernel may reach another device: no remote copies, remote signals or barrier semaphores. Data moves between devices by JAX's collectives and lax.ppermute only.
A program may use at most 64 MiB of HBM per device.

```python
import jax
import jax.numpy as jnp
from jax import lax

P_SIZE = 128
TRAIL = 64
ROWS = 524288


def draw_panel(key, part):
    k_base, k_cols, k_rows, k_left, k_right, k_sing = jax.random.split(jax.random.fold_in(key, 17), 6)
    left_turn, _ = jnp.linalg.qr(jax.random.normal(k_left, (P_SIZE, P_SIZE), jnp.float32))
    right_turn, _ = jnp.linalg.qr(jax.random.normal(k_right, (P_SIZE, P_SIZE), jnp.float32))
    spread = jnp.log(500.0)
    place = jnp.arange(P_SIZE, dtype=jnp.int32)
    base = jax.random.truncated_normal(k_base, -4.0, 4.0, (P_SIZE, ROWS), jnp.float32)
    cols = jnp.exp(jax.random.uniform(k_cols, (P_SIZE, 1), jnp.float32, 0.0, jnp.log(10.0)))
    level = jax.random.uniform(k_sing, (P_SIZE,), jnp.float32, 0.0, 1.0)
    level = jnp.where(place == 0, 0.0, jnp.where(place == 1, 1.0, level))
    singular = jnp.exp(-spread * level)
    mixing = jnp.dot(left_turn * singular[None, :], right_turn, precision=lax.Precision.HIGHEST)
    mixed = 3.5 * jnp.dot(mixing, base, precision=lax.Precision.HIGHEST)
    rising = 1.0 + 2.0 * jnp.arange(ROWS, dtype=jnp.float32)[None, :] / ROWS
    rows = jnp.exp(jax.random.uniform(k_rows, (1, ROWS), jnp.float32, 0.0, jnp.log(10.0))) * rising
    return jnp.clip(mixed * cols * rows, -3000.0, 3000.0)


def block_levels(stream_key, shape, cuts, low, high):
    def one(axis_at, blocks):
        draws = jax.random.uniform(jax.random.fold_in(jax.random.fold_in(stream_key, 6), axis_at), (blocks,), jnp.float32, low / len(cuts), high / len(cuts))
        return jnp.repeat(jnp.exp(draws), shape[axis_at] // blocks).reshape((-1,) + (1,) * (len(shape) - axis_at - 1))

    level = one(*cuts[0])
    for cut in cuts[1:]:
        level = level * one(*cut)
    return level


def normal_values(stream_key, dims, scale, limit, cuts=(), kind=jnp.bfloat16):
    array = scale * jax.random.normal(stream_key, dims, jnp.float32)
    if cuts:
        array = array * block_levels(stream_key, dims, cuts, -0.22, 0.18)
    return jnp.clip(array, -limit, limit).astype(kind)


def setup_inputs(seed: int = 0) -> dict:
    seeds = jax.random.split(jax.random.key(seed), 3)
    panel = draw_panel(jax.random.fold_in(seeds[2], 71), 0)
    trailing = normal_values(seeds[1], (TRAIL, ROWS), 1.0, 6.0, ((1, 128),), jnp.float32)
    return {"panel": panel, "trailing": trailing}


def matmul(left, right):
    return jnp.dot(left.astype(jnp.float32), right.astype(jnp.float32), precision=lax.Precision.HIGHEST, preferred_element_type=jnp.float32)

def lower_solve(lower, rhs):
    return lax.linalg.triangular_solve(lower, rhs, left_side=True, lower=True)

def reference(panel, trailing):
    first_low = jnp.linalg.cholesky(matmul(panel, panel.T))
    first = lower_solve(first_low, panel)
    second_low = jnp.linalg.cholesky(matmul(first, first.T))
    basis_t = lower_solve(second_low, first)
    whole_low = matmul(first_low, second_low)
    coupling = matmul(basis_t, trailing.T)
    updated = trailing - matmul(coupling.T, basis_t)
    scale = jnp.sqrt(jnp.float32(ROWS))
    return (basis_t * scale, whole_low.T / scale, coupling, updated)
```

```python
import jax
import jax.numpy as jnp
from jax import lax
from jax.experimental import pallas as pl
from jax.experimental.pallas import tpu as pltpu
from jax.sharding import PartitionSpec as P

AXES = ("gx", "gy", "gz")
HIGHEST = lax.Precision.HIGHEST
F32 = jnp.float32
BF16 = jnp.bfloat16
CHUNK = 1024
PANEL_COLS = 8
SMALL = 4e-3
MAGIC = 1.5 * 2.0**23


def round_int(x):
    return (x + MAGIC) - MAGIC


def two_sum(a, b):
    total = a + b
    part = total - a
    return total, (a - (total - part)) + (b - part)


def snap(x):
    c = x * 4097.0
    return c - (c - x)


def power_below(x):
    p = snap(jnp.exp2(jnp.floor(jnp.log2(jnp.maximum(x, 1e-30)))))
    return p, snap(1.0 / p)


def slices(hi, lo, count):
    digits = []
    for k in range(count):
        d = round_int(hi)
        digits.append(d)
        if k < count - 1:
            hi = (hi - d) * 256.0
            if lo is not None:
                lo = lo * 256.0
                new = hi + lo
                lo = lo - (new - hi)
                hi = new
    return digits


def nt(a, b, **kw):
    return lax.dot_general(a, b, (((1,), (1,)), ((), ())), preferred_element_type=F32, **kw)


def nn(a, b, **kw):
    return lax.dot_general(a, b, (((1,), (0,)), ((), ())), preferred_element_type=F32, **kw)


def iota(shape, axis):
    return lax.broadcasted_iota(jnp.int32, shape, axis)


def gram_kernel(core_ref, panel_ref, trail_ref, keep_ref, send_ref, ops, hi_ref, lo_ref, ca_ref):
    step = pl.program_id(0)
    n, t = panel_ref.shape[0], trail_ref.shape[0]

    @pl.when(step == 0)
    def _():
        hi_ref[...] = jnp.zeros_like(hi_ref)
        lo_ref[...] = jnp.zeros_like(lo_ref)
        ca_ref[...] = jnp.zeros_like(ca_ref)

    x = panel_ref[...]
    p, inv = power_below(jnp.max(jnp.abs(x), axis=1, keepdims=True))
    a = x * (inv * 64.0)
    d1 = round_int(a)
    r1 = (a - d1) * 256.0
    d2 = round_int(r1)
    ops[0:n, :] = d1.astype(BF16)
    ops[n : 2 * n, :] = d2.astype(BF16)
    ops[2 * n : 3 * n, :] = ((r1 - d2) * 256.0).astype(BF16)
    c = trail_ref[...]
    c1 = c.astype(BF16)
    rc = c - c1.astype(F32)
    c2 = rc.astype(BF16)
    ops[3 * n : 3 * n + t, :] = c1
    ops[3 * n + t : 3 * n + 2 * t, :] = c2
    ops[3 * n + 2 * t : 3 * n + 3 * t, :] = (rc - c2.astype(F32)).astype(BF16)

    m = nt(ops[...], ops[0 : 3 * n, :])

    def blk(i, j):
        return m[i * n : (i + 1) * n, j * n : (j + 1) * n]

    def cblk(i, j):
        return m[3 * n + i * t : 3 * n + (i + 1) * t, j * n : (j + 1) * n]

    row = jnp.broadcast_to(p * (1.0 / 64.0), (n, n))
    col = row.T
    scale = row * col
    h, e = two_sum(blk(0, 0), (blk(0, 1) + blk(1, 0)) * 2.0**-8)
    rest = (blk(0, 2) + blk(2, 0) + blk(1, 1)) * 2.0**-16
    rest = rest + ((blk(1, 2) + blk(2, 1)) * 2.0**-24 + blk(2, 2) * 2.0**-32)
    hi, err = two_sum(hi_ref[...], h * scale)
    hi_ref[...] = hi
    lo_ref[...] += err + (e + rest) * scale
    ca = (cblk(2, 0) + cblk(1, 1) * 2.0**-8 + cblk(0, 2) * 2.0**-16) + (cblk(1, 0) + cblk(0, 1) * 2.0**-8)
    ca_ref[...] += (ca + cblk(0, 0)) * col[0:t, :]

    @pl.when(step == pl.num_programs(0) - 1)
    def _():
        core = core_ref[0]
        half = n // 2
        i, j = iota((half, n), 0), iota((half, n), 1)

        def fold(g):
            top, bottom = g[:half, :], g[half:, :]
            body = jnp.where((j >= half) & (i >= j - half), pltpu.roll(top, half, 1), bottom)
            diag = jnp.sum(jnp.where(i == j - half, bottom, 0.0), axis=0, keepdims=True)
            return body, jnp.broadcast_to(diag, (8, n))

        hi_body, hi_diag = fold(hi_ref[...])
        lo_body, lo_diag = fold(lo_ref[...])
        ca = ca_ref[...]
        q = half // 2
        tq = t // 2

        def put(ref, first):
            def pick(v, size):
                return jnp.where(first, v[:size, :], v[size:, :])

            ref[0:q, :] = pick(hi_body, q)
            ref[q : q + 8, :] = hi_diag
            ref[q + 8 : 2 * q + 8, :] = pick(lo_body, q)
            ref[2 * q + 8 : 2 * q + 16, :] = lo_diag
            ref[2 * q + 16 :, :] = pick(ca, tq)

        put(keep_ref, core == 0)
        put(send_ref, core == 1)


def local_gram(core, panel, trailing):
    n, rows = panel.shape
    t = trailing.shape[0]
    out = jax.ShapeDtypeStruct((n // 2 + 16 + t // 2, n), F32)
    whole = pl.BlockSpec(out.shape, lambda i: (0, 0))
    return pl.pallas_call(
        gram_kernel,
        grid=(rows // CHUNK,),
        in_specs=[
            pl.BlockSpec(memory_space=pltpu.SMEM),
            pl.BlockSpec((n, CHUNK), lambda i: (0, i)),
            pl.BlockSpec((t, CHUNK), lambda i: (0, i)),
        ],
        out_specs=[whole, whole],
        out_shape=[out, out],
        scratch_shapes=[
            pltpu.VMEM((3 * (n + t), CHUNK), BF16),
            pltpu.VMEM((n, n), F32),
            pltpu.VMEM((n, n), F32),
            pltpu.VMEM((t, n), F32),
        ],
        compiler_params=pltpu.CompilerParams(vmem_limit_bytes=32 << 20),
        name="gram",
    )(core, panel, trailing)


def add_pair(a, b, words):
    hi, err = two_sum(a[:words, :], b[:words, :])
    return hi, (a[words : 2 * words, :] + b[words : 2 * words, :]) + err, a[2 * words :, :] + b[2 * words :, :]


def add_kernel(words, *refs):
    *ins, out = refs
    parts = [add_pair(ins[k][...], ins[k + 1][...], words) for k in range(0, len(ins), 2)]
    total = parts[0]
    if len(parts) == 2:
        hi, err = two_sum(parts[0][0], parts[1][0])
        total = (hi, (parts[0][1] + parts[1][1]) + err, parts[0][2] + parts[1][2])
    out[:words, :] = total[0]
    out[words : 2 * words, :] = total[1]
    out[2 * words :, :] = total[2]


def add_packed(words, *arrays):
    spec = pl.BlockSpec(memory_space=pltpu.VMEM)
    return pl.pallas_call(
        lambda *refs: add_kernel(words, *refs),
        in_specs=[spec] * len(arrays),
        out_specs=spec,
        out_shape=jax.ShapeDtypeStruct(arrays[0].shape, F32),
        name="add_packed",
    )(*arrays)


def exchange(value, mask):
    size = lax.axis_size(AXES)
    return lax.ppermute(value, AXES, [(s, s ^ mask) for s in range(size)])


def chol_inv(s):
    blocks = len(s)
    n = 8 * blocks
    rid, lid = iota((8, n), 0), iota((8, n), 1)
    w = [jnp.where(lid == rid + 8 * r, 1.0, 0.0) for r in range(blocks)]
    s = list(s)
    for first in range(0, n, PANEL_COLS):
        r0 = first // 8
        cols = [
            [jnp.broadcast_to(s[r][:, first + k : first + k + 1], (8, n)) for r in range(r0, blocks)]
            for k in range(PANEL_COLS)
        ]
        scales = []
        for k in range(PANEL_COLS):
            pivot = cols[k][0][k : k + 1, :]
            inv = 1.0 / pivot
            mult = [c * inv for c in cols[k]]
            mult[0] = jnp.where(rid > k, mult[0], 0.0)
            for later in range(k + 1, PANEL_COLS):
                e = cols[later][0][k : k + 1, :]
                cols[later] = [c - m * e for c, m in zip(cols[later], mult)]
            srow, wrow = s[r0][k : k + 1, :], w[r0][k : k + 1, :]
            for i, m in enumerate(mult):
                s[r0 + i] = s[r0 + i] - m * srow
                w[r0 + i] = w[r0 + i] - m * wrow
            scales.append(lax.rsqrt(pivot))
        for k, d in enumerate(scales):
            w[r0] = jnp.where(rid == k, w[r0] * d, w[r0])
    return w


def factor_kernel(rows_all, core_ref, own_ref, other_ref, wz_ref, upper_ref, coup_ref, wcat, gcat, tcat, v_ref):
    n = upper_ref.shape[0]
    t = coup_ref.shape[1]
    half, q, tq = n // 2, n // 4, t // 2
    first = core_ref[0] == 0
    own, other = own_ref[...], other_ref[...]
    a, b = jnp.where(first, own, other), jnp.where(first, other, own)
    i, j = iota((n, n), 0), iota((n, n), 1)
    hi_, hj_ = iota((half, n), 0), iota((half, n), 1)

    def unfold(start):
        body = jnp.concatenate([a[start : start + q, :], b[start : start + q, :]], axis=0)
        diag = jnp.broadcast_to(a[start + q : start + q + 1, :], (half, n))
        top = jnp.where((hj_ < half) & (hi_ >= hj_), pltpu.roll(body, half, 1), 0.0)
        keep = jnp.where((hj_ < half) | (hi_ < hj_ - half), body, 0.0)
        bottom = jnp.where(hi_ == hj_ - half, diag, keep)
        part = jnp.concatenate([top, bottom], axis=0)
        return jnp.where(i == j, part, part + part.T)

    g_hi, g_lo = unfold(0), unfold(q + 8)
    ca = jnp.concatenate([a[2 * q + 16 :, :], b[2 * q + 16 :, :]], axis=0)
    g_hi, g_lo = two_sum(g_hi, g_lo)

    diag = jnp.sum(jnp.where(i == j, g_hi, 0.0), axis=0, keepdims=True)
    pc, inv_pc = power_below(jnp.sqrt(diag))
    ic = jnp.broadcast_to(inv_pc, (n, n))
    eq = ic * ic.T
    s_hi, s_lo = g_hi * eq, g_lo * eq

    w = jnp.concatenate(chol_inv([s_hi[8 * r : 8 * r + 8, :] for r in range(n // 8)]), axis=0)

    qr, inv_qr = power_below(jnp.max(jnp.abs(w), axis=1, keepdims=True))
    wd = slices(w * (inv_qr * 64.0), None, 3)
    qs = qr * (1.0 / 64.0)
    wt = (wd[0] + wd[1] * 2.0**-8 + wd[2] * 2.0**-16) * qs
    for k in range(3):
        wcat[:, k * n : (k + 1) * n] = wd[k].astype(BF16)
    gd = slices(s_hi * 32.0, s_lo * 32.0, 6)
    for k in range(6):
        gcat[(5 - k) * n : (6 - k) * n, :] = gd[k].astype(BF16)

    def weigh(parts):
        hi, lo = parts[0], None
        for k, part in enumerate(parts[1:]):
            hi, err = two_sum(hi, part * 2.0 ** (-8 * (k + 1)))
            lo = err if lo is None else lo + err
        return two_sum(hi, lo)

    def t_level(k):
        width = min(k + 1, 3) * n
        return nn(wcat[:, 0:width], gcat[(5 - k) * n : (5 - k) * n + width, :])

    t_hi, t_lo = weigh([t_level(k) for k in range(6)])
    tau, inv_tau = power_below(jnp.max(jnp.abs(t_hi), axis=1, keepdims=True))
    td = slices(t_hi * (inv_tau * 64.0), t_lo * (inv_tau * 64.0), 4)
    for k in range(4):
        tcat[:, (3 - k) * n : (4 - k) * n] = td[k].astype(BF16)

    def m_level(k):
        width = min(k + 1, 3) * n
        return nt(tcat[:, (3 - k) * n : (3 - k) * n + width], wcat[:, 0:width])

    m_hi, m_lo = weigh([m_level(k) for k in range(4)])
    qb = jnp.broadcast_to(qs, (n, n))
    scale = qb.T * (qb * (tau * (1.0 / 2048.0)))
    e = (m_hi * scale - jnp.where(i == j, 1.0, 0.0)) + m_lo * scale

    def phi(x):
        return jnp.where(i > j, x, jnp.where(i == j, 0.5 * x, 0.0))

    f = phi(e)
    size = jnp.sum(f * f)

    @pl.when(size <= SMALL * SMALL)
    def _():
        fb = f.astype(BF16)
        v_ref[...] = (jnp.where(i == j, 1.0, 0.0) - f) + (phi(nt(fb, fb)) + nn(fb, fb))

    @pl.when(jnp.logical_not(size <= SMALL * SMALL))
    def _():
        lower = jnp.where(i >= j, e, 0.0)
        full = jnp.where(i == j, e + 1.0, lower + lower.T)
        blocks = chol_inv([full[8 * r : 8 * r + 8, :] for r in range(n // 8)])
        for r in range(n // 8):
            v_ref[8 * r : 8 * r + 8, :] = blocks[r]

    v = v_ref[...]
    w_new = nn(v, wt, precision=HIGHEST) * ic
    t_true = t_hi * (qs * (1.0 / 32.0)) * jnp.broadcast_to(pc, (n, n))
    root = jnp.sqrt(jnp.float32(rows_all))
    upper_ref[...] = jnp.where(i <= j, nn(v, t_true, precision=HIGHEST) / root, 0.0)
    coupling = nt(w_new, ca, precision=HIGHEST)
    coup_ref[...] = coupling
    wz_ref[:n, :] = w_new * root
    wz_ref[n:, :] = lax.dot_general(coupling, w_new, (((0,), (0,)), ((), ())), preferred_element_type=F32, precision=HIGHEST)


def factor(core, own, other, n, t, rows_all):
    spec = pl.BlockSpec(memory_space=pltpu.VMEM)
    return pl.pallas_call(
        lambda *refs: factor_kernel(rows_all, *refs),
        in_specs=[pl.BlockSpec(memory_space=pltpu.SMEM), spec, spec],
        out_specs=[spec] * 3,
        out_shape=[
            jax.ShapeDtypeStruct((n + t, n), F32),
            jax.ShapeDtypeStruct((n, n), F32),
            jax.ShapeDtypeStruct((n, t), F32),
        ],
        scratch_shapes=[
            pltpu.VMEM((n, 3 * n), BF16),
            pltpu.VMEM((6 * n, n), BF16),
            pltpu.VMEM((n, 4 * n), BF16),
            pltpu.VMEM((n, n), F32),
        ],
        compiler_params=pltpu.CompilerParams(vmem_limit_bytes=32 << 20),
        name="factor",
    )(core, own, other)


def shards(panel, trailing):
    n, t = panel.shape[0], trailing.shape[0]
    rows_all = panel.shape[1] * lax.axis_size(AXES)
    core = jnp.reshape(lax.axis_index("gy") % 2, (1,)).astype(jnp.int32)
    words = n // 4 + 8
    keep, send = local_gram(core, panel, trailing)
    total = add_packed(words, keep, exchange(send, 4))
    for masks in ((1, 3, 2), (8, 72, 64), (16, 48, 32)):
        near, wrap, far = (exchange(total, m) for m in masks)
        total = add_packed(words, total, near, far, wrap)
    other = exchange(total, 4)
    wz, upper, coupling = factor(core, total, other, n, t, rows_all)
    basis_t = nn(wz[:n], panel, precision=HIGHEST)
    updated = trailing - nn(wz[n:], panel, precision=HIGHEST)
    return basis_t, upper, coupling, updated


def solution(mesh):
    placed = (P(None, AXES), P(None, AXES))
    return jax.shard_map(
        shards,
        mesh=mesh,
        in_specs=placed,
        out_specs=(P(None, AXES), P(), P(), P(None, AXES)),
        check_vma=False,
    )
```

```python
import jax
import jax.numpy as jnp
from jax import lax
from jax.experimental import pallas as pl
from jax.experimental.pallas import tpu as pltpu
from jax.sharding import PartitionSpec as P

AXES = ("gx", "gy", "gz")
HIGHEST = lax.Precision.HIGHEST
F32 = jnp.float32
BF16 = jnp.bfloat16
CHUNK = 1024
OUT_CHUNK = 512
PANEL_COLS = 8
SMALL = 4e-3
MAGIC = 1.5 * 2.0**23


def round_int(x):
    return (x + MAGIC) - MAGIC


def two_sum(a, b):
    total = a + b
    part = total - a
    return total, (a - (total - part)) + (b - part)


def snap(x):
    c = x * 4097.0
    return c - (c - x)


def power_below(x):
    p = snap(jnp.exp2(jnp.floor(jnp.log2(jnp.maximum(x, 1e-30)))))
    return p, snap(1.0 / p)


def slices(hi, lo, count):
    digits = []
    for k in range(count):
        d = round_int(hi)
        digits.append(d)
        if k < count - 1:
            hi = (hi - d) * 256.0
            if lo is not None:
                lo = lo * 256.0
                new = hi + lo
                lo = lo - (new - hi)
                hi = new
    return digits


def nt(a, b, **kw):
    return lax.dot_general(a, b, (((1,), (1,)), ((), ())), preferred_element_type=F32, **kw)


def nn(a, b, **kw):
    return lax.dot_general(a, b, (((1,), (0,)), ((), ())), preferred_element_type=F32, **kw)


def iota(shape, axis):
    return lax.broadcasted_iota(jnp.int32, shape, axis)


def gram_kernel(core_ref, panel_ref, trail_ref, keep_ref, send_ref, ops, hi_ref, lo_ref, ca_ref):
    step = pl.program_id(0)
    n, t = panel_ref.shape[0], trail_ref.shape[0]

    @pl.when(step == 0)
    def _():
        hi_ref[...] = jnp.zeros_like(hi_ref)
        lo_ref[...] = jnp.zeros_like(lo_ref)
        ca_ref[...] = jnp.zeros_like(ca_ref)

    x = panel_ref[...]
    p, inv = power_below(jnp.max(jnp.abs(x), axis=1, keepdims=True))
    a = x * (inv * 64.0)
    d1 = round_int(a)
    r1 = (a - d1) * 256.0
    d2 = round_int(r1)
    ops[0:n, :] = d1.astype(BF16)
    ops[n : 2 * n, :] = d2.astype(BF16)
    ops[2 * n : 3 * n, :] = ((r1 - d2) * 256.0).astype(BF16)
    c = trail_ref[...]
    c1 = c.astype(BF16)
    rc = c - c1.astype(F32)
    c2 = rc.astype(BF16)
    ops[3 * n : 3 * n + t, :] = c1
    ops[3 * n + t : 3 * n + 2 * t, :] = c2
    ops[3 * n + 2 * t : 3 * n + 3 * t, :] = (rc - c2.astype(F32)).astype(BF16)

    m = nt(ops[...], ops[0 : 3 * n, :])

    def blk(i, j):
        return m[i * n : (i + 1) * n, j * n : (j + 1) * n]

    def cblk(i, j):
        return m[3 * n + i * t : 3 * n + (i + 1) * t, j * n : (j + 1) * n]

    row = jnp.broadcast_to(p * (1.0 / 64.0), (n, n))
    col = row.T
    scale = row * col
    h, e = two_sum(blk(0, 0), (blk(0, 1) + blk(1, 0)) * 2.0**-8)
    rest = (blk(0, 2) + blk(2, 0) + blk(1, 1)) * 2.0**-16
    rest = rest + ((blk(1, 2) + blk(2, 1)) * 2.0**-24 + blk(2, 2) * 2.0**-32)
    hi, err = two_sum(hi_ref[...], h * scale)
    hi_ref[...] = hi
    lo_ref[...] += err + (e + rest) * scale
    ca = (cblk(2, 0) + cblk(1, 1) * 2.0**-8 + cblk(0, 2) * 2.0**-16) + (cblk(1, 0) + cblk(0, 1) * 2.0**-8)
    ca_ref[...] += (ca + cblk(0, 0)) * col[0:t, :]

    @pl.when(step == pl.num_programs(0) - 1)
    def _():
        core = core_ref[0]
        half = n // 2
        i, j = iota((half, n), 0), iota((half, n), 1)

        def fold(g):
            top, bottom = g[:half, :], g[half:, :]
            body = jnp.where((j >= half) & (i >= j - half), pltpu.roll(top, half, 1), bottom)
            diag = jnp.sum(jnp.where(i == j - half, bottom, 0.0), axis=0, keepdims=True)
            return body, jnp.broadcast_to(diag, (8, n))

        hi_body, hi_diag = fold(hi_ref[...])
        lo_body, lo_diag = fold(lo_ref[...])
        ca = ca_ref[...]
        q = half // 2
        tq = t // 2

        def put(ref, first):
            def pick(v, size):
                return jnp.where(first, v[:size, :], v[size:, :])

            ref[0:q, :] = pick(hi_body, q)
            ref[q : q + 8, :] = hi_diag
            ref[q + 8 : 2 * q + 8, :] = pick(lo_body, q)
            ref[2 * q + 8 : 2 * q + 16, :] = lo_diag
            ref[2 * q + 16 :, :] = pick(ca, tq)

        put(keep_ref, core == 0)
        put(send_ref, core == 1)


def local_gram(core, panel, trailing):
    n, rows = panel.shape
    t = trailing.shape[0]
    out = jax.ShapeDtypeStruct((n // 2 + 16 + t // 2, n), F32)
    whole = pl.BlockSpec(out.shape, lambda i: (0, 0))
    return pl.pallas_call(
        gram_kernel,
        grid=(rows // CHUNK,),
        in_specs=[
            pl.BlockSpec(memory_space=pltpu.SMEM),
            pl.BlockSpec((n, CHUNK), lambda i: (0, i)),
            pl.BlockSpec((t, CHUNK), lambda i: (0, i)),
        ],
        out_specs=[whole, whole],
        out_shape=[out, out],
        scratch_shapes=[
            pltpu.VMEM((3 * (n + t), CHUNK), BF16),
            pltpu.VMEM((n, n), F32),
            pltpu.VMEM((n, n), F32),
            pltpu.VMEM((t, n), F32),
        ],
        compiler_params=pltpu.CompilerParams(vmem_limit_bytes=32 << 20),
        name="gram",
    )(core, panel, trailing)


def add_packed(words, *arrays):
    parts, errors = list(arrays), []
    while len(parts) > 1:
        pairs = []
        for a, b in zip(parts[::2], parts[1::2]):
            errors.append(two_sum(a[:words], b[:words])[1])
            pairs.append(a + b)
        parts = pairs
    error = errors[0] if len(errors) == 1 else (errors[0] + errors[1]) + errors[2]
    rest = parts[0].shape[0] - 2 * words
    return parts[0] + jnp.pad(error, ((words, rest), (0, 0)))


def exchange(value, mask):
    size = lax.axis_size(AXES)
    return lax.ppermute(value, AXES, [(s, s ^ mask) for s in range(size)])


def chol_inv(s):
    blocks = len(s)
    n = 8 * blocks
    rid, lid = iota((8, n), 0), iota((8, n), 1)
    w = [jnp.where(lid == rid + 8 * r, 1.0, 0.0) for r in range(blocks)]
    s = list(s)
    for first in range(0, n, PANEL_COLS):
        r0 = first // 8
        cols = [
            [jnp.broadcast_to(s[r][:, first + k : first + k + 1], (8, n)) for r in range(r0, blocks)]
            for k in range(PANEL_COLS)
        ]
        scales = []
        for k in range(PANEL_COLS):
            pivot = cols[k][0][k : k + 1, :]
            inv = 1.0 / pivot
            mult = [c * inv for c in cols[k]]
            mult[0] = jnp.where(rid > k, mult[0], 0.0)
            for later in range(k + 1, PANEL_COLS):
                e = cols[later][0][k : k + 1, :]
                cols[later] = [c - m * e for c, m in zip(cols[later], mult)]
            srow, wrow = s[r0][k : k + 1, :], w[r0][k : k + 1, :]
            for i, m in enumerate(mult):
                s[r0 + i] = s[r0 + i] - m * srow
                w[r0 + i] = w[r0 + i] - m * wrow
            scales.append(lax.rsqrt(pivot))
        for k, d in enumerate(scales):
            w[r0] = jnp.where(rid == k, w[r0] * d, w[r0])
    return w


def factor_kernel(rows_all, core_ref, own_ref, other_ref, wz_ref, upper_ref, coup_ref, wcat, gcat, tcat, v_ref):
    n = upper_ref.shape[0]
    t = coup_ref.shape[0]
    half, q, tq = n // 2, n // 4, t // 2
    first = core_ref[0] == 0
    own, other = own_ref[...], other_ref[...]
    a, b = jnp.where(first, own, other), jnp.where(first, other, own)
    i, j = iota((n, n), 0), iota((n, n), 1)
    hi_, hj_ = iota((half, n), 0), iota((half, n), 1)

    def unfold(start):
        body = jnp.concatenate([a[start : start + q, :], b[start : start + q, :]], axis=0)
        diag = jnp.broadcast_to(a[start + q : start + q + 1, :], (half, n))
        top = jnp.where((hj_ < half) & (hi_ >= hj_), pltpu.roll(body, half, 1), 0.0)
        keep = jnp.where((hj_ < half) | (hi_ < hj_ - half), body, 0.0)
        bottom = jnp.where(hi_ == hj_ - half, diag, keep)
        part = jnp.concatenate([top, bottom], axis=0)
        return jnp.where(i == j, part, part + part.T)

    g_hi, g_lo = unfold(0), unfold(q + 8)
    ca = jnp.concatenate([a[2 * q + 16 :, :], b[2 * q + 16 :, :]], axis=0)
    g_hi, g_lo = two_sum(g_hi, g_lo)

    diag = jnp.sum(jnp.where(i == j, g_hi, 0.0), axis=0, keepdims=True)
    pc, inv_pc = power_below(jnp.sqrt(diag))
    ic = jnp.broadcast_to(inv_pc, (n, n))
    eq = ic * ic.T
    s_hi, s_lo = g_hi * eq, g_lo * eq

    w = jnp.concatenate(chol_inv([s_hi[8 * r : 8 * r + 8, :] for r in range(n // 8)]), axis=0)

    qr, inv_qr = power_below(jnp.max(jnp.abs(w), axis=1, keepdims=True))
    wd = slices(w * (inv_qr * 64.0), None, 3)
    qs = qr * (1.0 / 64.0)
    wt = (wd[0] + wd[1] * 2.0**-8 + wd[2] * 2.0**-16) * qs
    for k in range(3):
        wcat[:, k * n : (k + 1) * n] = wd[k].astype(BF16)
    gd = slices(s_hi * 32.0, s_lo * 32.0, 6)
    for k in range(6):
        gcat[(5 - k) * n : (6 - k) * n, :] = gd[k].astype(BF16)

    def weigh(parts):
        hi, lo = parts[0], None
        for k, part in enumerate(parts[1:]):
            hi, err = two_sum(hi, part * 2.0 ** (-8 * (k + 1)))
            lo = err if lo is None else lo + err
        return two_sum(hi, lo)

    def t_level(k):
        width = min(k + 1, 3) * n
        return nn(wcat[:, 0:width], gcat[(5 - k) * n : (5 - k) * n + width, :])

    t_hi, t_lo = weigh([t_level(k) for k in range(6)])
    tau, inv_tau = power_below(jnp.max(jnp.abs(t_hi), axis=1, keepdims=True))
    td = slices(t_hi * (inv_tau * 64.0), t_lo * (inv_tau * 64.0), 4)
    for k in range(4):
        tcat[:, (3 - k) * n : (4 - k) * n] = td[k].astype(BF16)

    def m_level(k):
        width = min(k + 1, 3) * n
        return nt(tcat[:, (3 - k) * n : (3 - k) * n + width], wcat[:, 0:width])

    m_hi, m_lo = weigh([m_level(k) for k in range(4)])
    qb = jnp.broadcast_to(qs, (n, n))
    scale = qb.T * (qb * (tau * (1.0 / 2048.0)))
    e = (m_hi * scale - jnp.where(i == j, 1.0, 0.0)) + m_lo * scale

    def phi(x):
        return jnp.where(i > j, x, jnp.where(i == j, 0.5 * x, 0.0))

    f = phi(e)
    size = jnp.sum(f * f)

    @pl.when(size <= SMALL * SMALL)
    def _():
        fb = f.astype(BF16)
        v_ref[...] = (jnp.where(i == j, 1.0, 0.0) - f) + (phi(nt(fb, fb)) + nn(fb, fb))

    @pl.when(jnp.logical_not(size <= SMALL * SMALL))
    def _():
        lower = jnp.where(i >= j, e, 0.0)
        full = jnp.where(i == j, e + 1.0, lower + lower.T)
        blocks = chol_inv([full[8 * r : 8 * r + 8, :] for r in range(n // 8)])
        for r in range(n // 8):
            v_ref[8 * r : 8 * r + 8, :] = blocks[r]

    v = v_ref[...]
    y = nt(wt, ca * inv_pc, precision=HIGHEST)
    t_true = t_hi * (qs * (1.0 / 32.0)) * jnp.broadcast_to(pc, (n, n))
    wide = nn(v, jnp.concatenate([wt, t_true, y], axis=1), precision=HIGHEST)
    w_new = wide[:, :n] * ic
    root = jnp.sqrt(jnp.float32(rows_all))
    upper_ref[...] = jnp.where(i <= j, wide[:, n : 2 * n] / root, 0.0)
    coupling_t = wide[:, 2 * n :].T
    coup_ref[...] = coupling_t
    wz_ref[:n, :] = w_new
    wz_ref[n:, :] = nn(coupling_t, w_new, precision=HIGHEST)


def factor(core, own, other, n, t, rows_all):
    spec = pl.BlockSpec(memory_space=pltpu.VMEM)
    return pl.pallas_call(
        lambda *refs: factor_kernel(rows_all, *refs),
        in_specs=[pl.BlockSpec(memory_space=pltpu.SMEM), spec, spec],
        out_specs=[spec] * 3,
        out_shape=[
            jax.ShapeDtypeStruct((n + t, n), F32),
            jax.ShapeDtypeStruct((n, n), F32),
            jax.ShapeDtypeStruct((t, n), F32),
        ],
        scratch_shapes=[
            pltpu.VMEM((n, 3 * n), BF16),
            pltpu.VMEM((6 * n, n), BF16),
            pltpu.VMEM((n, 4 * n), BF16),
            pltpu.VMEM((n, n), F32),
        ],
        compiler_params=pltpu.CompilerParams(vmem_limit_bytes=32 << 20),
        name="factor",
    )(core, own, other)


def apply_kernel(rows_all, wz_ref, panel_ref, trail_ref, basis_ref, updated_ref):
    n = panel_ref.shape[0]
    width = basis_ref.shape[1]
    at = pl.multiple_of(pl.program_id(0) * width, width)
    out = nn(wz_ref[...], panel_ref[:, pl.ds(at, width)], precision=HIGHEST)
    basis_ref[...] = out[:n, :] * jnp.sqrt(jnp.float32(rows_all))
    updated_ref[...] = trail_ref[:, pl.ds(at, width)] - out[n:, :]


def apply_factors(wz, panel, trailing, rows_all):
    n, rows = panel.shape
    t = trailing.shape[0]
    spec = pl.BlockSpec(memory_space=pltpu.VMEM)
    return pl.pallas_call(
        lambda *refs: apply_kernel(rows_all, *refs),
        grid=(rows // OUT_CHUNK,),
        in_specs=[spec, spec, spec],
        out_specs=[pl.BlockSpec((n, OUT_CHUNK), lambda i: (0, i)), pl.BlockSpec((t, OUT_CHUNK), lambda i: (0, i))],
        out_shape=[jax.ShapeDtypeStruct((n, rows), F32), jax.ShapeDtypeStruct((t, rows), F32)],
        compiler_params=pltpu.CompilerParams(vmem_limit_bytes=32 << 20),
        name="apply",
    )(wz, panel, trailing)


def shards(panel, trailing):
    n, t = panel.shape[0], trailing.shape[0]
    rows_all = panel.shape[1] * lax.axis_size(AXES)
    core = jnp.reshape(lax.axis_index("gy") % 2, (1,)).astype(jnp.int32)
    words = n // 4 + 8
    streamed = (pltpu.with_memory_space_constraint(a, pltpu.HBM) for a in (panel, trailing))
    keep, send = local_gram(core, *streamed)
    total = add_packed(words, keep, exchange(send, 4))
    for masks in ((1, 3, 2), (8, 72, 64), (16, 48, 32)):
        near, wrap, far = (exchange(total, m) for m in masks)
        total = add_packed(words, total, near, far, wrap)
    other = exchange(total, 4)
    wz, upper, coupling_t = factor(core, total, other, n, t, rows_all)
    basis_t, updated = apply_factors(wz, panel, trailing, rows_all)
    return basis_t, upper, coupling_t.T, updated


def solution(mesh):
    placed = (P(None, AXES), P(None, AXES))
    return jax.shard_map(
        shards,
        mesh=mesh,
        in_specs=placed,
        out_specs=(P(None, AXES), P(), P(), P(None, AXES)),
        check_vma=False,
    )
```

```python
import jax
import jax.numpy as jnp
from jax import lax
from jax.experimental import pallas as pl
from jax.experimental.pallas import tpu as pltpu
from jax.sharding import PartitionSpec as P

AXES = ("gx", "gy", "gz")
HIGHEST = lax.Precision.HIGHEST
F32 = jnp.float32
BF16 = jnp.bfloat16
CHUNK = 2048
OUT_CHUNK = 512
PANEL_COLS = 8
SMALL = 4e-3
MAGIC = 1.5 * 2.0**23


def round_int(x):
    return (x + MAGIC) - MAGIC


def two_sum(a, b):
    total = a + b
    part = total - a
    return total, (a - (total - part)) + (b - part)


def snap(x):
    c = x * 4097.0
    return c - (c - x)


def power_below(x):
    p = snap(jnp.exp2(jnp.floor(jnp.log2(jnp.maximum(x, 1e-30)))))
    return p, snap(1.0 / p)


def slices(hi, lo, count):
    digits = []
    for k in range(count):
        d = round_int(hi)
        digits.append(d)
        if k < count - 1:
            hi = (hi - d) * 256.0
            if lo is not None:
                lo = lo * 256.0
                new = hi + lo
                lo = lo - (new - hi)
                hi = new
    return digits


def nt(a, b, **kw):
    return lax.dot_general(a, b, (((1,), (1,)), ((), ())), preferred_element_type=F32, **kw)


def nn(a, b, **kw):
    return lax.dot_general(a, b, (((1,), (0,)), ((), ())), preferred_element_type=F32, **kw)


def iota(shape, axis):
    return lax.broadcasted_iota(jnp.int32, shape, axis)


def gram_kernel(core_ref, panel, trail, keep_ref, send_ref, pbuf, tbuf, ops, hi_ref, lo_ref, mix_ref, ca_ref, ac_ref, sems):
    n, rows = panel.shape
    t = trail.shape[0]
    steps = rows // CHUNK
    copies = []
    for k in range(steps):
        at = pl.ds(k * CHUNK, CHUNK)
        pair = (
            pltpu.make_async_copy(panel.at[:, at], pbuf.at[k], sems.at[0, k]),
            pltpu.make_async_copy(trail.at[:, at], tbuf.at[k], sems.at[1, k]),
        )
        for copy in pair:
            copy.start()
        copies.append(pair)

    def split(k):
        copies[k][0].wait()
        x = pbuf[k]
        p, inv = power_below(jnp.max(jnp.abs(x), axis=1, keepdims=True))
        a = x * (inv * 32.0)
        d1 = round_int(a)
        r1 = (a - d1) * 256.0
        d2 = round_int(r1)
        d3 = (r1 - d2) * 256.0
        copies[k][1].wait()
        c = tbuf[k]
        c1 = c.astype(BF16)
        rc = c - c1.astype(F32)
        c2 = rc.astype(BF16)
        c3 = rc - c2.astype(F32)
        at = 0
        for part in (c3, d1, d2, d3, c1, c2):
            ops[k, at : at + part.shape[0], :] = part.astype(BF16)
            at += part.shape[0]
        return p

    def product(k, p):
        left = nt(ops[k, 0 : t + 2 * n, :], ops[k, t : t + 2 * n, :])
        right = nt(ops[k, t : t + 3 * n, :], ops[k, t + 2 * n :, :])
        c3d1, left = left[:t, :n], left[t:, :]
        row = jnp.broadcast_to(p * (1.0 / 32.0), (n, n))
        col = row.T
        scale = row * col
        h, e = two_sum(left[:n, :n], (left[:n, n:] + left[n:, :n]) * 2.0**-8)
        e = e + (left[n:, n:] * 2.0**-16 + right[2 * n :, :n] * 2.0**-32)
        mix = (right[:n, :n] * 2.0**-16 + right[n : 2 * n, :n] * 2.0**-24) * scale
        ac = right[2 * n :, n : n + t] * 2.0**-16 + right[n : 2 * n, n + t :] * 2.0**-8
        ac = ac + (right[n : 2 * n, n : n + t] * 2.0**-8 + right[:n, n + t :])
        ac = (ac + right[:n, n : n + t]) * row[:, :t]
        ca = c3d1 * col[:t, :]
        if k == 0:
            hi_ref[...], lo_ref[...] = h * scale, e * scale
            mix_ref[...], ca_ref[...], ac_ref[...] = mix, ca, ac
        else:
            hi, err = two_sum(hi_ref[...], h * scale)
            hi_ref[...] = hi
            lo_ref[...] += err + e * scale
            mix_ref[...] += mix
            ca_ref[...] += ca
            ac_ref[...] += ac

    p = split(0)
    for k in range(steps):
        following = split(k + 1) if k + 1 < steps else None
        product(k, p)
        p = following

    core = core_ref[0]
    half = n // 2
    i, j = iota((half, n), 0), iota((half, n), 1)

    def fold(g):
        top, bottom = g[:half, :], g[half:, :]
        body = jnp.where((j >= half) & (i >= j - half), pltpu.roll(top, half, 1), bottom)
        diag = jnp.sum(jnp.where(i == j - half, bottom, 0.0), axis=0, keepdims=True)
        return body, jnp.broadcast_to(diag, (8, n))

    mix = mix_ref[...]
    hi, lo = two_sum(hi_ref[...], lo_ref[...] + (mix + mix.T))
    hi_body, hi_diag = fold(hi)
    lo_body, lo_diag = fold(lo)
    ca = ca_ref[...] + ac_ref[...].T
    q = half // 2
    tq = t // 2

    def put(ref, first):
        def pick(v, size):
            return jnp.where(first, v[:size, :], v[size:, :])

        ref[0:q, :] = pick(hi_body, q)
        ref[q : q + 8, :] = hi_diag
        ref[q + 8 : 2 * q + 8, :] = pick(lo_body, q)
        ref[2 * q + 8 : 2 * q + 16, :] = lo_diag
        ref[2 * q + 16 :, :] = pick(ca, tq)

    put(keep_ref, core == 0)
    put(send_ref, core == 1)


def local_gram(core, panel, trailing):
    n, rows = panel.shape
    t = trailing.shape[0]
    steps = rows // CHUNK
    out = jax.ShapeDtypeStruct((n // 2 + 16 + t // 2, n), F32)
    vmem, hbm = pl.BlockSpec(memory_space=pltpu.VMEM), pl.BlockSpec(memory_space=pltpu.HBM)
    return pl.pallas_call(
        gram_kernel,
        in_specs=[pl.BlockSpec(memory_space=pltpu.SMEM), hbm, hbm],
        out_specs=[vmem, vmem],
        out_shape=[out, out],
        scratch_shapes=[
            pltpu.VMEM((steps, n, CHUNK), F32),
            pltpu.VMEM((steps, t, CHUNK), F32),
            pltpu.VMEM((steps, 3 * (n + t), CHUNK), BF16),
            pltpu.VMEM((n, n), F32),
            pltpu.VMEM((n, n), F32),
            pltpu.VMEM((n, n), F32),
            pltpu.VMEM((t, n), F32),
            pltpu.VMEM((n, t), F32),
            pltpu.SemaphoreType.DMA((2, steps)),
        ],
        compiler_params=pltpu.CompilerParams(vmem_limit_bytes=32 << 20),
        name="gram",
    )(core, panel, trailing)


def add_packed(words, *arrays):
    parts, errors = list(arrays), []
    while len(parts) > 1:
        pairs = []
        for a, b in zip(parts[::2], parts[1::2]):
            errors.append(two_sum(a[:words], b[:words])[1])
            pairs.append(a + b)
        parts = pairs
    error = errors[0] if len(errors) == 1 else (errors[0] + errors[1]) + errors[2]
    rest = parts[0].shape[0] - 2 * words
    return parts[0] + jnp.pad(error, ((words, rest), (0, 0)))


def exchange(value, mask):
    size = lax.axis_size(AXES)
    return lax.ppermute(value, AXES, [(s, s ^ mask) for s in range(size)])


def chol_inv(s):
    blocks = len(s)
    n = 8 * blocks
    rid, lid = iota((8, n), 0), iota((8, n), 1)
    w = [jnp.where(lid == rid + 8 * r, 1.0, 0.0) for r in range(blocks)]
    s = list(s)
    for first in range(0, n, PANEL_COLS):
        r0 = first // 8
        cols = [
            [jnp.broadcast_to(s[r][:, first + k : first + k + 1], (8, n)) for r in range(r0, blocks)]
            for k in range(PANEL_COLS)
        ]
        scales = []
        for k in range(PANEL_COLS):
            pivot = cols[k][0][k : k + 1, :]
            inv = 1.0 / pivot
            mult = [c * inv for c in cols[k]]
            mult[0] = jnp.where(rid > k, mult[0], 0.0)
            for later in range(k + 1, PANEL_COLS):
                e = cols[later][0][k : k + 1, :]
                cols[later] = [c - m * e for c, m in zip(cols[later], mult)]
            srow, wrow = s[r0][k : k + 1, :], w[r0][k : k + 1, :]
            for i, m in enumerate(mult):
                s[r0 + i] = s[r0 + i] - m * srow
                w[r0 + i] = w[r0 + i] - m * wrow
            scales.append(lax.rsqrt(pivot))
        for k, d in enumerate(scales):
            w[r0] = jnp.where(rid == k, w[r0] * d, w[r0])
    return w


def factor_kernel(rows_all, core_ref, own_ref, other_ref, wz_ref, upper_ref, coup_ref, wcat, gcat, tcat, v_ref):
    n = upper_ref.shape[0]
    t = coup_ref.shape[0]
    half, q, tq = n // 2, n // 4, t // 2
    first = core_ref[0] == 0
    own, other = own_ref[...], other_ref[...]
    a, b = jnp.where(first, own, other), jnp.where(first, other, own)
    i, j = iota((n, n), 0), iota((n, n), 1)
    hi_, hj_ = iota((half, n), 0), iota((half, n), 1)

    def unfold(start):
        body = jnp.concatenate([a[start : start + q, :], b[start : start + q, :]], axis=0)
        diag = jnp.broadcast_to(a[start + q : start + q + 1, :], (half, n))
        top = jnp.where((hj_ < half) & (hi_ >= hj_), pltpu.roll(body, half, 1), 0.0)
        keep = jnp.where((hj_ < half) | (hi_ < hj_ - half), body, 0.0)
        bottom = jnp.where(hi_ == hj_ - half, diag, keep)
        part = jnp.concatenate([top, bottom], axis=0)
        return jnp.where(i == j, part, part + part.T)

    g_hi, g_lo = unfold(0), unfold(q + 8)
    ca = jnp.concatenate([a[2 * q + 16 :, :], b[2 * q + 16 :, :]], axis=0)
    g_hi, g_lo = two_sum(g_hi, g_lo)

    diag = jnp.sum(jnp.where(i == j, g_hi, 0.0), axis=0, keepdims=True)
    pc, inv_pc = power_below(jnp.sqrt(diag))
    ic = jnp.broadcast_to(inv_pc, (n, n))
    eq = ic * ic.T
    s_hi, s_lo = g_hi * eq, g_lo * eq

    w = jnp.concatenate(chol_inv([s_hi[8 * r : 8 * r + 8, :] for r in range(n // 8)]), axis=0)

    qr, inv_qr = power_below(jnp.max(jnp.abs(w), axis=1, keepdims=True))
    wd = slices(w * (inv_qr * 64.0), None, 3)
    qs = qr * (1.0 / 64.0)
    wt = (wd[0] + wd[1] * 2.0**-8 + wd[2] * 2.0**-16) * qs
    for k in range(3):
        wcat[:, k * n : (k + 1) * n] = wd[k].astype(BF16)
    gd = slices(s_hi * 32.0, s_lo * 32.0, 6)
    for k in range(6):
        gcat[(5 - k) * n : (6 - k) * n, :] = gd[k].astype(BF16)

    def weigh(parts):
        hi, lo = parts[0], None
        for k, part in enumerate(parts[1:]):
            hi, err = two_sum(hi, part * 2.0 ** (-8 * (k + 1)))
            lo = err if lo is None else lo + err
        return two_sum(hi, lo)

    def t_level(k):
        width = min(k + 1, 3) * n
        return nn(wcat[:, 0:width], gcat[(5 - k) * n : (5 - k) * n + width, :])

    t_hi, t_lo = weigh([t_level(k) for k in range(6)])
    tau, inv_tau = power_below(jnp.max(jnp.abs(t_hi), axis=1, keepdims=True))
    td = slices(t_hi * (inv_tau * 64.0), t_lo * (inv_tau * 64.0), 4)
    for k in range(4):
        tcat[:, (3 - k) * n : (4 - k) * n] = td[k].astype(BF16)

    def m_level(k):
        width = min(k + 1, 3) * n
        return nt(tcat[:, (3 - k) * n : (3 - k) * n + width], wcat[:, 0:width])

    m_hi, m_lo = weigh([m_level(k) for k in range(4)])
    qb = jnp.broadcast_to(qs, (n, n))
    scale = qb.T * (qb * (tau * (1.0 / 2048.0)))
    e = (m_hi * scale - jnp.where(i == j, 1.0, 0.0)) + m_lo * scale

    def phi(x):
        return jnp.where(i > j, x, jnp.where(i == j, 0.5 * x, 0.0))

    f = phi(e)
    size = jnp.sum(f * f)

    @pl.when(size <= SMALL * SMALL)
    def _():
        fb = f.astype(BF16)
        v_ref[...] = (jnp.where(i == j, 1.0, 0.0) - f) + (phi(nt(fb, fb)) + nn(fb, fb))

    @pl.when(jnp.logical_not(size <= SMALL * SMALL))
    def _():
        lower = jnp.where(i >= j, e, 0.0)
        full = jnp.where(i == j, e + 1.0, lower + lower.T)
        blocks = chol_inv([full[8 * r : 8 * r + 8, :] for r in range(n // 8)])
        for r in range(n // 8):
            v_ref[8 * r : 8 * r + 8, :] = blocks[r]

    v = v_ref[...]
    y = nt(wt, ca * inv_pc, precision=HIGHEST)
    t_true = t_hi * (qs * (1.0 / 32.0)) * jnp.broadcast_to(pc, (n, n))
    wide = nn(v, jnp.concatenate([wt, t_true, y], axis=1), precision=HIGHEST)
    w_new = wide[:, :n] * ic
    root = jnp.sqrt(jnp.float32(rows_all))
    upper_ref[...] = jnp.where(i <= j, wide[:, n : 2 * n] / root, 0.0)
    coupling_t = wide[:, 2 * n :].T
    coup_ref[...] = coupling_t
    wz_ref[:n, :] = w_new
    wz_ref[n:, :] = nn(coupling_t, w_new, precision=HIGHEST)


def factor(core, own, other, n, t, rows_all):
    spec = pl.BlockSpec(memory_space=pltpu.VMEM)
    return pl.pallas_call(
        lambda *refs: factor_kernel(rows_all, *refs),
        in_specs=[pl.BlockSpec(memory_space=pltpu.SMEM), spec, spec],
        out_specs=[spec] * 3,
        out_shape=[
            jax.ShapeDtypeStruct((n + t, n), F32),
            jax.ShapeDtypeStruct((n, n), F32),
            jax.ShapeDtypeStruct((t, n), F32),
        ],
        scratch_shapes=[
            pltpu.VMEM((n, 3 * n), BF16),
            pltpu.VMEM((6 * n, n), BF16),
            pltpu.VMEM((n, 4 * n), BF16),
            pltpu.VMEM((n, n), F32),
        ],
        compiler_params=pltpu.CompilerParams(vmem_limit_bytes=32 << 20),
        name="factor",
    )(core, own, other)


def apply_kernel(rows_all, wz_ref, panel_ref, trail_ref, basis, updated, words, basis_buf, updated_buf, sems):
    n, rows = panel_ref.shape
    root = jnp.sqrt(jnp.float32(rows_all))

    def split(x):
        x1 = x.astype(BF16)
        rest = x - x1.astype(F32)
        x2 = rest.astype(BF16)
        return x1, x2, (rest - x2.astype(F32)).astype(BF16)

    w1, w2, w3 = split(wz_ref[...])
    for k, w in enumerate((w1, w2, w1, w2, w1, w3)):
        words[:, k * n : (k + 1) * n] = w
    copies = []
    for k in range(rows // OUT_CHUNK):
        at = pl.ds(k * OUT_CHUNK, OUT_CHUNK)
        a1, a2, a3 = split(panel_ref[:, at])
        out = nn(words[...], jnp.concatenate([a1, a2, a2, a1, a3, a1], axis=0))
        basis_buf[k] = out[:n, :] * root
        updated_buf[k] = trail_ref[:, at] - out[n:, :]
        for copy in (
            pltpu.make_async_copy(basis_buf.at[k], basis.at[:, at], sems.at[0, k]),
            pltpu.make_async_copy(updated_buf.at[k], updated.at[:, at], sems.at[1, k]),
        ):
            copy.start()
            copies.append(copy)
    for copy in copies:
        copy.wait()


def apply_factors(wz, panel, trailing, rows_all):
    n, rows = panel.shape
    t = trailing.shape[0]
    steps = rows // OUT_CHUNK
    vmem, hbm = pl.BlockSpec(memory_space=pltpu.VMEM), pl.BlockSpec(memory_space=pltpu.HBM)
    return pl.pallas_call(
        lambda *refs: apply_kernel(rows_all, *refs),
        in_specs=[vmem] * 3,
        out_specs=[hbm] * 2,
        out_shape=[jax.ShapeDtypeStruct((n, rows), F32), jax.ShapeDtypeStruct((t, rows), F32)],
        scratch_shapes=[
            pltpu.VMEM((n + t, 6 * n), BF16),
            pltpu.VMEM((steps, n, OUT_CHUNK), F32),
            pltpu.VMEM((steps, t, OUT_CHUNK), F32),
            pltpu.SemaphoreType.DMA((2, steps)),
        ],
        compiler_params=pltpu.CompilerParams(vmem_limit_bytes=32 << 20),
        name="apply",
    )(wz, panel, trailing)


def shards(panel, trailing):
    n, t = panel.shape[0], trailing.shape[0]
    rows_all = panel.shape[1] * lax.axis_size(AXES)
    core = jnp.reshape(lax.axis_index("gy") % 2, (1,)).astype(jnp.int32)
    words = n // 4 + 8
    streamed = (pltpu.with_memory_space_constraint(a, pltpu.HBM) for a in (panel, trailing))
    keep, send = local_gram(core, *streamed)
    total = add_packed(words, keep, exchange(send, 4))
    for masks in ((1, 3, 2), (8, 72, 64), (16, 48, 32)):
        near, wrap, far = (exchange(total, m) for m in masks)
        total = add_packed(words, total, near, far, wrap)
    other = exchange(total, 4)
    wz, upper, coupling_t = factor(core, total, other, n, t, rows_all)
    basis_t, updated = apply_factors(wz, panel, trailing, rows_all)
    return basis_t, upper, coupling_t.T, updated


def solution(mesh):
    placed = (P(None, AXES), P(None, AXES))
    return jax.shard_map(
        shards,
        mesh=mesh,
        in_specs=placed,
        out_specs=(P(None, AXES), P(), P(), P(None, AXES)),
        check_vma=False,
    )
```

```python
import jax
import jax.numpy as jnp
from jax import lax
from jax.experimental import pallas as pl
from jax.experimental.pallas import tpu as pltpu
from jax.sharding import PartitionSpec as P

AXES = ("gx", "gy", "gz")
HIGHEST = lax.Precision.HIGHEST
F32 = jnp.float32
BF16 = jnp.bfloat16
CHUNK = 2048
OUT_CHUNK = 512
PANEL_COLS = 8
SMALL = 4e-3
MAGIC = 1.5 * 2.0**23


def round_int(x):
    return (x + MAGIC) - MAGIC


def two_sum(a, b):
    total = a + b
    part = total - a
    return total, (a - (total - part)) + (b - part)


def snap(x):
    c = x * 4097.0
    return c - (c - x)


def power_below(x):
    p = snap(jnp.exp2(jnp.floor(jnp.log2(jnp.maximum(x, 1e-30)))))
    return p, snap(1.0 / p)


def slices(hi, lo, count):
    digits = []
    for k in range(count):
        d = round_int(hi)
        digits.append(d)
        if k < count - 1:
            hi = (hi - d) * 256.0
            if lo is not None:
                lo = lo * 256.0
                new = hi + lo
                lo = lo - (new - hi)
                hi = new
    return digits


def nt(a, b, **kw):
    return lax.dot_general(a, b, (((1,), (1,)), ((), ())), preferred_element_type=F32, **kw)


def nn(a, b, **kw):
    return lax.dot_general(a, b, (((1,), (0,)), ((), ())), preferred_element_type=F32, **kw)


def iota(shape, axis):
    return lax.broadcasted_iota(jnp.int32, shape, axis)


def gram_kernel(core_ref, panel, trail, keep_ref, send_ref, pbuf, tbuf, ops, hi_ref, lo_ref, mix_ref, ca_ref, ac_ref, sems):
    n, rows = panel.shape
    t = trail.shape[0]
    steps = rows // CHUNK
    copies = []
    for k in range(steps):
        at = pl.ds(k * CHUNK, CHUNK)
        pair = (
            pltpu.make_async_copy(panel.at[:, at], pbuf.at[k], sems.at[0, k]),
            pltpu.make_async_copy(trail.at[:, at], tbuf.at[k], sems.at[1, k]),
        )
        for copy in pair:
            copy.start()
        copies.append(pair)

    def split(k):
        copies[k][0].wait()
        x = pbuf[k]
        p, inv = power_below(jnp.max(jnp.abs(x), axis=1, keepdims=True))
        a = x * (inv * 32.0)
        d1 = round_int(a)
        r1 = (a - d1) * 256.0
        d2 = round_int(r1)
        d3 = (r1 - d2) * 256.0
        copies[k][1].wait()
        c = tbuf[k]
        c1 = c.astype(BF16)
        rc = c - c1.astype(F32)
        c2 = rc.astype(BF16)
        c3 = rc - c2.astype(F32)
        at = 0
        for part in (c3, d1, d2, d3, c1, c2):
            ops[k, at : at + part.shape[0], :] = part.astype(BF16)
            at += part.shape[0]
        return p

    def product(k, p):
        left = nt(ops[k, 0 : t + 2 * n, :], ops[k, t : t + 2 * n, :])
        right = nt(ops[k, t : t + 3 * n, :], ops[k, t + 2 * n :, :])
        c3d1, left = left[:t, :n], left[t:, :]
        row = jnp.broadcast_to(p * (1.0 / 32.0), (n, n))
        col = row.T
        scale = row * col
        h, e = two_sum(left[:n, :n], (left[:n, n:] + left[n:, :n]) * 2.0**-8)
        e = e + (left[n:, n:] * 2.0**-16 + right[2 * n :, :n] * 2.0**-32)
        mix = (right[:n, :n] * 2.0**-16 + right[n : 2 * n, :n] * 2.0**-24) * scale
        ac = right[2 * n :, n : n + t] * 2.0**-16 + right[n : 2 * n, n + t :] * 2.0**-8
        ac = ac + (right[n : 2 * n, n : n + t] * 2.0**-8 + right[:n, n + t :])
        ac = (ac + right[:n, n : n + t]) * row[:, :t]
        ca = c3d1 * col[:t, :]
        if k == 0:
            hi_ref[...], lo_ref[...] = h * scale, e * scale
            mix_ref[...], ca_ref[...], ac_ref[...] = mix, ca, ac
        else:
            hi, err = two_sum(hi_ref[...], h * scale)
            hi_ref[...] = hi
            lo_ref[...] += err + e * scale
            mix_ref[...] += mix
            ca_ref[...] += ca
            ac_ref[...] += ac

    p = split(0)
    for k in range(steps):
        following = split(k + 1) if k + 1 < steps else None
        product(k, p)
        p = following

    core = core_ref[0]
    half = n // 2
    i, j = iota((half, n), 0), iota((half, n), 1)

    def fold(g):
        top, bottom = g[:half, :], g[half:, :]
        body = jnp.where((j >= half) & (i >= j - half), pltpu.roll(top, half, 1), bottom)
        diag = jnp.sum(jnp.where(i == j - half, bottom, 0.0), axis=0, keepdims=True)
        return body, jnp.broadcast_to(diag, (8, n))

    mix = mix_ref[...]
    hi, lo = two_sum(hi_ref[...], lo_ref[...] + (mix + mix.T))
    hi_body, hi_diag = fold(hi)
    lo_body, lo_diag = fold(lo)
    ca = ca_ref[...] + ac_ref[...].T
    q = half // 2
    tq = t // 2

    def put(ref, first):
        def pick(v, size):
            return jnp.where(first, v[:size, :], v[size:, :])

        ref[0:q, :] = pick(hi_body, q)
        ref[q : q + 8, :] = hi_diag
        ref[q + 8 : 2 * q + 8, :] = pick(lo_body, q)
        ref[2 * q + 8 : 2 * q + 16, :] = lo_diag
        ref[2 * q + 16 :, :] = pick(ca, tq)

    put(keep_ref, core == 0)
    put(send_ref, core == 1)


def local_gram(core, panel, trailing):
    n, rows = panel.shape
    t = trailing.shape[0]
    steps = rows // CHUNK
    out = jax.ShapeDtypeStruct((n // 2 + 16 + t // 2, n), F32)
    vmem, hbm = pl.BlockSpec(memory_space=pltpu.VMEM), pl.BlockSpec(memory_space=pltpu.HBM)
    return pl.pallas_call(
        gram_kernel,
        in_specs=[pl.BlockSpec(memory_space=pltpu.SMEM), hbm, hbm],
        out_specs=[vmem, vmem],
        out_shape=[out, out],
        scratch_shapes=[
            pltpu.VMEM((steps, n, CHUNK), F32),
            pltpu.VMEM((steps, t, CHUNK), F32),
            pltpu.VMEM((steps, 3 * (n + t), CHUNK), BF16),
            pltpu.VMEM((n, n), F32),
            pltpu.VMEM((n, n), F32),
            pltpu.VMEM((n, n), F32),
            pltpu.VMEM((t, n), F32),
            pltpu.VMEM((n, t), F32),
            pltpu.SemaphoreType.DMA((2, steps)),
        ],
        compiler_params=pltpu.CompilerParams(vmem_limit_bytes=32 << 20),
        name="gram",
    )(core, panel, trailing)


def add_packed(words, *arrays):
    parts, errors = list(arrays), []
    while len(parts) > 1:
        pairs = []
        for a, b in zip(parts[::2], parts[1::2]):
            errors.append(two_sum(a[:words], b[:words])[1])
            pairs.append(a + b)
        parts = pairs
    error = errors[0] if len(errors) == 1 else (errors[0] + errors[1]) + errors[2]
    rest = parts[0].shape[0] - 2 * words
    return parts[0] + jnp.pad(error, ((words, rest), (0, 0)))


def exchange(value, mask):
    size = lax.axis_size(AXES)
    return lax.ppermute(value, AXES, [(s, s ^ mask) for s in range(size)])


def chol_inv(s):
    blocks = len(s)
    n = 8 * blocks
    rid, lid = iota((8, n), 0), iota((8, n), 1)
    w = [jnp.where(lid == rid + 8 * r, 1.0, 0.0) for r in range(blocks)]
    s = list(s)
    for first in range(0, n, PANEL_COLS):
        r0 = first // 8
        cols = [
            [jnp.broadcast_to(s[r][:, first + k : first + k + 1], (8, n)) for r in range(r0, blocks)]
            for k in range(PANEL_COLS)
        ]
        scales = []
        for k in range(PANEL_COLS):
            pivot = cols[k][0][k : k + 1, :]
            inv = 1.0 / pivot
            mult = [c * inv for c in cols[k]]
            mult[0] = jnp.where(rid > k, mult[0], 0.0)
            for later in range(k + 1, PANEL_COLS):
                e = cols[later][0][k : k + 1, :]
                cols[later] = [c - m * e for c, m in zip(cols[later], mult)]
            srow, wrow = s[r0][k : k + 1, :], w[r0][k : k + 1, :]
            for i, m in enumerate(mult):
                s[r0 + i] = s[r0 + i] - m * srow
                w[r0 + i] = w[r0 + i] - m * wrow
            scales.append(lax.rsqrt(pivot))
        for k, d in enumerate(scales):
            w[r0] = jnp.where(rid == k, w[r0] * d, w[r0])
    return w


def split3(x):
    x1 = x.astype(BF16)
    rest = x - x1.astype(F32)
    x2 = rest.astype(BF16)
    return x1, x2, (rest - x2.astype(F32)).astype(BF16)


def apply_factors(wz, scale, panel, trailing, basis, updated, words, basis_buf, updated_buf, sems):
    n, rows = panel.shape
    w1, w2, w3 = split3(wz)
    for k, w in enumerate((w1, w2, w1, w2, w1, w3)):
        words[:, k * n : (k + 1) * n] = w
    copies = []
    for k in range(rows // OUT_CHUNK):
        at = pl.ds(k * OUT_CHUNK, OUT_CHUNK)
        a1, a2, a3 = split3(panel[:, at])
        out = nn(words[...], jnp.concatenate([a1, a2, a2, a1, a3, a1], axis=0))
        basis_buf[k] = out[:n, :] * scale
        updated_buf[k] = trailing[:, at] - out[n:, :]
        for copy in (
            pltpu.make_async_copy(basis_buf.at[k], basis.at[:, at], sems.at[0, k]),
            pltpu.make_async_copy(updated_buf.at[k], updated.at[:, at], sems.at[1, k]),
        ):
            copy.start()
            copies.append(copy)
    for copy in copies:
        copy.wait()


def factor_kernel(
    rows_all, core_ref, own_ref, other_ref, panel, trailing, basis, updated, upper_ref, coup_ref,
    wcat, gcat, tcat, v_ref, panel_buf, trail_buf, in_sems, words, basis_buf, updated_buf, out_sems,
):
    loads = (
        pltpu.make_async_copy(panel, panel_buf, in_sems.at[0]),
        pltpu.make_async_copy(trailing, trail_buf, in_sems.at[1]),
    )
    for load in loads:
        load.start()
    n = upper_ref.shape[0]
    t = coup_ref.shape[0]
    half, q, tq = n // 2, n // 4, t // 2
    first = core_ref[0] == 0
    own, other = own_ref[...], other_ref[...]
    a, b = jnp.where(first, own, other), jnp.where(first, other, own)
    i, j = iota((n, n), 0), iota((n, n), 1)
    hi_, hj_ = iota((half, n), 0), iota((half, n), 1)

    def unfold(start):
        body = jnp.concatenate([a[start : start + q, :], b[start : start + q, :]], axis=0)
        diag = jnp.broadcast_to(a[start + q : start + q + 1, :], (half, n))
        top = jnp.where((hj_ < half) & (hi_ >= hj_), pltpu.roll(body, half, 1), 0.0)
        keep = jnp.where((hj_ < half) | (hi_ < hj_ - half), body, 0.0)
        bottom = jnp.where(hi_ == hj_ - half, diag, keep)
        part = jnp.concatenate([top, bottom], axis=0)
        return jnp.where(i == j, part, part + part.T)

    g_hi, g_lo = unfold(0), unfold(q + 8)
    ca = jnp.concatenate([a[2 * q + 16 :, :], b[2 * q + 16 :, :]], axis=0)
    g_hi, g_lo = two_sum(g_hi, g_lo)

    diag = jnp.sum(jnp.where(i == j, g_hi, 0.0), axis=0, keepdims=True)
    pc, inv_pc = power_below(jnp.sqrt(diag))
    ic = jnp.broadcast_to(inv_pc, (n, n))
    eq = ic * ic.T
    s_hi, s_lo = g_hi * eq, g_lo * eq

    w = jnp.concatenate(chol_inv([s_hi[8 * r : 8 * r + 8, :] for r in range(n // 8)]), axis=0)

    qr, inv_qr = power_below(jnp.max(jnp.abs(w), axis=1, keepdims=True))
    wd = slices(w * (inv_qr * 64.0), None, 3)
    qs = qr * (1.0 / 64.0)
    wt = (wd[0] + wd[1] * 2.0**-8 + wd[2] * 2.0**-16) * qs
    for k in range(3):
        wcat[:, k * n : (k + 1) * n] = wd[k].astype(BF16)
    gd = slices(s_hi * 32.0, s_lo * 32.0, 6)
    for k in range(6):
        gcat[(5 - k) * n : (6 - k) * n, :] = gd[k].astype(BF16)

    def weigh(parts):
        hi, lo = parts[0], None
        for k, part in enumerate(parts[1:]):
            hi, err = two_sum(hi, part * 2.0 ** (-8 * (k + 1)))
            lo = err if lo is None else lo + err
        return two_sum(hi, lo)

    def t_level(k):
        width = min(k + 1, 3) * n
        return nn(wcat[:, 0:width], gcat[(5 - k) * n : (5 - k) * n + width, :])

    t_hi, t_lo = weigh([t_level(k) for k in range(6)])
    tau, inv_tau = power_below(jnp.max(jnp.abs(t_hi), axis=1, keepdims=True))
    td = slices(t_hi * (inv_tau * 64.0), t_lo * (inv_tau * 64.0), 4)
    for k in range(4):
        tcat[:, (3 - k) * n : (4 - k) * n] = td[k].astype(BF16)

    def m_level(k):
        width = min(k + 1, 3) * n
        return nt(tcat[:, (3 - k) * n : (3 - k) * n + width], wcat[:, 0:width])

    m_hi, m_lo = weigh([m_level(k) for k in range(4)])
    qb = jnp.broadcast_to(qs, (n, n))
    scale = qb.T * (qb * (tau * (1.0 / 2048.0)))
    e = (m_hi * scale - jnp.where(i == j, 1.0, 0.0)) + m_lo * scale

    def phi(x):
        return jnp.where(i > j, x, jnp.where(i == j, 0.5 * x, 0.0))

    f = phi(e)
    size = jnp.sum(f * f)

    @pl.when(size <= SMALL * SMALL)
    def _():
        fb = f.astype(BF16)
        v_ref[...] = (jnp.where(i == j, 1.0, 0.0) - f) + (phi(nt(fb, fb)) + nn(fb, fb))

    @pl.when(jnp.logical_not(size <= SMALL * SMALL))
    def _():
        lower = jnp.where(i >= j, e, 0.0)
        full = jnp.where(i == j, e + 1.0, lower + lower.T)
        blocks = chol_inv([full[8 * r : 8 * r + 8, :] for r in range(n // 8)])
        for r in range(n // 8):
            v_ref[8 * r : 8 * r + 8, :] = blocks[r]

    v = v_ref[...]
    y = nt(wt, ca * inv_pc, precision=HIGHEST)
    t_true = t_hi * (qs * (1.0 / 32.0)) * jnp.broadcast_to(pc, (n, n))
    wide = nn(v, jnp.concatenate([wt, t_true, y], axis=1), precision=HIGHEST)
    w_new = wide[:, :n] * ic
    root = jnp.sqrt(jnp.float32(rows_all))
    upper_ref[...] = jnp.where(i <= j, wide[:, n : 2 * n] / root, 0.0)
    coupling_t = wide[:, 2 * n :].T
    coup_ref[...] = coupling_t
    wz = jnp.concatenate([w_new, nn(coupling_t, w_new, precision=HIGHEST)], axis=0)
    for load in loads:
        load.wait()
    apply_factors(wz, root, panel_buf, trail_buf, basis, updated, words, basis_buf, updated_buf, out_sems)


def factor(core, own, other, panel, trailing, rows_all):
    n, rows = panel.shape
    t = trailing.shape[0]
    steps = rows // OUT_CHUNK
    vmem, hbm = pl.BlockSpec(memory_space=pltpu.VMEM), pl.BlockSpec(memory_space=pltpu.HBM)
    return pl.pallas_call(
        lambda *refs: factor_kernel(rows_all, *refs),
        in_specs=[pl.BlockSpec(memory_space=pltpu.SMEM), vmem, vmem, hbm, hbm],
        out_specs=[hbm, hbm, vmem, vmem],
        out_shape=[
            jax.ShapeDtypeStruct((n, rows), F32),
            jax.ShapeDtypeStruct((t, rows), F32),
            jax.ShapeDtypeStruct((n, n), F32),
            jax.ShapeDtypeStruct((t, n), F32),
        ],
        scratch_shapes=[
            pltpu.VMEM((n, 3 * n), BF16),
            pltpu.VMEM((6 * n, n), BF16),
            pltpu.VMEM((n, 4 * n), BF16),
            pltpu.VMEM((n, n), F32),
            pltpu.VMEM((n, rows), F32),
            pltpu.VMEM((t, rows), F32),
            pltpu.SemaphoreType.DMA((2,)),
            pltpu.VMEM((n + t, 6 * n), BF16),
            pltpu.VMEM((steps, n, OUT_CHUNK), F32),
            pltpu.VMEM((steps, t, OUT_CHUNK), F32),
            pltpu.SemaphoreType.DMA((2, steps)),
        ],
        compiler_params=pltpu.CompilerParams(vmem_limit_bytes=48 << 20),
        name="factor",
    )(core, own, other, panel, trailing)


def shards(panel, trailing):
    n, t = panel.shape[0], trailing.shape[0]
    rows_all = panel.shape[1] * lax.axis_size(AXES)
    core = jnp.reshape(lax.axis_index("gy") % 2, (1,)).astype(jnp.int32)
    words = n // 4 + 8
    panel, trailing = (pltpu.with_memory_space_constraint(a, pltpu.HBM) for a in (panel, trailing))
    keep, send = local_gram(core, panel, trailing)
    total = add_packed(words, keep, exchange(send, 4))
    for masks in ((1, 3, 2), (8, 72, 64), (16, 48, 32)):
        near, wrap, far = (exchange(total, m) for m in masks)
        total = add_packed(words, total, near, far, wrap)
    other = exchange(total, 4)
    basis_t, updated, upper, coupling_t = factor(core, total, other, panel, trailing, rows_all)
    return basis_t, upper, coupling_t.T, updated


def solution(mesh):
    placed = (P(None, AXES), P(None, AXES))
    return jax.shard_map(
        shards,
        mesh=mesh,
        in_specs=placed,
        out_specs=(P(None, AXES), P(), P(), P(None, AXES)),
        check_vma=False,
    )
```

```python
import jax
import jax.numpy as jnp
from jax import lax
from jax.experimental import pallas as pl
from jax.experimental.pallas import tpu as pltpu
from jax.sharding import PartitionSpec as P

AXES = ("gx", "gy", "gz")
HIGHEST = lax.Precision.HIGHEST
F32 = jnp.float32
BF16 = jnp.bfloat16
CHUNK = 2048
OUT_CHUNK = 512
PANEL_COLS = 8
SMALL = 4e-3
MAGIC = 1.5 * 2.0**23


def round_int(x):
    return (x + MAGIC) - MAGIC


def two_sum(a, b):
    total = a + b
    part = total - a
    return total, (a - (total - part)) + (b - part)


def snap(x):
    c = x * 4097.0
    return c - (c - x)


def power_below(x):
    p = snap(jnp.exp2(jnp.floor(jnp.log2(jnp.maximum(x, 1e-30)))))
    return p, snap(1.0 / p)


def slices(hi, lo, count):
    digits = []
    for k in range(count):
        d = round_int(hi)
        digits.append(d)
        if k < count - 1:
            hi = (hi - d) * 256.0
            if lo is not None:
                lo = lo * 256.0
                new = hi + lo
                lo = lo - (new - hi)
                hi = new
    return digits


def nt(a, b, **kw):
    return lax.dot_general(a, b, (((1,), (1,)), ((), ())), preferred_element_type=F32, **kw)


def nn(a, b, **kw):
    return lax.dot_general(a, b, (((1,), (0,)), ((), ())), preferred_element_type=F32, **kw)


def iota(shape, axis):
    return lax.broadcasted_iota(jnp.int32, shape, axis)


def gram_kernel(core_ref, panel, trail, keep_ref, send_ref, pbuf, tbuf, ops, hi_ref, lo_ref, mix_ref, ca_ref, ac_ref, sems):
    n, rows = panel.shape
    t = trail.shape[0]
    steps = rows // CHUNK
    copies = []
    for k in range(steps):
        at = pl.ds(k * CHUNK, CHUNK)
        pair = (
            pltpu.make_async_copy(panel.at[:, at], pbuf.at[k], sems.at[0, k]),
            pltpu.make_async_copy(trail.at[:, at], tbuf.at[k], sems.at[1, k]),
        )
        for copy in pair:
            copy.start()
        copies.append(pair)

    def split(k):
        copies[k][0].wait()
        x = pbuf[k]
        p, inv = power_below(jnp.max(jnp.abs(x), axis=1, keepdims=True))
        a = x * (inv * 32.0)
        d1 = round_int(a)
        r1 = (a - d1) * 256.0
        d2 = round_int(r1)
        d3 = (r1 - d2) * 256.0
        copies[k][1].wait()
        c = tbuf[k]
        c1 = c.astype(BF16)
        rc = c - c1.astype(F32)
        c2 = rc.astype(BF16)
        c3 = rc - c2.astype(F32)
        at = 0
        for part in (c3, d1, d2, d3, c1, c2):
            ops[k, at : at + part.shape[0], :] = part.astype(BF16)
            at += part.shape[0]
        return p

    def product(k, p):
        left = nt(ops[k, 0 : t + 2 * n, :], ops[k, t : t + 2 * n, :])
        right = nt(ops[k, t : t + 3 * n, :], ops[k, t + 2 * n :, :])
        c3d1, left = left[:t, :n], left[t:, :]
        row = jnp.broadcast_to(p * (1.0 / 32.0), (n, n))
        col = row.T
        scale = row * col
        h, e = two_sum(left[:n, :n], (left[:n, n:] + left[n:, :n]) * 2.0**-8)
        e = e + (left[n:, n:] * 2.0**-16 + right[2 * n :, :n] * 2.0**-32)
        mix = (right[:n, :n] * 2.0**-16 + right[n : 2 * n, :n] * 2.0**-24) * scale
        ac = right[2 * n :, n : n + t] * 2.0**-16 + right[n : 2 * n, n + t :] * 2.0**-8
        ac = ac + (right[n : 2 * n, n : n + t] * 2.0**-8 + right[:n, n + t :])
        ac = (ac + right[:n, n : n + t]) * row[:, :t]
        ca = c3d1 * col[:t, :]
        if k == 0:
            hi_ref[...], lo_ref[...] = h * scale, e * scale
            mix_ref[...], ca_ref[...], ac_ref[...] = mix, ca, ac
        else:
            hi, err = two_sum(hi_ref[...], h * scale)
            hi_ref[...] = hi
            lo_ref[...] += err + e * scale
            mix_ref[...] += mix
            ca_ref[...] += ca
            ac_ref[...] += ac

    p = split(0)
    for k in range(steps):
        following = split(k + 1) if k + 1 < steps else None
        product(k, p)
        p = following

    core = core_ref[0]
    half = n // 2
    i, j = iota((half, n), 0), iota((half, n), 1)

    def fold(g):
        top, bottom = g[:half, :], g[half:, :]
        body = jnp.where((j >= half) & (i >= j - half), pltpu.roll(top, half, 1), bottom)
        diag = jnp.sum(jnp.where(i == j - half, bottom, 0.0), axis=0, keepdims=True)
        return body, jnp.broadcast_to(diag, (8, n))

    mix = mix_ref[...]
    hi, lo = two_sum(hi_ref[...], lo_ref[...] + (mix + mix.T))
    hi_body, hi_diag = fold(hi)
    lo_body, lo_diag = fold(lo)
    ca = ca_ref[...] + ac_ref[...].T
    q = half // 2
    tq = t // 2

    def put(ref, first):
        def pick(v, size):
            return jnp.where(first, v[:size, :], v[size:, :])

        ref[0:q, :] = pick(hi_body, q)
        ref[q : q + 8, :] = hi_diag
        ref[q + 8 : 2 * q + 8, :] = pick(lo_body, q)
        ref[2 * q + 8 : 2 * q + 16, :] = lo_diag
        ref[2 * q + 16 :, :] = pick(ca, tq)

    put(keep_ref, core == 0)
    put(send_ref, core == 1)


def local_gram(core, panel, trailing):
    n, rows = panel.shape
    t = trailing.shape[0]
    steps = rows // CHUNK
    out = jax.ShapeDtypeStruct((n // 2 + 16 + t // 2, n), F32)
    vmem, hbm = pl.BlockSpec(memory_space=pltpu.VMEM), pl.BlockSpec(memory_space=pltpu.HBM)
    return pl.pallas_call(
        gram_kernel,
        in_specs=[pl.BlockSpec(memory_space=pltpu.SMEM), hbm, hbm],
        out_specs=[vmem, vmem],
        out_shape=[out, out],
        scratch_shapes=[
            pltpu.VMEM((steps, n, CHUNK), F32),
            pltpu.VMEM((steps, t, CHUNK), F32),
            pltpu.VMEM((steps, 3 * (n + t), CHUNK), BF16),
            pltpu.VMEM((n, n), F32),
            pltpu.VMEM((n, n), F32),
            pltpu.VMEM((n, n), F32),
            pltpu.VMEM((t, n), F32),
            pltpu.VMEM((n, t), F32),
            pltpu.SemaphoreType.DMA((2, steps)),
        ],
        compiler_params=pltpu.CompilerParams(vmem_limit_bytes=32 << 20),
        name="gram",
    )(core, panel, trailing)


def add_packed(words, *arrays):
    parts, errors = list(arrays), []
    while len(parts) > 1:
        pairs = []
        for a, b in zip(parts[::2], parts[1::2]):
            errors.append(two_sum(a[:words], b[:words])[1])
            pairs.append(a + b)
        parts = pairs
    error = errors[0] if len(errors) == 1 else (errors[0] + errors[1]) + errors[2]
    rest = parts[0].shape[0] - 2 * words
    return parts[0] + jnp.pad(error, ((words, rest), (0, 0)))


def exchange(value, mask):
    size = lax.axis_size(AXES)
    return lax.ppermute(value, AXES, [(s, s ^ mask) for s in range(size)])


def chol_inv(s):
    blocks = len(s)
    n = 8 * blocks
    rid, lid = iota((8, n), 0), iota((8, n), 1)
    w = [jnp.where(lid == rid + 8 * r, 1.0, 0.0) for r in range(blocks)]
    s = list(s)
    for first in range(0, n, PANEL_COLS):
        r0 = first // 8
        cols = [
            [jnp.broadcast_to(s[r][:, first + k : first + k + 1], (8, n)) for r in range(r0, blocks)]
            for k in range(PANEL_COLS)
        ]
        scales = []
        for k in range(PANEL_COLS):
            pivot = cols[k][0][k : k + 1, :]
            inv = 1.0 / pivot
            mult = [c * inv for c in cols[k]]
            mult[0] = jnp.where(rid > k, mult[0], 0.0)
            for later in range(k + 1, PANEL_COLS):
                e = cols[later][0][k : k + 1, :]
                cols[later] = [c - m * e for c, m in zip(cols[later], mult)]
            srow, wrow = s[r0][k : k + 1, :], w[r0][k : k + 1, :]
            for i, m in enumerate(mult):
                s[r0 + i] = s[r0 + i] - m * srow
                w[r0 + i] = w[r0 + i] - m * wrow
            scales.append(lax.rsqrt(pivot))
        for k, d in enumerate(scales):
            w[r0] = jnp.where(rid == k, w[r0] * d, w[r0])
    return w


def split3(x):
    x1 = x.astype(BF16)
    rest = x - x1.astype(F32)
    x2 = rest.astype(BF16)
    return x1, x2, (rest - x2.astype(F32)).astype(BF16)


def apply_factors(wz, scale, panel, trailing, basis, updated, words, basis_buf, updated_buf, sems):
    n, rows = panel.shape
    w1, w2, w3 = split3(wz)
    for k, w in enumerate((w1, w2, w1, w2, w1, w3)):
        words[:, k * n : (k + 1) * n] = w
    copies = []
    for k in range(rows // OUT_CHUNK):
        at = pl.ds(k * OUT_CHUNK, OUT_CHUNK)
        a1, a2, a3 = split3(panel[:, at])
        out = nn(words[...], jnp.concatenate([a1, a2, a2, a1, a3, a1], axis=0))
        basis_buf[k] = out[:n, :] * scale
        updated_buf[k] = trailing[:, at] - out[n:, :]
        for copy in (
            pltpu.make_async_copy(basis_buf.at[k], basis.at[:, at], sems.at[0, k]),
            pltpu.make_async_copy(updated_buf.at[k], updated.at[:, at], sems.at[1, k]),
        ):
            copy.start()
            copies.append(copy)
    for copy in copies:
        copy.wait()


def factor_kernel(
    rows_all, core_ref, own_ref, other_ref, panel, trailing, basis, updated, upper_ref, coup_ref,
    wcat, gcat, tcat, v_ref, panel_buf, trail_buf, in_sems, words, basis_buf, updated_buf, out_sems,
):
    loads = (
        pltpu.make_async_copy(panel, panel_buf, in_sems.at[0]),
        pltpu.make_async_copy(trailing, trail_buf, in_sems.at[1]),
    )
    for load in loads:
        load.start()
    n = upper_ref.shape[0]
    t = coup_ref.shape[0]
    half, q, tq = n // 2, n // 4, t // 2
    first = core_ref[0] == 0
    own, other = own_ref[...], other_ref[...]
    a, b = jnp.where(first, own, other), jnp.where(first, other, own)
    i, j = iota((n, n), 0), iota((n, n), 1)
    hi_, hj_ = iota((half, n), 0), iota((half, n), 1)

    def unfold(start):
        body = jnp.concatenate([a[start : start + q, :], b[start : start + q, :]], axis=0)
        diag = jnp.broadcast_to(a[start + q : start + q + 1, :], (half, n))
        top = jnp.where((hj_ < half) & (hi_ >= hj_), pltpu.roll(body, half, 1), 0.0)
        keep = jnp.where((hj_ < half) | (hi_ < hj_ - half), body, 0.0)
        bottom = jnp.where(hi_ == hj_ - half, diag, keep)
        part = jnp.concatenate([top, bottom], axis=0)
        return jnp.where(i == j, part, part + part.T)

    g_hi, g_lo = unfold(0), unfold(q + 8)
    ca = jnp.concatenate([a[2 * q + 16 :, :], b[2 * q + 16 :, :]], axis=0)
    g_hi, g_lo = two_sum(g_hi, g_lo)

    diag = jnp.sum(jnp.where(i == j, g_hi, 0.0), axis=0, keepdims=True)
    pc, inv_pc = power_below(jnp.sqrt(diag))
    ic = jnp.broadcast_to(inv_pc, (n, n))
    eq = ic * ic.T
    s_hi, s_lo = g_hi * eq, g_lo * eq

    w = jnp.concatenate(chol_inv([s_hi[8 * r : 8 * r + 8, :] for r in range(n // 8)]), axis=0)

    qr, inv_qr = power_below(jnp.max(jnp.abs(w), axis=1, keepdims=True))
    wd = slices(w * (inv_qr * 64.0), None, 3)
    qs = qr * (1.0 / 64.0)
    wt = (wd[0] + wd[1] * 2.0**-8 + wd[2] * 2.0**-16) * qs
    for k in range(3):
        wcat[:, k * n : (k + 1) * n] = wd[k].astype(BF16)
    gd = slices(s_hi * 32.0, s_lo * 32.0, 6)
    for k in range(6):
        gcat[(5 - k) * n : (6 - k) * n, :] = gd[k].astype(BF16)

    def weigh(parts):
        hi, lo = parts[0], None
        for k, part in enumerate(parts[1:]):
            hi, err = two_sum(hi, part * 2.0 ** (-8 * (k + 1)))
            lo = err if lo is None else lo + err
        return two_sum(hi, lo)

    def t_level(k):
        width = min(k + 1, 3) * n
        return nn(wcat[:, 0:width], gcat[(5 - k) * n : (5 - k) * n + width, :])

    t_hi, t_lo = weigh([t_level(k) for k in range(6)])
    tau, inv_tau = power_below(jnp.max(jnp.abs(t_hi), axis=1, keepdims=True))
    td = slices(t_hi * (inv_tau * 64.0), t_lo * (inv_tau * 64.0), 4)
    for k in range(4):
        tcat[:, (3 - k) * n : (4 - k) * n] = td[k].astype(BF16)

    def m_level(k):
        width = min(k + 1, 3) * n
        return nt(tcat[:, (3 - k) * n : (3 - k) * n + width], wcat[:, 0:width])

    m_hi, m_lo = weigh([m_level(k) for k in range(4)])
    qb = jnp.broadcast_to(qs, (n, n))
    scale = qb.T * (qb * (tau * (1.0 / 2048.0)))
    e = (m_hi * scale - jnp.where(i == j, 1.0, 0.0)) + m_lo * scale

    def phi(x):
        return jnp.where(i > j, x, jnp.where(i == j, 0.5 * x, 0.0))

    f = phi(e)
    size = jnp.sum(f * f)

    @pl.when(size <= SMALL * SMALL)
    def _():
        fb = f.astype(BF16)
        v_ref[...] = (jnp.where(i == j, 1.0, 0.0) - f) + (phi(nt(fb, fb)) + nn(fb, fb))

    @pl.when(jnp.logical_not(size <= SMALL * SMALL))
    def _():
        lower = jnp.where(i >= j, e, 0.0)
        full = jnp.where(i == j, e + 1.0, lower + lower.T)
        blocks = chol_inv([full[8 * r : 8 * r + 8, :] for r in range(n // 8)])
        for r in range(n // 8):
            v_ref[8 * r : 8 * r + 8, :] = blocks[r]

    v = v_ref[...]
    y = nt(wt, ca * inv_pc, precision=HIGHEST)
    t_true = t_hi * (qs * (1.0 / 32.0)) * jnp.broadcast_to(pc, (n, n))
    wide = nn(v, jnp.concatenate([wt, t_true, y], axis=1), precision=HIGHEST)
    w_new = wide[:, :n] * ic
    root = jnp.sqrt(jnp.float32(rows_all))
    upper_ref[...] = jnp.where(i <= j, wide[:, n : 2 * n] / root, 0.0)
    coupling_t = wide[:, 2 * n :].T
    coup_ref[...] = coupling_t
    wz = jnp.concatenate([w_new, nn(coupling_t, w_new, precision=HIGHEST)], axis=0)
    for load in loads:
        load.wait()
    apply_factors(wz, root, panel_buf, trail_buf, basis, updated, words, basis_buf, updated_buf, out_sems)


def factor(core, own, other, panel, trailing, rows_all):
    n, rows = panel.shape
    t = trailing.shape[0]
    steps = rows // OUT_CHUNK
    vmem, hbm = pl.BlockSpec(memory_space=pltpu.VMEM), pl.BlockSpec(memory_space=pltpu.HBM)
    return pl.pallas_call(
        lambda *refs: factor_kernel(rows_all, *refs),
        in_specs=[pl.BlockSpec(memory_space=pltpu.SMEM), vmem, vmem, hbm, hbm],
        out_specs=[hbm, hbm, vmem, vmem],
        out_shape=[
            jax.ShapeDtypeStruct((n, rows), F32),
            jax.ShapeDtypeStruct((t, rows), F32),
            jax.ShapeDtypeStruct((n, n), F32),
            jax.ShapeDtypeStruct((t, n), F32),
        ],
        scratch_shapes=[
            pltpu.VMEM((n, 3 * n), BF16),
            pltpu.VMEM((6 * n, n), BF16),
            pltpu.VMEM((n, 4 * n), BF16),
            pltpu.VMEM((n, n), F32),
            pltpu.VMEM((n, rows), F32),
            pltpu.VMEM((t, rows), F32),
            pltpu.SemaphoreType.DMA((2,)),
            pltpu.VMEM((n + t, 6 * n), BF16),
            pltpu.VMEM((steps, n, OUT_CHUNK), F32),
            pltpu.VMEM((steps, t, OUT_CHUNK), F32),
            pltpu.SemaphoreType.DMA((2, steps)),
        ],
        compiler_params=pltpu.CompilerParams(vmem_limit_bytes=48 << 20),
        name="factor",
    )(core, own, other, panel, trailing)


def shards(panel, trailing):
    n, t = panel.shape[0], trailing.shape[0]
    rows_all = panel.shape[1] * lax.axis_size(AXES)
    core = jnp.reshape(lax.axis_index("gy") % 2, (1,)).astype(jnp.int32)
    words = n // 4 + 8
    panel, trailing = (pltpu.with_memory_space_constraint(a, pltpu.HBM) for a in (panel, trailing))
    keep, send = local_gram(core, panel, trailing)
    total = add_packed(words, keep, exchange(send, 4))
    for masks in ((1, 3, 2), (8, 72, 64), (16, 48, 32)):
        near, wrap, far = (exchange(total, m) for m in masks)
        total = add_packed(words, total, wrap, near, far)
    other = exchange(total, 4)
    basis_t, updated, upper, coupling_t = factor(core, total, other, panel, trailing, rows_all)
    return basis_t, upper, coupling_t.T, updated


def solution(mesh):
    placed = (P(None, AXES), P(None, AXES))
    return jax.shard_map(
        shards,
        mesh=mesh,
        in_specs=placed,
        out_specs=(P(None, AXES), P(), P(), P(None, AXES)),
        check_vma=False,
    )
```

```python
import jax
import jax.numpy as jnp
from jax import lax
from jax.experimental import pallas as pl
from jax.experimental.pallas import tpu as pltpu
from jax.sharding import PartitionSpec as P

AXES = ("gx", "gy", "gz")
HIGHEST = lax.Precision.HIGHEST
F32 = jnp.float32
BF16 = jnp.bfloat16
CHUNK = 2048
OUT_CHUNK = 512
NEAR = 4
SMALL = 4e-3
MAGIC = 1.5 * 2.0**23


def round_int(x):
    return (x + MAGIC) - MAGIC


def two_sum(a, b):
    total = a + b
    part = total - a
    return total, (a - (total - part)) + (b - part)


def snap(x):
    c = x * (2.0**23 + 1.0)
    return c - (c - x)


def power_near(x):
    p = snap(jnp.maximum(x, 1e-30))
    return p, snap(1.0 / p)


def slices(hi, lo, count):
    digits = []
    for k in range(count):
        d = round_int(hi)
        digits.append(d)
        if k < count - 1:
            hi = (hi - d) * 256.0
            if lo is not None:
                lo = lo * 256.0
                new = hi + lo
                lo = lo - (new - hi)
                hi = new
    return digits


def nt(a, b, **kw):
    return lax.dot_general(a, b, (((1,), (1,)), ((), ())), preferred_element_type=F32, **kw)


def nn(a, b, **kw):
    return lax.dot_general(a, b, (((1,), (0,)), ((), ())), preferred_element_type=F32, **kw)


def iota(shape, axis):
    return lax.broadcasted_iota(jnp.int32, shape, axis)


def gram_kernel(core_ref, panel, trail, keep_ref, send_ref, pbuf, tbuf, ops, hi_ref, lo_ref, mix_ref, ca_ref, ac_ref, sems):
    n, rows = panel.shape
    t = trail.shape[0]
    steps = rows // CHUNK
    copies = []
    for k in range(steps):
        at = pl.ds(k * CHUNK, CHUNK)
        pair = (
            pltpu.make_async_copy(panel.at[:, at], pbuf.at[k], sems.at[0, k]),
            pltpu.make_async_copy(trail.at[:, at], tbuf.at[k], sems.at[1, k]),
        )
        for copy in pair:
            copy.start()
        copies.append(pair)

    def split(k):
        copies[k][0].wait()
        x = pbuf[k]
        p, inv = power_near(jnp.max(jnp.abs(x), axis=1, keepdims=True))
        a = x * (inv * 32.0)
        d1 = round_int(a)
        r1 = (a - d1) * 256.0
        d2 = round_int(r1)
        d3 = (r1 - d2) * 256.0
        copies[k][1].wait()
        c = tbuf[k]
        c1 = c.astype(BF16)
        rc = c - c1.astype(F32)
        c2 = rc.astype(BF16)
        c3 = rc - c2.astype(F32)
        at = 0
        for part in (c3, d1, d2, d3, c1, c2):
            ops[k, at : at + part.shape[0], :] = part.astype(BF16)
            at += part.shape[0]
        return p

    def product(k, p):
        left = nt(ops[k, 0 : t + 2 * n, :], ops[k, t : t + 2 * n, :])
        right = nt(ops[k, t : t + 3 * n, :], ops[k, t + 2 * n :, :])
        c3d1, left = left[:t, :n], left[t:, :]
        row = jnp.broadcast_to(p * (1.0 / 32.0), (n, n))
        col = row.T
        scale = row * col
        h, e = two_sum(left[:n, :n], (left[:n, n:] + left[n:, :n]) * 2.0**-8)
        e = e + (left[n:, n:] * 2.0**-16 + right[2 * n :, :n] * 2.0**-32)
        mix = (right[:n, :n] * 2.0**-16 + right[n : 2 * n, :n] * 2.0**-24) * scale
        ac = right[2 * n :, n : n + t] * 2.0**-16 + right[n : 2 * n, n + t :] * 2.0**-8
        ac = ac + (right[n : 2 * n, n : n + t] * 2.0**-8 + right[:n, n + t :])
        ac = (ac + right[:n, n : n + t]) * row[:, :t]
        ca = c3d1 * col[:t, :]
        if k == 0:
            hi_ref[...], lo_ref[...] = h * scale, e * scale
            mix_ref[...], ca_ref[...], ac_ref[...] = mix, ca, ac
        else:
            hi, err = two_sum(hi_ref[...], h * scale)
            hi_ref[...] = hi
            lo_ref[...] += err + e * scale
            mix_ref[...] += mix
            ca_ref[...] += ca
            ac_ref[...] += ac

    p = split(0)
    for k in range(steps):
        following = split(k + 1) if k + 1 < steps else None
        product(k, p)
        p = following

    core = core_ref[0]
    half = n // 2
    i, j = iota((half, n), 0), iota((half, n), 1)

    def fold(g):
        top, bottom = g[:half, :], g[half:, :]
        body = jnp.where((j >= half) & (i >= j - half), pltpu.roll(top, half, 1), bottom)
        diag = jnp.sum(jnp.where(i == j - half, bottom, 0.0), axis=0, keepdims=True)
        return body, jnp.broadcast_to(diag, (8, n))

    mix = mix_ref[...]
    hi, lo = two_sum(hi_ref[...], lo_ref[...] + (mix + mix.T))
    hi_body, hi_diag = fold(hi)
    lo_body, lo_diag = fold(lo)
    ca = ca_ref[...] + ac_ref[...].T
    q = half // 2
    tq = t // 2

    def put(ref, first):
        def pick(v, size):
            return jnp.where(first, v[:size, :], v[size:, :])

        ref[0:q, :] = pick(hi_body, q)
        ref[q : q + 8, :] = hi_diag
        ref[q + 8 : 2 * q + 8, :] = pick(lo_body, q)
        ref[2 * q + 8 : 2 * q + 16, :] = lo_diag
        ref[2 * q + 16 :, :] = pick(ca, tq)

    put(keep_ref, core == 0)
    put(send_ref, core == 1)


def local_gram(core, panel, trailing):
    n, rows = panel.shape
    t = trailing.shape[0]
    steps = rows // CHUNK
    out = jax.ShapeDtypeStruct((n // 2 + 16 + t // 2, n), F32)
    vmem, hbm = pl.BlockSpec(memory_space=pltpu.VMEM), pl.BlockSpec(memory_space=pltpu.HBM)
    return pl.pallas_call(
        gram_kernel,
        in_specs=[pl.BlockSpec(memory_space=pltpu.SMEM), hbm, hbm],
        out_specs=[vmem, vmem],
        out_shape=[out, out],
        scratch_shapes=[
            pltpu.VMEM((steps, n, CHUNK), F32),
            pltpu.VMEM((steps, t, CHUNK), F32),
            pltpu.VMEM((steps, 3 * (n + t), CHUNK), BF16),
            pltpu.VMEM((n, n), F32),
            pltpu.VMEM((n, n), F32),
            pltpu.VMEM((n, n), F32),
            pltpu.VMEM((t, n), F32),
            pltpu.VMEM((n, t), F32),
            pltpu.SemaphoreType.DMA((2, steps)),
        ],
        compiler_params=pltpu.CompilerParams(vmem_limit_bytes=32 << 20),
        name="gram",
    )(core, panel, trailing)


def add_packed(words, *arrays):
    parts, errors = list(arrays), []
    while len(parts) > 1:
        pairs = []
        for a, b in zip(parts[::2], parts[1::2]):
            errors.append(two_sum(a[:words], b[:words])[1])
            pairs.append(a + b)
        parts = pairs
    error = errors[0] if len(errors) == 1 else (errors[0] + errors[1]) + errors[2]
    rest = parts[0].shape[0] - 2 * words
    return parts[0] + jnp.pad(error, ((words, rest), (0, 0)))


def exchange(value, mask):
    size = lax.axis_size(AXES)
    return lax.ppermute(value, AXES, [(s, s ^ mask) for s in range(size)])


def split3(x):
    x1 = x.astype(BF16)
    rest = x - x1.astype(F32)
    x2 = rest.astype(BF16)
    return x1, x2, (rest - x2.astype(F32)).astype(BF16)


def chol_inv(s):
    blocks = len(s)
    n = 8 * blocks
    rid, lid = iota((8, n), 0), iota((8, n), 1)
    s, w = list(s), [jnp.where(lid == rid + 8 * r, 1.0, 0.0) for r in range(blocks)]

    def spread(r, first):
        return [jnp.broadcast_to(s[r][:, first + k : first + k + 1], (8, n)) for k in range(8)]

    cols = {r: spread(r, 0) for r in (0, 1)}
    for r0 in range(blocks):
        first = 8 * r0
        near = range(r0, min(r0 + 3, blocks))
        for r in near:
            if r not in cols:
                cols[r] = spread(r, first)
        ahead = {r: spread(r, first + 8) for r in near if r > r0}
        edges, invs, srows, wrows, scales = {}, [], [], [], []
        inv_rows = jnp.zeros((8, n), F32)
        for k in range(8):
            pivot = cols[r0][k][k : k + 1, :]
            inv = 1.0 / pivot
            mult = {r: cols[r][k] * inv for r in near}
            mult[r0] = jnp.where(rid > k, mult[r0], 0.0)
            for later in range(k + 1, 8):
                edges[k, later] = edge = cols[r0][later][k : k + 1, :]
                for r in near:
                    cols[r][later] = cols[r][later] - mult[r] * edge
            if ahead:
                for q in range(8):
                    edge = cols[r0 + 1][k][q : q + 1, :]
                    for r in ahead:
                        ahead[r][q] = ahead[r][q] - mult[r] * edge
            srow, wrow = s[r0][k : k + 1, :], w[r0][k : k + 1, :]
            for r in near:
                s[r] = s[r] - mult[r] * srow
                w[r] = w[r] - mult[r] * wrow
            inv_rows = jnp.where(rid == k, inv, inv_rows)
            invs.append(inv)
            srows.append(srow)
            wrows.append(wrow)
            scales.append(lax.rsqrt(pivot))
        for r in range(r0 + 3, min(r0 + NEAR, blocks)):
            col = spread(r, first)
            for k in range(8):
                mult = col[k] * invs[k]
                for later in range(k + 1, 8):
                    col[later] = col[later] - mult * edges[k, later]
                s[r] = s[r] - mult * srows[k]
                w[r] = w[r] - mult * wrows[k]
        if r0 + NEAR < blocks:
            l1, l2, l3 = split3(s[r0] * inv_rows)
            r1, r2, r3 = split3(jnp.concatenate([s[r0], w[r0]], axis=1))

            def stack(*parts):
                return jnp.concatenate([p.astype(F32) for p in parts], axis=0).astype(BF16)

            left, right = stack(l1, l2, l1, l2, l1, l3), stack(r1, r2, r2, r1, r3, r1)
            update = lax.dot_general(left, right, (((0,), (0,)), ((), ())), preferred_element_type=F32)
            for r in range(r0 + NEAR, blocks):
                s[r] = s[r] - update[8 * r : 8 * r + 8, :n]
                w[r] = w[r] - update[8 * r : 8 * r + 8, n:]
        for k, d in enumerate(scales):
            w[r0] = jnp.where(rid == k, w[r0] * d, w[r0])
        cols = ahead
    return w


def apply_factors(wz, scale, panel, trailing, basis, updated, words, basis_buf, updated_buf, sems):
    n, rows = panel.shape
    w1, w2, w3 = split3(wz)
    for k, w in enumerate((w1, w2, w1, w2, w1, w3)):
        words[:, k * n : (k + 1) * n] = w
    copies = []
    for k in range(rows // OUT_CHUNK):
        at = pl.ds(k * OUT_CHUNK, OUT_CHUNK)
        a1, a2, a3 = split3(panel[:, at])
        out = nn(words[...], jnp.concatenate([a1, a2, a2, a1, a3, a1], axis=0))
        basis_buf[k] = out[:n, :] * scale
        updated_buf[k] = trailing[:, at] - out[n:, :]
        for copy in (
            pltpu.make_async_copy(basis_buf.at[k], basis.at[:, at], sems.at[0, k]),
            pltpu.make_async_copy(updated_buf.at[k], updated.at[:, at], sems.at[1, k]),
        ):
            copy.start()
            copies.append(copy)
    for copy in copies:
        copy.wait()


def factor_kernel(
    rows_all, core_ref, own_ref, other_ref, panel, trailing, basis, updated, upper_ref, coup_ref,
    wcat, gcat, tcat, v_ref, panel_buf, trail_buf, in_sems, words, basis_buf, updated_buf, out_sems,
):
    loads = (
        pltpu.make_async_copy(panel, panel_buf, in_sems.at[0]),
        pltpu.make_async_copy(trailing, trail_buf, in_sems.at[1]),
    )
    for load in loads:
        load.start()
    n = upper_ref.shape[0]
    t = coup_ref.shape[0]
    half, q, tq = n // 2, n // 4, t // 2
    first = core_ref[0] == 0
    own, other = own_ref[...], other_ref[...]
    a, b = jnp.where(first, own, other), jnp.where(first, other, own)
    i, j = iota((n, n), 0), iota((n, n), 1)
    hi_, hj_ = iota((half, n), 0), iota((half, n), 1)

    def unfold(start):
        body = jnp.concatenate([a[start : start + q, :], b[start : start + q, :]], axis=0)
        diag = jnp.broadcast_to(a[start + q : start + q + 1, :], (half, n))
        top = jnp.where((hj_ < half) & (hi_ >= hj_), pltpu.roll(body, half, 1), 0.0)
        keep = jnp.where((hj_ < half) | (hi_ < hj_ - half), body, 0.0)
        bottom = jnp.where(hi_ == hj_ - half, diag, keep)
        part = jnp.concatenate([top, bottom], axis=0)
        return jnp.where(i == j, part, part + part.T)

    g_hi, g_lo = unfold(0), unfold(q + 8)
    ca = jnp.concatenate([a[2 * q + 16 :, :], b[2 * q + 16 :, :]], axis=0)
    g_hi, g_lo = two_sum(g_hi, g_lo)

    diag = jnp.sum(jnp.where(i == j, g_hi, 0.0), axis=0, keepdims=True)
    pc, inv_pc = power_near(jnp.sqrt(diag))
    ic = jnp.broadcast_to(inv_pc, (n, n))
    eq = ic * ic.T
    s_hi, s_lo = g_hi * eq, g_lo * eq

    w = jnp.concatenate(chol_inv([s_hi[8 * r : 8 * r + 8, :] for r in range(n // 8)]), axis=0)

    qr, inv_qr = power_near(jnp.max(jnp.abs(w), axis=1, keepdims=True))
    wd = slices(w * (inv_qr * 64.0), None, 3)
    qs = qr * (1.0 / 64.0)
    wt = (wd[0] + wd[1] * 2.0**-8 + wd[2] * 2.0**-16) * qs
    for k in range(3):
        wcat[:, k * n : (k + 1) * n] = wd[k].astype(BF16)
    gd = slices(s_hi * 32.0, s_lo * 32.0, 6)
    for k in range(6):
        gcat[(5 - k) * n : (6 - k) * n, :] = gd[k].astype(BF16)

    def weigh(parts):
        hi, lo = parts[0], None
        for k, part in enumerate(parts[1:]):
            hi, err = two_sum(hi, part * 2.0 ** (-8 * (k + 1)))
            lo = err if lo is None else lo + err
        return two_sum(hi, lo)

    def t_level(k):
        width = min(k + 1, 3) * n
        return nn(wcat[:, 0:width], gcat[(5 - k) * n : (5 - k) * n + width, :])

    t_hi, t_lo = weigh([t_level(k) for k in range(6)])
    tau, inv_tau = power_near(jnp.max(jnp.abs(t_hi), axis=1, keepdims=True))
    td = slices(t_hi * (inv_tau * 64.0), t_lo * (inv_tau * 64.0), 4)
    for k in range(4):
        tcat[:, (3 - k) * n : (4 - k) * n] = td[k].astype(BF16)

    def m_level(k):
        width = min(k + 1, 3) * n
        return nt(tcat[:, (3 - k) * n : (3 - k) * n + width], wcat[:, 0:width])

    m_hi, m_lo = weigh([m_level(k) for k in range(4)])
    qb = jnp.broadcast_to(qs, (n, n))
    scale = qb.T * (qb * (tau * (1.0 / 2048.0)))
    e = (m_hi * scale - jnp.where(i == j, 1.0, 0.0)) + m_lo * scale

    def phi(x):
        return jnp.where(i > j, x, jnp.where(i == j, 0.5 * x, 0.0))

    f = phi(e)
    size = jnp.sum(f * f)

    @pl.when(size <= SMALL * SMALL)
    def _():
        fb = f.astype(BF16)
        v_ref[...] = (jnp.where(i == j, 1.0, 0.0) - f) + (phi(nt(fb, fb)) + nn(fb, fb))

    @pl.when(jnp.logical_not(size <= SMALL * SMALL))
    def _():
        lower = jnp.where(i >= j, e, 0.0)
        full = jnp.where(i == j, e + 1.0, lower + lower.T)
        blocks = chol_inv([full[8 * r : 8 * r + 8, :] for r in range(n // 8)])
        for r in range(n // 8):
            v_ref[8 * r : 8 * r + 8, :] = blocks[r]

    v = v_ref[...]
    y = nt(wt, ca * inv_pc, precision=HIGHEST)
    t_true = t_hi * (qs * (1.0 / 32.0)) * jnp.broadcast_to(pc, (n, n))
    wide = nn(v, jnp.concatenate([wt, t_true, y], axis=1), precision=HIGHEST)
    w_new = wide[:, :n] * ic
    root = jnp.sqrt(jnp.float32(rows_all))
    upper_ref[...] = jnp.where(i <= j, wide[:, n : 2 * n] / root, 0.0)
    coupling_t = wide[:, 2 * n :].T
    coup_ref[...] = coupling_t
    wz = jnp.concatenate([w_new, nn(coupling_t, w_new, precision=HIGHEST)], axis=0)
    for load in loads:
        load.wait()
    apply_factors(wz, root, panel_buf, trail_buf, basis, updated, words, basis_buf, updated_buf, out_sems)


def factor(core, own, other, panel, trailing, rows_all):
    n, rows = panel.shape
    t = trailing.shape[0]
    steps = rows // OUT_CHUNK
    vmem, hbm = pl.BlockSpec(memory_space=pltpu.VMEM), pl.BlockSpec(memory_space=pltpu.HBM)
    return pl.pallas_call(
        lambda *refs: factor_kernel(rows_all, *refs),
        in_specs=[pl.BlockSpec(memory_space=pltpu.SMEM), vmem, vmem, hbm, hbm],
        out_specs=[hbm, hbm, vmem, vmem],
        out_shape=[
            jax.ShapeDtypeStruct((n, rows), F32),
            jax.ShapeDtypeStruct((t, rows), F32),
            jax.ShapeDtypeStruct((n, n), F32),
            jax.ShapeDtypeStruct((t, n), F32),
        ],
        scratch_shapes=[
            pltpu.VMEM((n, 3 * n), BF16),
            pltpu.VMEM((6 * n, n), BF16),
            pltpu.VMEM((n, 4 * n), BF16),
            pltpu.VMEM((n, n), F32),
            pltpu.VMEM((n, rows), F32),
            pltpu.VMEM((t, rows), F32),
            pltpu.SemaphoreType.DMA((2,)),
            pltpu.VMEM((n + t, 6 * n), BF16),
            pltpu.VMEM((steps, n, OUT_CHUNK), F32),
            pltpu.VMEM((steps, t, OUT_CHUNK), F32),
            pltpu.SemaphoreType.DMA((2, steps)),
        ],
        compiler_params=pltpu.CompilerParams(vmem_limit_bytes=48 << 20),
        name="factor",
    )(core, own, other, panel, trailing)


def shards(panel, trailing):
    n, t = panel.shape[0], trailing.shape[0]
    rows_all = panel.shape[1] * lax.axis_size(AXES)
    core = jnp.reshape(lax.axis_index("gy") % 2, (1,)).astype(jnp.int32)
    words = n // 4 + 8
    panel, trailing = (pltpu.with_memory_space_constraint(a, pltpu.HBM) for a in (panel, trailing))
    keep, send = local_gram(core, panel, trailing)
    total = add_packed(words, keep, exchange(send, 4))
    for masks in ((1, 3, 2), (8, 72, 64), (16, 48, 32)):
        near, wrap, far = (exchange(total, m) for m in masks)
        total = add_packed(words, total, wrap, near, far)
    other = exchange(total, 4)
    basis_t, updated, upper, coupling_t = factor(core, total, other, panel, trailing, rows_all)
    return basis_t, upper, coupling_t.T, updated


def solution(mesh):
    placed = (P(None, AXES), P(None, AXES))
    return jax.shard_map(
        shards,
        mesh=mesh,
        in_specs=placed,
        out_specs=(P(None, AXES), P(), P(), P(None, AXES)),
        check_vma=False,
    )
```

```python
import jax
import jax.numpy as jnp
from jax import lax
from jax.experimental import pallas as pl
from jax.experimental.pallas import tpu as pltpu
from jax.sharding import PartitionSpec as P

AXES = ("gx", "gy", "gz")
HIGHEST = lax.Precision.HIGHEST
F32 = jnp.float32
BF16 = jnp.bfloat16
CHUNK = 2048
OUT_CHUNK = 512
NEAR = 4
SMALL = 2e-2
MAGIC = 1.5 * 2.0**23


def round_int(x):
    return (x + MAGIC) - MAGIC


def two_sum(a, b):
    total = a + b
    part = total - a
    return total, (a - (total - part)) + (b - part)


def snap(x):
    c = x * (2.0**23 + 1.0)
    return c - (c - x)


def power_near(x):
    p = snap(jnp.maximum(x, 1e-30))
    return p, snap(1.0 / p)


def slices(hi, lo, count):
    digits = []
    for k in range(count):
        d = round_int(hi)
        digits.append(d)
        if k < count - 1:
            hi = (hi - d) * 256.0
            if lo is not None:
                lo = lo * 256.0
                new = hi + lo
                lo = lo - (new - hi)
                hi = new
    return digits


def nt(a, b, **kw):
    return lax.dot_general(a, b, (((1,), (1,)), ((), ())), preferred_element_type=F32, **kw)


def nn(a, b, **kw):
    return lax.dot_general(a, b, (((1,), (0,)), ((), ())), preferred_element_type=F32, **kw)


def iota(shape, axis):
    return lax.broadcasted_iota(jnp.int32, shape, axis)


def gram_kernel(core_ref, panel, trail, keep_ref, send_ref, pbuf, tbuf, ops, hi_ref, lo_ref, mix_ref, ca_ref, ac_ref, sems):
    n, rows = panel.shape
    t = trail.shape[0]
    steps = rows // CHUNK
    copies = []
    for k in range(steps):
        at = pl.ds(k * CHUNK, CHUNK)
        pair = (
            pltpu.make_async_copy(panel.at[:, at], pbuf.at[k], sems.at[0, k]),
            pltpu.make_async_copy(trail.at[:, at], tbuf.at[k], sems.at[1, k]),
        )
        for copy in pair:
            copy.start()
        copies.append(pair)

    def split(k):
        copies[k][0].wait()
        x = pbuf[k]
        p, inv = power_near(jnp.max(jnp.abs(x), axis=1, keepdims=True))
        a = x * (inv * 32.0)
        d1 = round_int(a)
        r1 = (a - d1) * 256.0
        d2 = round_int(r1)
        d3 = (r1 - d2) * 256.0
        copies[k][1].wait()
        c = tbuf[k]
        c1 = c.astype(BF16)
        rc = c - c1.astype(F32)
        c2 = rc.astype(BF16)
        c3 = rc - c2.astype(F32)
        at = 0
        for part in (c3, d1, d2, d3, c1, c2):
            ops[k, at : at + part.shape[0], :] = part.astype(BF16)
            at += part.shape[0]
        return p

    def product(k, p):
        left = nt(ops[k, 0 : t + 2 * n, :], ops[k, t : t + 2 * n, :])
        right = nt(ops[k, t : t + 3 * n, :], ops[k, t + 2 * n :, :])
        c3d1, left = left[:t, :n], left[t:, :]
        row = jnp.broadcast_to(p * (1.0 / 32.0), (n, n))
        col = row.T
        scale = row * col
        h, e = two_sum(left[:n, :n], (left[:n, n:] + left[n:, :n]) * 2.0**-8)
        e = e + (left[n:, n:] * 2.0**-16 + right[2 * n :, :n] * 2.0**-32)
        mix = (right[:n, :n] * 2.0**-16 + right[n : 2 * n, :n] * 2.0**-24) * scale
        ac = right[2 * n :, n : n + t] * 2.0**-16 + right[n : 2 * n, n + t :] * 2.0**-8
        ac = ac + (right[n : 2 * n, n : n + t] * 2.0**-8 + right[:n, n + t :])
        ac = (ac + right[:n, n : n + t]) * row[:, :t]
        ca = c3d1 * col[:t, :]
        if k == 0:
            hi_ref[...], lo_ref[...] = h * scale, e * scale
            mix_ref[...], ca_ref[...], ac_ref[...] = mix, ca, ac
        else:
            hi, err = two_sum(hi_ref[...], h * scale)
            hi_ref[...] = hi
            lo_ref[...] += err + e * scale
            mix_ref[...] += mix
            ca_ref[...] += ca
            ac_ref[...] += ac

    p = split(0)
    for k in range(steps):
        following = split(k + 1) if k + 1 < steps else None
        product(k, p)
        p = following

    core = core_ref[0]
    half = n // 2
    i, j = iota((half, n), 0), iota((half, n), 1)

    def fold(g):
        top, bottom = g[:half, :], g[half:, :]
        body = jnp.where((j >= half) & (i >= j - half), pltpu.roll(top, half, 1), bottom)
        diag = jnp.sum(jnp.where(i == j - half, bottom, 0.0), axis=0, keepdims=True)
        return body, jnp.broadcast_to(diag, (8, n))

    mix = mix_ref[...]
    hi, lo = two_sum(hi_ref[...], lo_ref[...] + (mix + mix.T))
    hi_body, hi_diag = fold(hi)
    lo_body, lo_diag = fold(lo)
    ca = ca_ref[...] + ac_ref[...].T
    q = half // 2
    tq = t // 2

    def put(ref, first):
        def pick(v, size):
            return jnp.where(first, v[:size, :], v[size:, :])

        ref[0:q, :] = pick(hi_body, q)
        ref[q : q + 8, :] = hi_diag
        ref[q + 8 : 2 * q + 8, :] = pick(lo_body, q)
        ref[2 * q + 8 : 2 * q + 16, :] = lo_diag
        ref[2 * q + 16 :, :] = pick(ca, tq)

    put(keep_ref, core == 0)
    put(send_ref, core == 1)


def local_gram(core, panel, trailing):
    n, rows = panel.shape
    t = trailing.shape[0]
    steps = rows // CHUNK
    out = jax.ShapeDtypeStruct((n // 2 + 16 + t // 2, n), F32)
    vmem, hbm = pl.BlockSpec(memory_space=pltpu.VMEM), pl.BlockSpec(memory_space=pltpu.HBM)
    return pl.pallas_call(
        gram_kernel,
        in_specs=[pl.BlockSpec(memory_space=pltpu.SMEM), hbm, hbm],
        out_specs=[vmem, vmem],
        out_shape=[out, out],
        scratch_shapes=[
            pltpu.VMEM((steps, n, CHUNK), F32),
            pltpu.VMEM((steps, t, CHUNK), F32),
            pltpu.VMEM((steps, 3 * (n + t), CHUNK), BF16),
            pltpu.VMEM((n, n), F32),
            pltpu.VMEM((n, n), F32),
            pltpu.VMEM((n, n), F32),
            pltpu.VMEM((t, n), F32),
            pltpu.VMEM((n, t), F32),
            pltpu.SemaphoreType.DMA((2, steps)),
        ],
        compiler_params=pltpu.CompilerParams(vmem_limit_bytes=32 << 20),
        name="gram",
    )(core, panel, trailing)


def add_packed(words, *arrays):
    parts, errors = list(arrays), []
    while len(parts) > 1:
        pairs = []
        for a, b in zip(parts[::2], parts[1::2]):
            errors.append(two_sum(a[:words], b[:words])[1])
            pairs.append(a + b)
        parts = pairs
    error = errors[0] if len(errors) == 1 else (errors[0] + errors[1]) + errors[2]
    rest = parts[0].shape[0] - 2 * words
    return parts[0] + jnp.pad(error, ((words, rest), (0, 0)))


def exchange(value, mask):
    size = lax.axis_size(AXES)
    return lax.ppermute(value, AXES, [(s, s ^ mask) for s in range(size)])


def split3(x):
    x1 = x.astype(BF16)
    rest = x - x1.astype(F32)
    x2 = rest.astype(BF16)
    return x1, x2, (rest - x2.astype(F32)).astype(BF16)


def chol_inv(s):
    blocks = len(s)
    n = 8 * blocks
    rid, lid = iota((8, n), 0), iota((8, n), 1)
    s, w = list(s), [jnp.where(lid == rid + 8 * r, 1.0, 0.0) for r in range(blocks)]

    def spread(r, first):
        return [jnp.broadcast_to(s[r][:, first + k : first + k + 1], (8, n)) for k in range(8)]

    cols = {r: spread(r, 0) for r in (0, 1)}
    for r0 in range(blocks):
        first = 8 * r0
        near = range(r0, min(r0 + 3, blocks))
        for r in near:
            if r not in cols:
                cols[r] = spread(r, first)
        ahead = {r: spread(r, first + 8) for r in near if r > r0}
        edges, invs, srows, wrows, scales = {}, [], [], [], []
        inv_rows = jnp.zeros((8, n), F32)
        for k in range(8):
            pivot = cols[r0][k][k : k + 1, :]
            inv = 1.0 / pivot
            mult = {r: cols[r][k] * inv for r in near}
            mult[r0] = jnp.where(rid > k, mult[r0], 0.0)
            for later in range(k + 1, 8):
                edges[k, later] = edge = cols[r0][later][k : k + 1, :]
                for r in near:
                    cols[r][later] = cols[r][later] - mult[r] * edge
            if ahead:
                for q in range(8):
                    edge = cols[r0 + 1][k][q : q + 1, :]
                    for r in ahead:
                        ahead[r][q] = ahead[r][q] - mult[r] * edge
            srow, wrow = s[r0][k : k + 1, :], w[r0][k : k + 1, :]
            for r in near:
                s[r] = s[r] - mult[r] * srow
                w[r] = w[r] - mult[r] * wrow
            inv_rows = jnp.where(rid == k, inv, inv_rows)
            invs.append(inv)
            srows.append(srow)
            wrows.append(wrow)
            scales.append(lax.rsqrt(pivot))
        for r in range(r0 + 3, min(r0 + NEAR, blocks)):
            col = spread(r, first)
            for k in range(8):
                mult = col[k] * invs[k]
                for later in range(k + 1, 8):
                    col[later] = col[later] - mult * edges[k, later]
                s[r] = s[r] - mult * srows[k]
                w[r] = w[r] - mult * wrows[k]
        if r0 + NEAR < blocks:
            l1, l2, l3 = split3(s[r0] * inv_rows)
            r1, r2, r3 = split3(jnp.concatenate([s[r0], w[r0]], axis=1))

            def stack(*parts):
                return jnp.concatenate([p.astype(F32) for p in parts], axis=0).astype(BF16)

            left, right = stack(l1, l2, l1, l2, l1, l3), stack(r1, r2, r2, r1, r3, r1)
            update = lax.dot_general(left, right, (((0,), (0,)), ((), ())), preferred_element_type=F32)
            for r in range(r0 + NEAR, blocks):
                s[r] = s[r] - update[8 * r : 8 * r + 8, :n]
                w[r] = w[r] - update[8 * r : 8 * r + 8, n:]
        for k, d in enumerate(scales):
            w[r0] = jnp.where(rid == k, w[r0] * d, w[r0])
        cols = ahead
    return w


def apply_factors(wz, scale, panel, trailing, basis, updated, words, basis_buf, updated_buf, sems):
    n, rows = panel.shape
    w1, w2, w3 = split3(wz)
    for k, w in enumerate((w1, w2, w1, w2, w1, w3)):
        words[:, k * n : (k + 1) * n] = w
    copies = []
    for k in range(rows // OUT_CHUNK):
        at = pl.ds(k * OUT_CHUNK, OUT_CHUNK)
        a1, a2, a3 = split3(panel[:, at])
        out = nn(words[...], jnp.concatenate([a1, a2, a2, a1, a3, a1], axis=0))
        basis_buf[k] = out[:n, :] * scale
        updated_buf[k] = trailing[:, at] - out[n:, :]
        for copy in (
            pltpu.make_async_copy(basis_buf.at[k], basis.at[:, at], sems.at[0, k]),
            pltpu.make_async_copy(updated_buf.at[k], updated.at[:, at], sems.at[1, k]),
        ):
            copy.start()
            copies.append(copy)
    for copy in copies:
        copy.wait()


def factor_kernel(
    rows_all, core_ref, own_ref, other_ref, panel, trailing, basis, updated, upper_ref, coup_ref,
    wcat, gcat, tcat, v_ref, panel_buf, trail_buf, in_sems, words, basis_buf, updated_buf, out_sems,
):
    loads = (
        pltpu.make_async_copy(panel, panel_buf, in_sems.at[0]),
        pltpu.make_async_copy(trailing, trail_buf, in_sems.at[1]),
    )
    for load in loads:
        load.start()
    n = upper_ref.shape[0]
    t = coup_ref.shape[0]
    half, q, tq = n // 2, n // 4, t // 2
    first = core_ref[0] == 0
    own, other = own_ref[...], other_ref[...]
    a, b = jnp.where(first, own, other), jnp.where(first, other, own)
    i, j = iota((n, n), 0), iota((n, n), 1)
    hi_, hj_ = iota((half, n), 0), iota((half, n), 1)

    def unfold(start):
        body = jnp.concatenate([a[start : start + q, :], b[start : start + q, :]], axis=0)
        diag = jnp.broadcast_to(a[start + q : start + q + 1, :], (half, n))
        top = jnp.where((hj_ < half) & (hi_ >= hj_), pltpu.roll(body, half, 1), 0.0)
        keep = jnp.where((hj_ < half) | (hi_ < hj_ - half), body, 0.0)
        bottom = jnp.where(hi_ == hj_ - half, diag, keep)
        part = jnp.concatenate([top, bottom], axis=0)
        return jnp.where(i == j, part, part + part.T)

    g_hi, g_lo = unfold(0), unfold(q + 8)
    ca = jnp.concatenate([a[2 * q + 16 :, :], b[2 * q + 16 :, :]], axis=0)
    g_hi, g_lo = two_sum(g_hi, g_lo)

    diag = jnp.sum(jnp.where(i == j, g_hi, 0.0), axis=0, keepdims=True)
    pc, inv_pc = power_near(jnp.sqrt(diag))
    ic = jnp.broadcast_to(inv_pc, (n, n))
    eq = ic * ic.T
    s_hi, s_lo = g_hi * eq, g_lo * eq

    w = jnp.concatenate(chol_inv([s_hi[8 * r : 8 * r + 8, :] for r in range(n // 8)]), axis=0)

    qr, inv_qr = power_near(jnp.max(jnp.abs(w), axis=1, keepdims=True))
    wd = slices(w * (inv_qr * 64.0), None, 3)
    qs = qr * (1.0 / 64.0)
    wt = (wd[0] + wd[1] * 2.0**-8 + wd[2] * 2.0**-16) * qs
    for k in range(3):
        wcat[:, k * n : (k + 1) * n] = wd[k].astype(BF16)
    gd = slices(s_hi * 32.0, s_lo * 32.0, 6)
    for k in range(6):
        gcat[(5 - k) * n : (6 - k) * n, :] = gd[k].astype(BF16)

    def weigh(parts):
        hi, lo = parts[0], None
        for k, part in enumerate(parts[1:]):
            hi, err = two_sum(hi, part * 2.0 ** (-8 * (k + 1)))
            lo = err if lo is None else lo + err
        return two_sum(hi, lo)

    def t_level(k):
        width = min(k + 1, 3) * n
        return nn(wcat[:, 0:width], gcat[(5 - k) * n : (5 - k) * n + width, :])

    t_hi, t_lo = weigh([t_level(k) for k in range(6)])
    tau, inv_tau = power_near(jnp.max(jnp.abs(t_hi), axis=1, keepdims=True))
    td = slices(t_hi * (inv_tau * 64.0), t_lo * (inv_tau * 64.0), 4)
    for k in range(4):
        tcat[:, (3 - k) * n : (4 - k) * n] = td[k].astype(BF16)

    def m_level(k):
        width = min(k + 1, 3) * n
        return nt(tcat[:, (3 - k) * n : (3 - k) * n + width], wcat[:, 0:width])

    m_hi, m_lo = weigh([m_level(k) for k in range(4)])
    qb = jnp.broadcast_to(qs, (n, n))
    scale = qb.T * (qb * (tau * (1.0 / 2048.0)))
    e = (m_hi * scale - jnp.where(i == j, 1.0, 0.0)) + m_lo * scale

    def phi(x):
        return jnp.where(i > j, x, jnp.where(i == j, 0.5 * x, 0.0))

    f = phi(e)
    size = jnp.sum(f * f)

    @pl.when(size <= SMALL * SMALL)
    def _():
        fb = f.astype(BF16)
        f2, square = -phi(nt(fb, fb)), nn(fb, fb)
        f2b = f2.astype(BF16)
        ab = jnp.concatenate([fb, f2b], axis=1)
        ba = jnp.concatenate([f2b, fb], axis=1)
        third = phi(nt(ab, ba)) + nn(ab, jnp.concatenate([(f2 - square).astype(BF16), fb], axis=0))
        v_ref[...] = (jnp.where(i == j, 1.0, 0.0) - f) + ((square - f2) + third)

    @pl.when(jnp.logical_not(size <= SMALL * SMALL))
    def _():
        lower = jnp.where(i >= j, e, 0.0)
        full = jnp.where(i == j, e + 1.0, lower + lower.T)
        blocks = chol_inv([full[8 * r : 8 * r + 8, :] for r in range(n // 8)])
        for r in range(n // 8):
            v_ref[8 * r : 8 * r + 8, :] = blocks[r]

    v = v_ref[...]
    y = nt(wt, ca * inv_pc, precision=HIGHEST)
    t_true = t_hi * (qs * (1.0 / 32.0)) * jnp.broadcast_to(pc, (n, n))
    wide = nn(v, jnp.concatenate([wt, t_true, y], axis=1), precision=HIGHEST)
    w_new = wide[:, :n] * ic
    root = jnp.sqrt(jnp.float32(rows_all))
    upper_ref[...] = jnp.where(i <= j, wide[:, n : 2 * n] / root, 0.0)
    coupling_t = wide[:, 2 * n :].T
    coup_ref[...] = coupling_t
    wz = jnp.concatenate([w_new, nn(coupling_t, w_new, precision=HIGHEST)], axis=0)
    for load in loads:
        load.wait()
    apply_factors(wz, root, panel_buf, trail_buf, basis, updated, words, basis_buf, updated_buf, out_sems)


def factor(core, own, other, panel, trailing, rows_all):
    n, rows = panel.shape
    t = trailing.shape[0]
    steps = rows // OUT_CHUNK
    vmem, hbm = pl.BlockSpec(memory_space=pltpu.VMEM), pl.BlockSpec(memory_space=pltpu.HBM)
    return pl.pallas_call(
        lambda *refs: factor_kernel(rows_all, *refs),
        in_specs=[pl.BlockSpec(memory_space=pltpu.SMEM), vmem, vmem, hbm, hbm],
        out_specs=[hbm, hbm, vmem, vmem],
        out_shape=[
            jax.ShapeDtypeStruct((n, rows), F32),
            jax.ShapeDtypeStruct((t, rows), F32),
            jax.ShapeDtypeStruct((n, n), F32),
            jax.ShapeDtypeStruct((t, n), F32),
        ],
        scratch_shapes=[
            pltpu.VMEM((n, 3 * n), BF16),
            pltpu.VMEM((6 * n, n), BF16),
            pltpu.VMEM((n, 4 * n), BF16),
            pltpu.VMEM((n, n), F32),
            pltpu.VMEM((n, rows), F32),
            pltpu.VMEM((t, rows), F32),
            pltpu.SemaphoreType.DMA((2,)),
            pltpu.VMEM((n + t, 6 * n), BF16),
            pltpu.VMEM((steps, n, OUT_CHUNK), F32),
            pltpu.VMEM((steps, t, OUT_CHUNK), F32),
            pltpu.SemaphoreType.DMA((2, steps)),
        ],
        compiler_params=pltpu.CompilerParams(vmem_limit_bytes=48 << 20),
        name="factor",
    )(core, own, other, panel, trailing)


def shards(panel, trailing):
    n, t = panel.shape[0], trailing.shape[0]
    rows_all = panel.shape[1] * lax.axis_size(AXES)
    core = jnp.reshape(lax.axis_index("gy") % 2, (1,)).astype(jnp.int32)
    words = n // 4 + 8
    panel, trailing = (pltpu.with_memory_space_constraint(a, pltpu.HBM) for a in (panel, trailing))
    keep, send = local_gram(core, panel, trailing)
    total = add_packed(words, keep, exchange(send, 4))
    for masks in ((1, 3, 2), (8, 72, 64), (16, 48, 32)):
        near, wrap, far = (exchange(total, m) for m in masks)
        total = add_packed(words, total, wrap, near, far)
    other = exchange(total, 4)
    basis_t, updated, upper, coupling_t = factor(core, total, other, panel, trailing, rows_all)
    return basis_t, upper, coupling_t.T, updated


def solution(mesh):
    placed = (P(None, AXES), P(None, AXES))
    return jax.shard_map(
        shards,
        mesh=mesh,
        in_specs=placed,
        out_specs=(P(None, AXES), P(), P(), P(None, AXES)),
        check_vma=False,
    )
```

```python
import jax
import jax.numpy as jnp
from jax import lax
from jax.experimental import pallas as pl
from jax.experimental.pallas import tpu as pltpu
from jax.sharding import PartitionSpec as P

AXES = ("gx", "gy", "gz")
HIGHEST = lax.Precision.HIGHEST
F32 = jnp.float32
BF16 = jnp.bfloat16
CHUNKS = 4
OUT_CHUNK = 512
NEAR = 4
SMALL = 2e-2
MAGIC = 1.5 * 2.0**23


def round_int(x):
    return (x + MAGIC) - MAGIC


def two_sum(a, b):
    total = a + b
    part = total - a
    return total, (a - (total - part)) + (b - part)


def snap(x):
    c = x * (2.0**23 + 1.0)
    return c - (c - x)


def power_near(x):
    p = snap(jnp.maximum(x, 1e-30))
    return p, snap(1.0 / p)


def slices(hi, lo, count):
    digits = []
    for k in range(count):
        d = round_int(hi)
        digits.append(d)
        if k < count - 1:
            hi = (hi - d) * 256.0
            if lo is not None:
                lo = lo * 256.0
                new = hi + lo
                lo = lo - (new - hi)
                hi = new
    return digits


def nt(a, b, **kw):
    return lax.dot_general(a, b, (((1,), (1,)), ((), ())), preferred_element_type=F32, **kw)


def nn(a, b, **kw):
    return lax.dot_general(a, b, (((1,), (0,)), ((), ())), preferred_element_type=F32, **kw)


def iota(shape, axis):
    return lax.broadcasted_iota(jnp.int32, shape, axis)


def gram_kernel(core_ref, panel, trail, keep_ref, send_ref, pbuf, tbuf, ops, sems):
    n, rows = panel.shape
    t = trail.shape[0]
    width = rows // CHUNKS
    copies = []
    for k in range(CHUNKS):
        at = pl.ds(k * width, width)
        pair = (
            pltpu.make_async_copy(panel.at[:, at], pbuf.at[k], sems.at[0, k]),
            pltpu.make_async_copy(trail.at[:, at], tbuf.at[k], sems.at[1, k]),
        )
        for copy in pair:
            copy.start()
        copies.append(pair)

    top = jnp.zeros((n, 128), F32)
    for k in range(CHUNKS):
        copies[k][0].wait()
        x = jnp.abs(pbuf[k])
        for q in range(0, width, 128):
            top = jnp.maximum(top, x[:, q : q + 128])
    for k in range(CHUNKS):
        copies[k][1].wait()
    p, inv = power_near(jnp.max(top, axis=1, keepdims=True))

    def split(k):
        a = pbuf[k] * (inv * 32.0)
        d1 = round_int(a)
        r1 = (a - d1) * 256.0
        d2 = round_int(r1)
        d3 = (r1 - d2) * 256.0
        c = tbuf[k]
        c1 = c.astype(BF16)
        rc = c - c1.astype(F32)
        c2 = rc.astype(BF16)
        c3 = rc - c2.astype(F32)
        at = 0
        for part in (c3, d1, d2, d3, c1, c2):
            ops[k, at : at + part.shape[0], :] = part.astype(BF16)
            at += part.shape[0]

    left, right = None, None
    split(0)
    for k in range(CHUNKS):
        if k + 1 < CHUNKS:
            split(k + 1)
        l = nt(ops[k, 0 : t + 2 * n, :], ops[k, t : t + 2 * n, :])
        r = nt(ops[k, t : t + 3 * n, :], ops[k, t + 2 * n :, :])
        left, right = (l, r) if left is None else (left + l, right + r)

    c3d1, left = left[:t, :n], left[t:, :]
    row = jnp.broadcast_to(p * (1.0 / 32.0), (n, n))
    col = row.T
    scale = row * col
    h, e = two_sum(left[:n, :n], (left[:n, n:] + left[n:, :n]) * 2.0**-8)
    e = e + (left[n:, n:] * 2.0**-16 + right[2 * n :, :n] * 2.0**-32)
    mix = right[:n, :n] * 2.0**-16 + right[n : 2 * n, :n] * 2.0**-24
    ac = right[2 * n :, n : n + t] * 2.0**-16 + right[n : 2 * n, n + t :] * 2.0**-8
    ac = ac + (right[n : 2 * n, n : n + t] * 2.0**-8 + right[:n, n + t :])
    ca = (c3d1 + (ac + right[:n, n : n + t]).T) * col[:t, :]

    core = core_ref[0]
    half = n // 2
    i, j = iota((half, n), 0), iota((half, n), 1)

    def fold(g):
        top, bottom = g[:half, :], g[half:, :]
        body = jnp.where((j >= half) & (i >= j - half), pltpu.roll(top, half, 1), bottom)
        diag = jnp.sum(jnp.where(i == j - half, bottom, 0.0), axis=0, keepdims=True)
        return body, jnp.broadcast_to(diag, (8, n))

    hi, lo = two_sum(h * scale, (e + (mix + mix.T)) * scale)
    hi_body, hi_diag = fold(hi)
    lo_body, lo_diag = fold(lo)
    q = half // 2
    tq = t // 2

    def put(ref, first):
        def pick(v, size):
            return jnp.where(first, v[:size, :], v[size:, :])

        ref[0:q, :] = pick(hi_body, q)
        ref[q : q + 8, :] = hi_diag
        ref[q + 8 : 2 * q + 8, :] = pick(lo_body, q)
        ref[2 * q + 8 : 2 * q + 16, :] = lo_diag
        ref[2 * q + 16 :, :] = pick(ca, tq)

    put(keep_ref, core == 0)
    put(send_ref, core == 1)


def local_gram(core, panel, trailing):
    n, rows = panel.shape
    t = trailing.shape[0]
    width = rows // CHUNKS
    out = jax.ShapeDtypeStruct((n // 2 + 16 + t // 2, n), F32)
    vmem, hbm = pl.BlockSpec(memory_space=pltpu.VMEM), pl.BlockSpec(memory_space=pltpu.HBM)
    return pl.pallas_call(
        gram_kernel,
        in_specs=[pl.BlockSpec(memory_space=pltpu.SMEM), hbm, hbm],
        out_specs=[vmem, vmem],
        out_shape=[out, out],
        scratch_shapes=[
            pltpu.VMEM((CHUNKS, n, width), F32),
            pltpu.VMEM((CHUNKS, t, width), F32),
            pltpu.VMEM((CHUNKS, 3 * (n + t), width), BF16),
            pltpu.SemaphoreType.DMA((2, CHUNKS)),
        ],
        compiler_params=pltpu.CompilerParams(vmem_limit_bytes=32 << 20),
        name="gram",
    )(core, panel, trailing)


def add_packed(words, *arrays):
    parts, errors = list(arrays), []
    while len(parts) > 1:
        pairs = []
        for a, b in zip(parts[::2], parts[1::2]):
            errors.append(two_sum(a[:words], b[:words])[1])
            pairs.append(a + b)
        parts = pairs
    error = errors[0] if len(errors) == 1 else (errors[0] + errors[1]) + errors[2]
    rest = parts[0].shape[0] - 2 * words
    return parts[0] + jnp.pad(error, ((words, rest), (0, 0)))


def exchange(value, mask):
    size = lax.axis_size(AXES)
    return lax.ppermute(value, AXES, [(s, s ^ mask) for s in range(size)])


def split3(x):
    x1 = x.astype(BF16)
    rest = x - x1.astype(F32)
    x2 = rest.astype(BF16)
    return x1, x2, (rest - x2.astype(F32)).astype(BF16)


def chol_inv(s):
    blocks = len(s)
    n = 8 * blocks
    rid, lid = iota((8, n), 0), iota((8, n), 1)
    s, w = list(s), [jnp.where(lid == rid + 8 * r, 1.0, 0.0) for r in range(blocks)]

    def spread(r, first):
        return [jnp.broadcast_to(s[r][:, first + k : first + k + 1], (8, n)) for k in range(8)]

    cols = {r: spread(r, 0) for r in (0, 1)}
    for r0 in range(blocks):
        first = 8 * r0
        near = range(r0, min(r0 + 3, blocks))
        for r in near:
            if r not in cols:
                cols[r] = spread(r, first)
        ahead = {r: spread(r, first + 8) for r in near if r > r0}
        edges, invs, srows, wrows, scales = {}, [], [], [], []
        inv_rows = jnp.zeros((8, n), F32)
        for k in range(8):
            pivot = cols[r0][k][k : k + 1, :]
            inv = 1.0 / pivot
            mult = {r: cols[r][k] * inv for r in near}
            mult[r0] = jnp.where(rid > k, mult[r0], 0.0)
            for later in range(k + 1, 8):
                edges[k, later] = edge = cols[r0][later][k : k + 1, :]
                for r in near:
                    cols[r][later] = cols[r][later] - mult[r] * edge
            if ahead:
                for q in range(8):
                    edge = cols[r0 + 1][k][q : q + 1, :]
                    for r in ahead:
                        ahead[r][q] = ahead[r][q] - mult[r] * edge
            srow, wrow = s[r0][k : k + 1, :], w[r0][k : k + 1, :]
            for r in near:
                s[r] = s[r] - mult[r] * srow
                w[r] = w[r] - mult[r] * wrow
            inv_rows = jnp.where(rid == k, inv, inv_rows)
            invs.append(inv)
            srows.append(srow)
            wrows.append(wrow)
            scales.append(lax.rsqrt(pivot))
        for r in range(r0 + 3, min(r0 + NEAR, blocks)):
            col = spread(r, first)
            for k in range(8):
                mult = col[k] * invs[k]
                for later in range(k + 1, 8):
                    col[later] = col[later] - mult * edges[k, later]
                s[r] = s[r] - mult * srows[k]
                w[r] = w[r] - mult * wrows[k]
        if r0 + NEAR < blocks:
            l1, l2, l3 = split3(s[r0] * inv_rows)
            r1, r2, r3 = split3(jnp.concatenate([s[r0], w[r0]], axis=1))

            def stack(*parts):
                return jnp.concatenate([p.astype(F32) for p in parts], axis=0).astype(BF16)

            left, right = stack(l1, l2, l1, l2, l1, l3), stack(r1, r2, r2, r1, r3, r1)
            update = lax.dot_general(left, right, (((0,), (0,)), ((), ())), preferred_element_type=F32)
            for r in range(r0 + NEAR, blocks):
                s[r] = s[r] - update[8 * r : 8 * r + 8, :n]
                w[r] = w[r] - update[8 * r : 8 * r + 8, n:]
        for k, d in enumerate(scales):
            w[r0] = jnp.where(rid == k, w[r0] * d, w[r0])
        cols = ahead
    return w


def apply_factors(wz, scale, panel, trailing, basis, updated, words, basis_buf, updated_buf, sems):
    n, rows = panel.shape
    w1, w2, w3 = split3(wz)
    for k, w in enumerate((w1, w2, w1, w2, w1, w3)):
        words[:, k * n : (k + 1) * n] = w
    copies = []
    for k in range(rows // OUT_CHUNK):
        at = pl.ds(k * OUT_CHUNK, OUT_CHUNK)
        a1, a2, a3 = split3(panel[:, at])
        out = nn(words[...], jnp.concatenate([a1, a2, a2, a1, a3, a1], axis=0))
        basis_buf[k] = out[:n, :] * scale
        updated_buf[k] = trailing[:, at] - out[n:, :]
        for copy in (
            pltpu.make_async_copy(basis_buf.at[k], basis.at[:, at], sems.at[0, k]),
            pltpu.make_async_copy(updated_buf.at[k], updated.at[:, at], sems.at[1, k]),
        ):
            copy.start()
            copies.append(copy)
    for copy in copies:
        copy.wait()


def factor_kernel(
    rows_all, core_ref, own_ref, other_ref, panel, trailing, basis, updated, upper_ref, coup_ref,
    wcat, gcat, tcat, v_ref, panel_buf, trail_buf, in_sems, words, basis_buf, updated_buf, out_sems,
):
    loads = (
        pltpu.make_async_copy(panel, panel_buf, in_sems.at[0]),
        pltpu.make_async_copy(trailing, trail_buf, in_sems.at[1]),
    )
    for load in loads:
        load.start()
    n = upper_ref.shape[0]
    t = coup_ref.shape[0]
    half, q, tq = n // 2, n // 4, t // 2
    first = core_ref[0] == 0
    own, other = own_ref[...], other_ref[...]
    a, b = jnp.where(first, own, other), jnp.where(first, other, own)
    i, j = iota((n, n), 0), iota((n, n), 1)
    hi_, hj_ = iota((half, n), 0), iota((half, n), 1)

    def unfold(start):
        body = jnp.concatenate([a[start : start + q, :], b[start : start + q, :]], axis=0)
        diag = jnp.broadcast_to(a[start + q : start + q + 1, :], (half, n))
        top = jnp.where((hj_ < half) & (hi_ >= hj_), pltpu.roll(body, half, 1), 0.0)
        keep = jnp.where((hj_ < half) | (hi_ < hj_ - half), body, 0.0)
        bottom = jnp.where(hi_ == hj_ - half, diag, keep)
        part = jnp.concatenate([top, bottom], axis=0)
        return jnp.where(i == j, part, part + part.T)

    g_hi, g_lo = unfold(0), unfold(q + 8)
    ca = jnp.concatenate([a[2 * q + 16 :, :], b[2 * q + 16 :, :]], axis=0)
    g_hi, g_lo = two_sum(g_hi, g_lo)

    diag = jnp.sum(jnp.where(i == j, g_hi, 0.0), axis=0, keepdims=True)
    pc, inv_pc = power_near(jnp.sqrt(diag))
    ic = jnp.broadcast_to(inv_pc, (n, n))
    eq = ic * ic.T
    s_hi, s_lo = g_hi * eq, g_lo * eq

    w = jnp.concatenate(chol_inv([s_hi[8 * r : 8 * r + 8, :] for r in range(n // 8)]), axis=0)

    qr, inv_qr = power_near(jnp.max(jnp.abs(w), axis=1, keepdims=True))
    wd = slices(w * (inv_qr * 64.0), None, 3)
    qs = qr * (1.0 / 64.0)
    wt = (wd[0] + wd[1] * 2.0**-8 + wd[2] * 2.0**-16) * qs
    for k in range(3):
        wcat[:, k * n : (k + 1) * n] = wd[k].astype(BF16)
    gd = slices(s_hi * 32.0, s_lo * 32.0, 6)
    for k in range(6):
        gcat[(5 - k) * n : (6 - k) * n, :] = gd[k].astype(BF16)

    def weigh(parts):
        hi, lo = parts[0], None
        for k, part in enumerate(parts[1:]):
            hi, err = two_sum(hi, part * 2.0 ** (-8 * (k + 1)))
            lo = err if lo is None else lo + err
        return two_sum(hi, lo)

    def t_level(k):
        width = min(k + 1, 3) * n
        return nn(wcat[:, 0:width], gcat[(5 - k) * n : (5 - k) * n + width, :])

    t_hi, t_lo = weigh([t_level(k) for k in range(6)])
    tau, inv_tau = power_near(jnp.max(jnp.abs(t_hi), axis=1, keepdims=True))
    td = slices(t_hi * (inv_tau * 64.0), t_lo * (inv_tau * 64.0), 4)
    for k in range(4):
        tcat[:, (3 - k) * n : (4 - k) * n] = td[k].astype(BF16)

    def m_level(k):
        width = min(k + 1, 3) * n
        return nt(tcat[:, (3 - k) * n : (3 - k) * n + width], wcat[:, 0:width])

    m_hi, m_lo = weigh([m_level(k) for k in range(4)])
    qb = jnp.broadcast_to(qs, (n, n))
    scale = qb.T * (qb * (tau * (1.0 / 2048.0)))
    e = (m_hi * scale - jnp.where(i == j, 1.0, 0.0)) + m_lo * scale

    def phi(x):
        return jnp.where(i > j, x, jnp.where(i == j, 0.5 * x, 0.0))

    f = phi(e)
    size = jnp.sum(f * f)

    @pl.when(size <= SMALL * SMALL)
    def _():
        fb = f.astype(BF16)
        f2, square = -phi(nt(fb, fb)), nn(fb, fb)
        f2b = f2.astype(BF16)
        ab = jnp.concatenate([fb, f2b], axis=1)
        ba = jnp.concatenate([f2b, fb], axis=1)
        third = phi(nt(ab, ba)) + nn(ab, jnp.concatenate([(f2 - square).astype(BF16), fb], axis=0))
        v_ref[...] = (jnp.where(i == j, 1.0, 0.0) - f) + ((square - f2) + third)

    @pl.when(jnp.logical_not(size <= SMALL * SMALL))
    def _():
        lower = jnp.where(i >= j, e, 0.0)
        full = jnp.where(i == j, e + 1.0, lower + lower.T)
        blocks = chol_inv([full[8 * r : 8 * r + 8, :] for r in range(n // 8)])
        for r in range(n // 8):
            v_ref[8 * r : 8 * r + 8, :] = blocks[r]

    v = v_ref[...]
    y = nt(wt, ca * inv_pc, precision=HIGHEST)
    t_true = t_hi * (qs * (1.0 / 32.0)) * jnp.broadcast_to(pc, (n, n))
    wide = nn(v, jnp.concatenate([wt, t_true, y], axis=1), precision=HIGHEST)
    w_new = wide[:, :n] * ic
    root = jnp.sqrt(jnp.float32(rows_all))
    upper_ref[...] = jnp.where(i <= j, wide[:, n : 2 * n] / root, 0.0)
    coupling_t = wide[:, 2 * n :].T
    coup_ref[...] = coupling_t
    wz = jnp.concatenate([w_new, nn(coupling_t, w_new, precision=HIGHEST)], axis=0)
    for load in loads:
        load.wait()
    apply_factors(wz, root, panel_buf, trail_buf, basis, updated, words, basis_buf, updated_buf, out_sems)


def factor(core, own, other, panel, trailing, rows_all):
    n, rows = panel.shape
    t = trailing.shape[0]
    steps = rows // OUT_CHUNK
    vmem, hbm = pl.BlockSpec(memory_space=pltpu.VMEM), pl.BlockSpec(memory_space=pltpu.HBM)
    return pl.pallas_call(
        lambda *refs: factor_kernel(rows_all, *refs),
        in_specs=[pl.BlockSpec(memory_space=pltpu.SMEM), vmem, vmem, hbm, hbm],
        out_specs=[hbm, hbm, vmem, vmem],
        out_shape=[
            jax.ShapeDtypeStruct((n, rows), F32),
            jax.ShapeDtypeStruct((t, rows), F32),
            jax.ShapeDtypeStruct((n, n), F32),
            jax.ShapeDtypeStruct((t, n), F32),
        ],
        scratch_shapes=[
            pltpu.VMEM((n, 3 * n), BF16),
            pltpu.VMEM((6 * n, n), BF16),
            pltpu.VMEM((n, 4 * n), BF16),
            pltpu.VMEM((n, n), F32),
            pltpu.VMEM((n, rows), F32),
            pltpu.VMEM((t, rows), F32),
            pltpu.SemaphoreType.DMA((2,)),
            pltpu.VMEM((n + t, 6 * n), BF16),
            pltpu.VMEM((steps, n, OUT_CHUNK), F32),
            pltpu.VMEM((steps, t, OUT_CHUNK), F32),
            pltpu.SemaphoreType.DMA((2, steps)),
        ],
        compiler_params=pltpu.CompilerParams(vmem_limit_bytes=48 << 20),
        name="factor",
    )(core, own, other, panel, trailing)


def shards(panel, trailing):
    n, t = panel.shape[0], trailing.shape[0]
    rows_all = panel.shape[1] * lax.axis_size(AXES)
    core = jnp.reshape(lax.axis_index("gy") % 2, (1,)).astype(jnp.int32)
    words = n // 4 + 8
    panel, trailing = (pltpu.with_memory_space_constraint(a, pltpu.HBM) for a in (panel, trailing))
    keep, send = local_gram(core, panel, trailing)
    total = add_packed(words, keep, exchange(send, 4))
    for masks in ((1, 3, 2), (8, 72, 64), (16, 48, 32)):
        near, wrap, far = (exchange(total, m) for m in masks)
        total = add_packed(words, total, wrap, near, far)
    other = exchange(total, 4)
    basis_t, updated, upper, coupling_t = factor(core, total, other, panel, trailing, rows_all)
    return basis_t, upper, coupling_t.T, updated


def solution(mesh):
    placed = (P(None, AXES), P(None, AXES))
    return jax.shard_map(
        shards,
        mesh=mesh,
        in_specs=placed,
        out_specs=(P(None, AXES), P(), P(), P(None, AXES)),
        check_vma=False,
    )
```

```python
import jax
import jax.numpy as jnp
from jax import lax
from jax.experimental import pallas as pl
from jax.experimental.pallas import tpu as pltpu
from jax.sharding import PartitionSpec as P

AXES = ("gx", "gy", "gz")
HIGHEST = lax.Precision.HIGHEST
F32 = jnp.float32
BF16 = jnp.bfloat16
CHUNKS = 4
OUT_CHUNK = 512
NEAR = 4
SMALL = 2e-2
MAGIC = 1.5 * 2.0**23


def round_int(x):
    return (x + MAGIC) - MAGIC


def two_sum(a, b):
    total = a + b
    part = total - a
    return total, (a - (total - part)) + (b - part)


def snap(x):
    c = x * (2.0**23 + 1.0)
    return c - (c - x)


def power_near(x):
    p = snap(jnp.maximum(x, 1e-30))
    return p, snap(1.0 / p)


def slices(hi, lo, count):
    digits = []
    for k in range(count):
        d = round_int(hi)
        digits.append(d)
        if k < count - 1:
            hi = (hi - d) * 256.0
            if lo is not None:
                lo = lo * 256.0
                new = hi + lo
                lo = lo - (new - hi)
                hi = new
    return digits


def nt(a, b, **kw):
    return lax.dot_general(a, b, (((1,), (1,)), ((), ())), preferred_element_type=F32, **kw)


def nn(a, b, **kw):
    return lax.dot_general(a, b, (((1,), (0,)), ((), ())), preferred_element_type=F32, **kw)


def iota(shape, axis):
    return lax.broadcasted_iota(jnp.int32, shape, axis)


def gram_kernel(core_ref, panel, trail, keep_ref, send_ref, pbuf, tbuf, ops, sems):
    n, rows = panel.shape
    t = trail.shape[0]
    width = rows // CHUNKS
    copies = []
    for k in range(CHUNKS):
        at = pl.ds(k * width, width)
        pair = (
            pltpu.make_async_copy(panel.at[:, at], pbuf.at[k], sems.at[0, k]),
            pltpu.make_async_copy(trail.at[:, at], tbuf.at[k], sems.at[1, k]),
        )
        for copy in pair:
            copy.start()
        copies.append(pair)

    top = jnp.zeros((n, 128), F32)
    for k in range(CHUNKS):
        copies[k][0].wait()
        x = jnp.abs(pbuf[k])
        for q in range(0, width, 128):
            top = jnp.maximum(top, x[:, q : q + 128])
    for k in range(CHUNKS):
        copies[k][1].wait()
    p, inv = power_near(jnp.max(top, axis=1, keepdims=True))

    def split(k):
        a = pbuf[k] * (inv * 32.0)
        d1 = round_int(a)
        r1 = (a - d1) * 256.0
        d2 = round_int(r1)
        d3 = (r1 - d2) * 256.0
        c = tbuf[k]
        c1 = c.astype(BF16)
        rc = c - c1.astype(F32)
        c2 = rc.astype(BF16)
        c3 = rc - c2.astype(F32)
        at = 0
        for part in (c3, d1, d2, d3, c1, c2):
            ops[k, at : at + part.shape[0], :] = part.astype(BF16)
            at += part.shape[0]

    left, right = None, None
    split(0)
    for k in range(CHUNKS):
        if k + 1 < CHUNKS:
            split(k + 1)
        l = nt(ops[k, 0 : t + 2 * n, :], ops[k, t : t + 2 * n, :])
        r = nt(ops[k, t : t + 3 * n, :], ops[k, t + 2 * n :, :])
        left, right = (l, r) if left is None else (left + l, right + r)

    c3d1, left = left[:t, :n], left[t:, :]
    row = jnp.broadcast_to(p * (1.0 / 32.0), (n, n))
    col = row.T
    scale = row * col
    h, e = two_sum(left[:n, :n], (left[:n, n:] + left[n:, :n]) * 2.0**-8)
    e = e + (left[n:, n:] * 2.0**-16 + right[2 * n :, :n] * 2.0**-32)
    mix = right[:n, :n] * 2.0**-16 + right[n : 2 * n, :n] * 2.0**-24
    ac = right[2 * n :, n : n + t] * 2.0**-16 + right[n : 2 * n, n + t :] * 2.0**-8
    ac = ac + (right[n : 2 * n, n : n + t] * 2.0**-8 + right[:n, n + t :])
    ca = (c3d1 + (ac + right[:n, n : n + t]).T) * col[:t, :]

    core = core_ref[0]
    half = n // 2
    i, j = iota((half, n), 0), iota((half, n), 1)

    def fold(g):
        top, bottom = g[:half, :], g[half:, :]
        body = jnp.where((j >= half) & (i >= j - half), pltpu.roll(top, half, 1), bottom)
        diag = jnp.sum(jnp.where(i == j - half, bottom, 0.0), axis=0, keepdims=True)
        return body, jnp.broadcast_to(diag, (8, n))

    hi, lo = two_sum(h * scale, (e + (mix + mix.T)) * scale)
    hi_body, hi_diag = fold(hi)
    lo_body, lo_diag = fold(lo)
    q = half // 2
    tq = t // 2

    def put(ref, first):
        def pick(v, size):
            return jnp.where(first, v[:size, :], v[size:, :])

        ref[0:q, :] = pick(hi_body, q)
        ref[q : q + 8, :] = hi_diag
        ref[q + 8 : 2 * q + 8, :] = pick(lo_body, q)
        ref[2 * q + 8 : 2 * q + 16, :] = lo_diag
        ref[2 * q + 16 :, :] = pick(ca, tq)

    put(keep_ref, core == 0)
    put(send_ref, core == 1)


def local_gram(core, panel, trailing):
    n, rows = panel.shape
    t = trailing.shape[0]
    width = rows // CHUNKS
    out = jax.ShapeDtypeStruct((n // 2 + 16 + t // 2, n), F32)
    vmem, hbm = pl.BlockSpec(memory_space=pltpu.VMEM), pl.BlockSpec(memory_space=pltpu.HBM)
    return pl.pallas_call(
        gram_kernel,
        in_specs=[pl.BlockSpec(memory_space=pltpu.SMEM), hbm, hbm],
        out_specs=[vmem, vmem],
        out_shape=[out, out],
        scratch_shapes=[
            pltpu.VMEM((CHUNKS, n, width), F32),
            pltpu.VMEM((CHUNKS, t, width), F32),
            pltpu.VMEM((CHUNKS, 3 * (n + t), width), BF16),
            pltpu.SemaphoreType.DMA((2, CHUNKS)),
        ],
        compiler_params=pltpu.CompilerParams(vmem_limit_bytes=32 << 20),
        name="gram",
    )(core, panel, trailing)


def add_packed(words, *arrays):
    parts, errors = list(arrays), []
    while len(parts) > 1:
        pairs = []
        for a, b in zip(parts[::2], parts[1::2]):
            errors.append(two_sum(a[:words], b[:words])[1])
            pairs.append(a + b)
        parts = pairs
    error = errors[0] if len(errors) == 1 else (errors[0] + errors[1]) + errors[2]
    rest = parts[0].shape[0] - 2 * words
    return parts[0] + jnp.pad(error, ((words, rest), (0, 0)))


def exchange(value, mask):
    size = lax.axis_size(AXES)
    return lax.ppermute(value, AXES, [(s, s ^ mask) for s in range(size)])


def split3(x):
    x1 = x.astype(BF16)
    rest = x - x1.astype(F32)
    x2 = rest.astype(BF16)
    return x1, x2, (rest - x2.astype(F32)).astype(BF16)


def chol_inv(s):
    blocks = len(s)
    n = 8 * blocks
    rid, lid = iota((8, n), 0), iota((8, n), 1)
    s, w = list(s), [jnp.where(lid == rid + 8 * r, 1.0, 0.0) for r in range(blocks)]

    def spread(r, first):
        return [jnp.broadcast_to(s[r][:, first + k : first + k + 1], (8, n)) for k in range(8)]

    cols = {r: spread(r, 0) for r in (0, 1)}
    for r0 in range(blocks):
        first = 8 * r0
        near = range(r0, min(r0 + 3, blocks))
        for r in near:
            if r not in cols:
                cols[r] = spread(r, first)
        ahead = {r: spread(r, first + 8) for r in near if r > r0}
        edges, invs, srows, wrows, scales = {}, [], [], [], []
        inv_rows = jnp.zeros((8, n), F32)
        for k in range(8):
            pivot = cols[r0][k][k : k + 1, :]
            inv = 1.0 / pivot
            mult = {r: cols[r][k] * inv for r in near}
            mult[r0] = jnp.where(rid > k, mult[r0], 0.0)
            for later in range(k + 1, 8):
                edges[k, later] = edge = cols[r0][later][k : k + 1, :]
                for r in near:
                    cols[r][later] = cols[r][later] - mult[r] * edge
            if ahead:
                for q in range(8):
                    edge = cols[r0 + 1][k][q : q + 1, :]
                    for r in ahead:
                        ahead[r][q] = ahead[r][q] - mult[r] * edge
            srow, wrow = s[r0][k : k + 1, :], w[r0][k : k + 1, :]
            for r in near:
                s[r] = s[r] - mult[r] * srow
                w[r] = w[r] - mult[r] * wrow
            inv_rows = jnp.where(rid == k, inv, inv_rows)
            invs.append(inv)
            srows.append(srow)
            wrows.append(wrow)
            scales.append(lax.rsqrt(pivot))
        for r in range(r0 + 3, min(r0 + NEAR, blocks)):
            col = spread(r, first)
            for k in range(8):
                mult = col[k] * invs[k]
                for later in range(k + 1, 8):
                    col[later] = col[later] - mult * edges[k, later]
                s[r] = s[r] - mult * srows[k]
                w[r] = w[r] - mult * wrows[k]
        if r0 + NEAR < blocks:
            l1, l2, l3 = split3(s[r0] * inv_rows)
            r1, r2, r3 = split3(jnp.concatenate([s[r0], w[r0]], axis=1))

            def stack(*parts):
                return jnp.concatenate([p.astype(F32) for p in parts], axis=0).astype(BF16)

            left, right = stack(l1, l2, l1, l2, l1, l3), stack(r1, r2, r2, r1, r3, r1)
            update = lax.dot_general(left, right, (((0,), (0,)), ((), ())), preferred_element_type=F32)
            for r in range(r0 + NEAR, blocks):
                s[r] = s[r] - update[8 * r : 8 * r + 8, :n]
                w[r] = w[r] - update[8 * r : 8 * r + 8, n:]
        for k, d in enumerate(scales):
            w[r0] = jnp.where(rid == k, w[r0] * d, w[r0])
        cols = ahead
    return w


def apply_factors(wz, scale, panel, trailing, basis, updated, words, basis_buf, updated_buf, sems):
    n, rows = panel.shape
    w1, w2, w3 = split3(wz)
    for k, w in enumerate((w1, w2, w1, w2, w1, w3)):
        words[:, k * n : (k + 1) * n] = w
    copies = []
    for k in range(rows // OUT_CHUNK):
        at = pl.ds(k * OUT_CHUNK, OUT_CHUNK)
        a1, a2, a3 = split3(panel[:, at])
        out = nn(words[...], jnp.concatenate([a1, a2, a2, a1, a3, a1], axis=0))
        basis_buf[k] = out[:n, :] * scale
        updated_buf[k] = trailing[:, at] - out[n:, :]
        for copy in (
            pltpu.make_async_copy(basis_buf.at[k], basis.at[:, at], sems.at[0, k]),
            pltpu.make_async_copy(updated_buf.at[k], updated.at[:, at], sems.at[1, k]),
        ):
            copy.start()
            copies.append(copy)
    for copy in copies:
        copy.wait()


def factor_kernel(
    rows_all, core_ref, own_ref, other_ref, panel, trailing, basis, updated, upper_ref, coup_ref,
    wcat, gcat, tcat, v_ref, panel_buf, trail_buf, in_sems, words, basis_buf, updated_buf, out_sems,
):
    loads = (
        pltpu.make_async_copy(panel, panel_buf, in_sems.at[0]),
        pltpu.make_async_copy(trailing, trail_buf, in_sems.at[1]),
    )
    for load in loads:
        load.start()
    n = upper_ref.shape[0]
    t = coup_ref.shape[0]
    half, q, tq = n // 2, n // 4, t // 2
    first = core_ref[0] == 0
    own, other = own_ref[...], other_ref[...]
    a, b = jnp.where(first, own, other), jnp.where(first, other, own)
    i, j = iota((n, n), 0), iota((n, n), 1)
    hi_, hj_ = iota((half, n), 0), iota((half, n), 1)

    def unfold(packed, diag_row):
        diag = jnp.broadcast_to(diag_row, (half, n))
        top = jnp.where((hj_ < half) & (hi_ >= hj_), pltpu.roll(packed, half, 1), 0.0)
        keep = jnp.where((hj_ < half) | (hi_ < hj_ - half), packed, 0.0)
        bottom = jnp.where(hi_ == hj_ - half, diag, keep)
        part = jnp.concatenate([top, bottom], axis=0)
        return jnp.where(i == j, part, part + part.T)

    def packed(start):
        return jnp.concatenate([a[start : start + q, :], b[start : start + q, :]], axis=0), a[start + q : start + q + 1, :]

    hi_body, hi_diag = packed(0)
    lo_body, lo_diag = packed(q + 8)
    ca = jnp.concatenate([a[2 * q + 16 :, :], b[2 * q + 16 :, :]], axis=0)
    hi_body, lo_body = two_sum(hi_body, lo_body)
    hi_diag, lo_diag = two_sum(hi_diag, lo_diag)
    g_hi, g_lo = unfold(hi_body, hi_diag), unfold(lo_body, lo_diag)
    w = jnp.concatenate(chol_inv([g_hi[8 * r : 8 * r + 8, :] for r in range(n // 8)]), axis=0)

    diag = jnp.sum(jnp.where(i == j, g_hi, 0.0), axis=0, keepdims=True)
    pc, inv_pc = power_near(jnp.sqrt(diag))
    ic = jnp.broadcast_to(inv_pc, (n, n))
    eq = ic * ic.T
    s_hi, s_lo = g_hi * eq, g_lo * eq
    w = w * jnp.broadcast_to(pc, (n, n))

    qr, inv_qr = power_near(jnp.max(jnp.abs(w), axis=1, keepdims=True))
    wd = slices(w * (inv_qr * 64.0), None, 3)
    qs = qr * (1.0 / 64.0)
    wt = (wd[0] + wd[1] * 2.0**-8 + wd[2] * 2.0**-16) * qs
    for k in range(3):
        wcat[:, k * n : (k + 1) * n] = wd[k].astype(BF16)
    gd = slices(s_hi * 32.0, s_lo * 32.0, 6)
    for k in range(6):
        gcat[(5 - k) * n : (6 - k) * n, :] = gd[k].astype(BF16)

    def weigh(parts):
        hi, lo = parts[0], None
        for k, part in enumerate(parts[1:]):
            hi, err = two_sum(hi, part * 2.0 ** (-8 * (k + 1)))
            lo = err if lo is None else lo + err
        return two_sum(hi, lo)

    def t_level(k):
        width = min(k + 1, 3) * n
        return nn(wcat[:, 0:width], gcat[(5 - k) * n : (5 - k) * n + width, :])

    t_hi, t_lo = weigh([t_level(k) for k in range(6)])
    tau, inv_tau = power_near(jnp.max(jnp.abs(t_hi), axis=1, keepdims=True))
    td = slices(t_hi * (inv_tau * 64.0), t_lo * (inv_tau * 64.0), 4)
    for k in range(4):
        tcat[:, (3 - k) * n : (4 - k) * n] = td[k].astype(BF16)

    def m_level(k):
        width = min(k + 1, 3) * n
        return nt(tcat[:, (3 - k) * n : (3 - k) * n + width], wcat[:, 0:width])

    m_hi, m_lo = weigh([m_level(k) for k in range(4)])
    qb = jnp.broadcast_to(qs, (n, n))
    scale = qb.T * (qb * (tau * (1.0 / 2048.0)))
    e = (m_hi * scale - jnp.where(i == j, 1.0, 0.0)) + m_lo * scale

    def phi(x):
        return jnp.where(i > j, x, jnp.where(i == j, 0.5 * x, 0.0))

    f = phi(e)
    size = jnp.sum(f * f)

    @pl.when(size <= SMALL * SMALL)
    def _():
        fb = f.astype(BF16)
        f2, square = -phi(nt(fb, fb)), nn(fb, fb)
        f2b = f2.astype(BF16)
        ab = jnp.concatenate([fb, f2b], axis=1)
        ba = jnp.concatenate([f2b, fb], axis=1)
        third = phi(nt(ab, ba)) + nn(ab, jnp.concatenate([(f2 - square).astype(BF16), fb], axis=0))
        v_ref[...] = (jnp.where(i == j, 1.0, 0.0) - f) + ((square - f2) + third)

    @pl.when(jnp.logical_not(size <= SMALL * SMALL))
    def _():
        lower = jnp.where(i >= j, e, 0.0)
        full = jnp.where(i == j, e + 1.0, lower + lower.T)
        blocks = chol_inv([full[8 * r : 8 * r + 8, :] for r in range(n // 8)])
        for r in range(n // 8):
            v_ref[8 * r : 8 * r + 8, :] = blocks[r]

    v = v_ref[...]
    y = nt(wt, ca * inv_pc, precision=HIGHEST)
    t_true = t_hi * (qs * (1.0 / 32.0)) * jnp.broadcast_to(pc, (n, n))
    wide = nn(v, jnp.concatenate([wt, t_true, y], axis=1), precision=HIGHEST)
    w_new = wide[:, :n] * ic
    root = jnp.sqrt(jnp.float32(rows_all))
    upper_ref[...] = jnp.where(i <= j, wide[:, n : 2 * n] * (1.0 / root), 0.0)
    coupling_t = wide[:, 2 * n :].T
    coup_ref[...] = coupling_t
    wz = jnp.concatenate([w_new, nn(coupling_t, w_new, precision=HIGHEST)], axis=0)
    for load in loads:
        load.wait()
    apply_factors(wz, root, panel_buf, trail_buf, basis, updated, words, basis_buf, updated_buf, out_sems)


def factor(core, own, other, panel, trailing, rows_all):
    n, rows = panel.shape
    t = trailing.shape[0]
    steps = rows // OUT_CHUNK
    vmem, hbm = pl.BlockSpec(memory_space=pltpu.VMEM), pl.BlockSpec(memory_space=pltpu.HBM)
    return pl.pallas_call(
        lambda *refs: factor_kernel(rows_all, *refs),
        in_specs=[pl.BlockSpec(memory_space=pltpu.SMEM), vmem, vmem, hbm, hbm],
        out_specs=[hbm, hbm, vmem, vmem],
        out_shape=[
            jax.ShapeDtypeStruct((n, rows), F32),
            jax.ShapeDtypeStruct((t, rows), F32),
            jax.ShapeDtypeStruct((n, n), F32),
            jax.ShapeDtypeStruct((t, n), F32),
        ],
        scratch_shapes=[
            pltpu.VMEM((n, 3 * n), BF16),
            pltpu.VMEM((6 * n, n), BF16),
            pltpu.VMEM((n, 4 * n), BF16),
            pltpu.VMEM((n, n), F32),
            pltpu.VMEM((n, rows), F32),
            pltpu.VMEM((t, rows), F32),
            pltpu.SemaphoreType.DMA((2,)),
            pltpu.VMEM((n + t, 6 * n), BF16),
            pltpu.VMEM((steps, n, OUT_CHUNK), F32),
            pltpu.VMEM((steps, t, OUT_CHUNK), F32),
            pltpu.SemaphoreType.DMA((2, steps)),
        ],
        compiler_params=pltpu.CompilerParams(vmem_limit_bytes=48 << 20),
        name="factor",
    )(core, own, other, panel, trailing)


def shards(panel, trailing):
    n, t = panel.shape[0], trailing.shape[0]
    rows_all = panel.shape[1] * lax.axis_size(AXES)
    core = jnp.reshape(lax.axis_index("gy") % 2, (1,)).astype(jnp.int32)
    words = n // 4 + 8
    panel, trailing = (pltpu.with_memory_space_constraint(a, pltpu.HBM) for a in (panel, trailing))
    keep, send = local_gram(core, panel, trailing)
    total = add_packed(words, keep, exchange(send, 4))
    for masks in ((1, 3, 2), (8, 72, 64), (16, 48, 32)):
        near, wrap, far = (exchange(total, m) for m in masks)
        total = add_packed(words, total, wrap, near, far)
    other = exchange(total, 4)
    basis_t, updated, upper, coupling_t = factor(core, total, other, panel, trailing, rows_all)
    return basis_t, upper, coupling_t.T, updated


def solution(mesh):
    placed = (P(None, AXES), P(None, AXES))
    return jax.shard_map(
        shards,
        mesh=mesh,
        in_specs=placed,
        out_specs=(P(None, AXES), P(), P(), P(None, AXES)),
        check_vma=False,
    )
```

```python
import jax
import jax.numpy as jnp
from jax import lax
from jax.experimental import pallas as pl
from jax.experimental.pallas import tpu as pltpu
from jax.sharding import PartitionSpec as P

AXES = ("gx", "gy", "gz")
HIGHEST = lax.Precision.HIGHEST
F32 = jnp.float32
BF16 = jnp.bfloat16
CHUNKS = 4
OUT_CHUNK = 512
NEAR = 4
SMALL = 2e-2
MAGIC = 1.5 * 2.0**23


def round_int(x):
    return (x + MAGIC) - MAGIC


def two_sum(a, b):
    total = a + b
    part = total - a
    return total, (a - (total - part)) + (b - part)


def snap(x):
    c = x * (2.0**23 + 1.0)
    return c - (c - x)


def power_near(x):
    p = snap(jnp.maximum(x, 1e-30))
    return p, snap(1.0 / p)


def slices(hi, lo, count):
    digits = []
    for k in range(count):
        d = round_int(hi)
        digits.append(d)
        if k < count - 1:
            hi = (hi - d) * 256.0
            if lo is not None:
                lo = lo * 256.0
                new = hi + lo
                lo = lo - (new - hi)
                hi = new
    return digits


def nt(a, b, **kw):
    return lax.dot_general(a, b, (((1,), (1,)), ((), ())), preferred_element_type=F32, **kw)


def nn(a, b, **kw):
    return lax.dot_general(a, b, (((1,), (0,)), ((), ())), preferred_element_type=F32, **kw)


def iota(shape, axis):
    return lax.broadcasted_iota(jnp.int32, shape, axis)


def gram_kernel(core_ref, panel, trail, keep_ref, send_ref, pbuf, tbuf, ops, sems):
    n, rows = panel.shape
    t = trail.shape[0]
    width = rows // CHUNKS
    copies = []
    for k in range(CHUNKS):
        at = pl.ds(k * width, width)
        pair = (
            pltpu.make_async_copy(panel.at[:, at], pbuf.at[k], sems.at[0, k]),
            pltpu.make_async_copy(trail.at[:, at], tbuf.at[k], sems.at[1, k]),
        )
        for copy in pair:
            copy.start()
        copies.append(pair)

    top = jnp.zeros((n, 128), F32)
    for k in range(CHUNKS):
        copies[k][0].wait()
        x = jnp.abs(pbuf[k])
        for q in range(0, width, 128):
            top = jnp.maximum(top, x[:, q : q + 128])
    for k in range(CHUNKS):
        copies[k][1].wait()
    p, inv = power_near(jnp.max(top, axis=1, keepdims=True))

    def split(k):
        a = pbuf[k] * (inv * 32.0)
        d1 = round_int(a)
        r1 = (a - d1) * 256.0
        d2 = round_int(r1)
        d3 = (r1 - d2) * 256.0
        c = tbuf[k]
        c1 = c.astype(BF16)
        rc = c - c1.astype(F32)
        c2 = rc.astype(BF16)
        c3 = rc - c2.astype(F32)
        at = 0
        for part in (c3, d1, d2, d3, c1, c2):
            ops[k, at : at + part.shape[0], :] = part.astype(BF16)
            at += part.shape[0]

    left, right = None, None
    split(0)
    for k in range(CHUNKS):
        if k + 1 < CHUNKS:
            split(k + 1)
        l = nt(ops[k, 0 : t + 2 * n, :], ops[k, t : t + 2 * n, :])
        r = nt(ops[k, t : t + 3 * n, :], ops[k, t + 2 * n :, :])
        left, right = (l, r) if left is None else (left + l, right + r)

    c3d1, left = left[:t, :n], left[t:, :]
    row = jnp.broadcast_to(p * (1.0 / 32.0), (n, n))
    col = row.T
    scale = row * col
    h, e = two_sum(left[:n, :n], (left[:n, n:] + left[n:, :n]) * 2.0**-8)
    e = e + (left[n:, n:] * 2.0**-16 + right[2 * n :, :n] * 2.0**-32)
    mix = right[:n, :n] * 2.0**-16 + right[n : 2 * n, :n] * 2.0**-24
    ac = right[2 * n :, n : n + t] * 2.0**-16 + right[n : 2 * n, n + t :] * 2.0**-8
    ac = ac + (right[n : 2 * n, n : n + t] * 2.0**-8 + right[:n, n + t :])
    ca = (c3d1 + (ac + right[:n, n : n + t]).T) * col[:t, :]

    core = core_ref[0]
    half = n // 2
    i, j = iota((half, n), 0), iota((half, n), 1)

    def fold(g):
        top, bottom = g[:half, :], g[half:, :]
        body = jnp.where((j >= half) & (i >= j - half), pltpu.roll(top, half, 1), bottom)
        diag = jnp.sum(jnp.where(i == j - half, bottom, 0.0), axis=0, keepdims=True)
        return body, jnp.broadcast_to(diag, (8, n))

    hi, lo = two_sum(h * scale, (e + (mix + mix.T)) * scale)
    hi_body, hi_diag = fold(hi)
    lo_body, lo_diag = fold(lo)
    q = half // 2
    tq = t // 2

    def put(ref, first):
        def pick(v, size):
            return jnp.where(first, v[:size, :], v[size:, :])

        ref[0:q, :] = pick(hi_body, q)
        ref[q : q + 8, :] = hi_diag
        ref[q + 8 : 2 * q + 8, :] = pick(lo_body, q)
        ref[2 * q + 8 : 2 * q + 16, :] = lo_diag
        ref[2 * q + 16 :, :] = pick(ca, tq)

    put(keep_ref, core == 0)
    put(send_ref, core == 1)


def local_gram(core, panel, trailing):
    n, rows = panel.shape
    t = trailing.shape[0]
    width = rows // CHUNKS
    out = jax.ShapeDtypeStruct((n // 2 + 16 + t // 2, n), F32)
    vmem, hbm = pl.BlockSpec(memory_space=pltpu.VMEM), pl.BlockSpec(memory_space=pltpu.HBM)
    return pl.pallas_call(
        gram_kernel,
        in_specs=[pl.BlockSpec(memory_space=pltpu.SMEM), hbm, hbm],
        out_specs=[vmem, vmem],
        out_shape=[out, out],
        scratch_shapes=[
            pltpu.VMEM((CHUNKS, n, width), F32),
            pltpu.VMEM((CHUNKS, t, width), F32),
            pltpu.VMEM((CHUNKS, 3 * (n + t), width), BF16),
            pltpu.SemaphoreType.DMA((2, CHUNKS)),
        ],
        compiler_params=pltpu.CompilerParams(vmem_limit_bytes=32 << 20),
        name="gram",
    )(core, panel, trailing)


def add_packed(words, *arrays):
    parts, errors = list(arrays), []
    while len(parts) > 1:
        pairs = []
        for a, b in zip(parts[::2], parts[1::2]):
            errors.append(two_sum(a[:words], b[:words])[1])
            pairs.append(a + b)
        parts = pairs
    error = errors[0] if len(errors) == 1 else (errors[0] + errors[1]) + errors[2]
    rest = parts[0].shape[0] - 2 * words
    return parts[0] + jnp.pad(error, ((words, rest), (0, 0)))


def exchange(value, mask):
    size = lax.axis_size(AXES)
    return lax.ppermute(value, AXES, [(s, s ^ mask) for s in range(size)])


def split3(x):
    x1 = x.astype(BF16)
    rest = x - x1.astype(F32)
    x2 = rest.astype(BF16)
    return x1, x2, (rest - x2.astype(F32)).astype(BF16)


def chol_inv(s):
    blocks = len(s)
    n = 8 * blocks
    rid, lid = iota((8, n), 0), iota((8, n), 1)
    s, w = list(s), [jnp.where(lid == rid + 8 * r, 1.0, 0.0) for r in range(blocks)]

    def spread(r, first):
        return [jnp.broadcast_to(s[r][:, first + k : first + k + 1], (8, n)) for k in range(8)]

    cols = {r: spread(r, 0) for r in (0, 1)}
    for r0 in range(blocks):
        first = 8 * r0
        near = range(r0, min(r0 + 3, blocks))
        for r in near:
            if r not in cols:
                cols[r] = spread(r, first)
        ahead = {r: spread(r, first + 8) for r in near if r > r0}
        edges, invs, srows, wrows, scales = {}, [], [], [], []
        inv_rows = jnp.zeros((8, n), F32)
        for k in range(8):
            pivot = cols[r0][k][k : k + 1, :]
            inv = 1.0 / pivot
            mult = {r: cols[r][k] * inv for r in near}
            mult[r0] = jnp.where(rid > k, mult[r0], 0.0)
            for later in range(k + 1, 8):
                edges[k, later] = edge = cols[r0][later][k : k + 1, :]
                for r in near:
                    cols[r][later] = cols[r][later] - mult[r] * edge
            if ahead:
                for q in range(8):
                    edge = cols[r0 + 1][k][q : q + 1, :]
                    for r in ahead:
                        ahead[r][q] = ahead[r][q] - mult[r] * edge
            srow, wrow = s[r0][k : k + 1, :], w[r0][k : k + 1, :]
            for r in near:
                s[r] = s[r] - mult[r] * srow
                w[r] = w[r] - mult[r] * wrow
            inv_rows = jnp.where(rid == k, inv, inv_rows)
            invs.append(inv)
            srows.append(srow)
            wrows.append(wrow)
            scales.append(lax.rsqrt(pivot))
        for r in range(r0 + 3, min(r0 + NEAR, blocks)):
            col = spread(r, first)
            for k in range(8):
                mult = col[k] * invs[k]
                for later in range(k + 1, 8):
                    col[later] = col[later] - mult * edges[k, later]
                s[r] = s[r] - mult * srows[k]
                w[r] = w[r] - mult * wrows[k]
        if r0 + NEAR < blocks:
            l1, l2, l3 = split3(s[r0] * inv_rows)
            r1, r2, r3 = split3(jnp.concatenate([s[r0], w[r0]], axis=1))

            def stack(*parts):
                return jnp.concatenate([p.astype(F32) for p in parts], axis=0).astype(BF16)

            left, right = stack(l1, l2, l1, l2, l1, l3), stack(r1, r2, r2, r1, r3, r1)
            update = lax.dot_general(left, right, (((0,), (0,)), ((), ())), preferred_element_type=F32)
            for r in range(r0 + NEAR, blocks):
                s[r] = s[r] - update[8 * r : 8 * r + 8, :n]
                w[r] = w[r] - update[8 * r : 8 * r + 8, n:]
        for k, d in enumerate(scales):
            w[r0] = jnp.where(rid == k, w[r0] * d, w[r0])
        cols = ahead
    return w


def apply_factors(wz, scale, panel, trailing, basis, updated, words, basis_buf, updated_buf, sems):
    n, rows = panel.shape
    w1, w2, w3 = split3(wz)
    for k, w in enumerate((w1, w2, w1, w2, w1, w3)):
        words[:, k * n : (k + 1) * n] = w
    copies = []
    for k in range(rows // OUT_CHUNK):
        at = pl.ds(k * OUT_CHUNK, OUT_CHUNK)
        a1, a2, a3 = split3(panel[:, at])
        out = nn(words[...], jnp.concatenate([a1, a2, a2, a1, a3, a1], axis=0))
        basis_buf[k] = out[:n, :] * scale
        updated_buf[k] = trailing[:, at] - out[n:, :]
        for copy in (
            pltpu.make_async_copy(basis_buf.at[k], basis.at[:, at], sems.at[0, k]),
            pltpu.make_async_copy(updated_buf.at[k], updated.at[:, at], sems.at[1, k]),
        ):
            copy.start()
            copies.append(copy)
    for copy in copies:
        copy.wait()


def factor_kernel(
    rows_all, core_ref, own_ref, other_ref, panel, trailing, basis, updated, upper, coup,
    upper_ref, coup_ref, small_sems, wcat, gcat, tcat, v_ref, panel_buf, trail_buf, in_sems, words, basis_buf, updated_buf, out_sems,
):
    loads = (
        pltpu.make_async_copy(panel, panel_buf, in_sems.at[0]),
        pltpu.make_async_copy(trailing, trail_buf, in_sems.at[1]),
    )
    for load in loads:
        load.start()
    n = upper_ref.shape[0]
    t = coup_ref.shape[0]
    half, q, tq = n // 2, n // 4, t // 2
    first = core_ref[0] == 0
    own, other = own_ref[...], other_ref[...]
    a, b = jnp.where(first, own, other), jnp.where(first, other, own)
    i, j = iota((n, n), 0), iota((n, n), 1)
    hi_, hj_ = iota((half, n), 0), iota((half, n), 1)

    def unfold(packed, diag_row):
        diag = jnp.broadcast_to(diag_row, (half, n))
        top = jnp.where((hj_ < half) & (hi_ >= hj_), pltpu.roll(packed, half, 1), 0.0)
        keep = jnp.where((hj_ < half) | (hi_ < hj_ - half), packed, 0.0)
        bottom = jnp.where(hi_ == hj_ - half, diag, keep)
        part = jnp.concatenate([top, bottom], axis=0)
        return jnp.where(i == j, part, part + part.T)

    def packed(start):
        return jnp.concatenate([a[start : start + q, :], b[start : start + q, :]], axis=0), a[start + q : start + q + 1, :]

    hi_body, hi_diag = packed(0)
    lo_body, lo_diag = packed(q + 8)
    ca = jnp.concatenate([a[2 * q + 16 :, :], b[2 * q + 16 :, :]], axis=0)
    hi_body, lo_body = two_sum(hi_body, lo_body)
    hi_diag, lo_diag = two_sum(hi_diag, lo_diag)
    g_hi, g_lo = unfold(hi_body, hi_diag), unfold(lo_body, lo_diag)
    w = jnp.concatenate(chol_inv([g_hi[8 * r : 8 * r + 8, :] for r in range(n // 8)]), axis=0)

    diag = jnp.sum(jnp.where(i == j, g_hi, 0.0), axis=0, keepdims=True)
    pc, inv_pc = power_near(jnp.sqrt(diag))
    ic = jnp.broadcast_to(inv_pc, (n, n))
    eq = ic * ic.T
    s_hi, s_lo = g_hi * eq, g_lo * eq
    w = w * jnp.broadcast_to(pc, (n, n))

    qr, inv_qr = power_near(jnp.max(jnp.abs(w), axis=1, keepdims=True))
    wd = slices(w * (inv_qr * 64.0), None, 3)
    qs = qr * (1.0 / 64.0)
    wt = (wd[0] + wd[1] * 2.0**-8 + wd[2] * 2.0**-16) * qs
    for k in range(3):
        wcat[:, k * n : (k + 1) * n] = wd[k].astype(BF16)
    gd = slices(s_hi * 32.0, s_lo * 32.0, 6)
    for k in range(6):
        gcat[(5 - k) * n : (6 - k) * n, :] = gd[k].astype(BF16)

    def weigh(parts):
        hi, lo = parts[0], None
        for k, part in enumerate(parts[1:]):
            hi, err = two_sum(hi, part * 2.0 ** (-8 * (k + 1)))
            lo = err if lo is None else lo + err
        return two_sum(hi, lo)

    def t_level(k):
        width = min(k + 1, 3) * n
        return nn(wcat[:, 0:width], gcat[(5 - k) * n : (5 - k) * n + width, :])

    t_hi, t_lo = weigh([t_level(k) for k in range(6)])
    tau, inv_tau = power_near(jnp.max(jnp.abs(t_hi), axis=1, keepdims=True))
    td = slices(t_hi * (inv_tau * 64.0), t_lo * (inv_tau * 64.0), 4)
    for k in range(4):
        tcat[:, (3 - k) * n : (4 - k) * n] = td[k].astype(BF16)

    def m_level(k):
        width = min(k + 1, 3) * n
        return nt(tcat[:, (3 - k) * n : (3 - k) * n + width], wcat[:, 0:width])

    m_hi, m_lo = weigh([m_level(k) for k in range(4)])
    qb = jnp.broadcast_to(qs, (n, n))
    scale = qb.T * (qb * (tau * (1.0 / 2048.0)))
    e = (m_hi * scale - jnp.where(i == j, 1.0, 0.0)) + m_lo * scale

    def phi(x):
        return jnp.where(i > j, x, jnp.where(i == j, 0.5 * x, 0.0))

    f = phi(e)
    size = jnp.sum(f * f)

    @pl.when(size <= SMALL * SMALL)
    def _():
        fb = f.astype(BF16)
        f2, square = -phi(nt(fb, fb)), nn(fb, fb)
        f2b = f2.astype(BF16)
        ab = jnp.concatenate([fb, f2b], axis=1)
        ba = jnp.concatenate([f2b, fb], axis=1)
        third = phi(nt(ab, ba)) + nn(ab, jnp.concatenate([(f2 - square).astype(BF16), fb], axis=0))
        v_ref[...] = (jnp.where(i == j, 1.0, 0.0) - f) + ((square - f2) + third)

    @pl.when(jnp.logical_not(size <= SMALL * SMALL))
    def _():
        lower = jnp.where(i >= j, e, 0.0)
        full = jnp.where(i == j, e + 1.0, lower + lower.T)
        blocks = chol_inv([full[8 * r : 8 * r + 8, :] for r in range(n // 8)])
        for r in range(n // 8):
            v_ref[8 * r : 8 * r + 8, :] = blocks[r]

    v = v_ref[...]
    y = nt(wt, ca * inv_pc, precision=HIGHEST)
    t_true = t_hi * (qs * (1.0 / 32.0)) * jnp.broadcast_to(pc, (n, n))
    wide = nn(v, jnp.concatenate([wt, t_true, y], axis=1), precision=HIGHEST)
    w_new = wide[:, :n] * ic
    root = jnp.sqrt(jnp.float32(rows_all))
    upper_ref[...] = jnp.where(i <= j, wide[:, n : 2 * n] * (1.0 / root), 0.0)
    coupling_t = wide[:, 2 * n :].T
    coup_ref[...] = coupling_t
    stores = (
        pltpu.make_async_copy(upper_ref, upper, small_sems.at[0]),
        pltpu.make_async_copy(coup_ref, coup, small_sems.at[1]),
    )
    for store in stores:
        store.start()
    wz = jnp.concatenate([w_new, nn(coupling_t, w_new, precision=HIGHEST)], axis=0)
    for load in loads:
        load.wait()
    apply_factors(wz, root, panel_buf, trail_buf, basis, updated, words, basis_buf, updated_buf, out_sems)
    for store in stores:
        store.wait()


def factor(core, own, other, panel, trailing, rows_all):
    n, rows = panel.shape
    t = trailing.shape[0]
    steps = rows // OUT_CHUNK
    vmem, hbm = pl.BlockSpec(memory_space=pltpu.VMEM), pl.BlockSpec(memory_space=pltpu.HBM)
    return pl.pallas_call(
        lambda *refs: factor_kernel(rows_all, *refs),
        in_specs=[pl.BlockSpec(memory_space=pltpu.SMEM), vmem, vmem, hbm, hbm],
        out_specs=[hbm] * 4,
        out_shape=[
            jax.ShapeDtypeStruct((n, rows), F32),
            jax.ShapeDtypeStruct((t, rows), F32),
            jax.ShapeDtypeStruct((n, n), F32),
            jax.ShapeDtypeStruct((t, n), F32),
        ],
        scratch_shapes=[
            pltpu.VMEM((n, n), F32),
            pltpu.VMEM((t, n), F32),
            pltpu.SemaphoreType.DMA((2,)),
            pltpu.VMEM((n, 3 * n), BF16),
            pltpu.VMEM((6 * n, n), BF16),
            pltpu.VMEM((n, 4 * n), BF16),
            pltpu.VMEM((n, n), F32),
            pltpu.VMEM((n, rows), F32),
            pltpu.VMEM((t, rows), F32),
            pltpu.SemaphoreType.DMA((2,)),
            pltpu.VMEM((n + t, 6 * n), BF16),
            pltpu.VMEM((steps, n, OUT_CHUNK), F32),
            pltpu.VMEM((steps, t, OUT_CHUNK), F32),
            pltpu.SemaphoreType.DMA((2, steps)),
        ],
        compiler_params=pltpu.CompilerParams(vmem_limit_bytes=48 << 20),
        name="factor",
    )(core, own, other, panel, trailing)


def shards(panel, trailing):
    n, t = panel.shape[0], trailing.shape[0]
    rows_all = panel.shape[1] * lax.axis_size(AXES)
    core = jnp.reshape(lax.axis_index("gy") % 2, (1,)).astype(jnp.int32)
    words = n // 4 + 8
    panel, trailing = (pltpu.with_memory_space_constraint(a, pltpu.HBM) for a in (panel, trailing))
    keep, send = local_gram(core, panel, trailing)
    total = add_packed(words, keep, exchange(send, 4))
    for masks in ((1, 3, 2), (8, 72, 64), (16, 48, 32)):
        near, wrap, far = (exchange(total, m) for m in masks)
        total = add_packed(words, total, wrap, near, far)
    other = exchange(total, 4)
    basis_t, updated, upper, coupling_t = factor(core, total, other, panel, trailing, rows_all)
    return basis_t, upper, coupling_t.T, updated


def solution(mesh):
    placed = (P(None, AXES), P(None, AXES))
    return jax.shard_map(
        shards,
        mesh=mesh,
        in_specs=placed,
        out_specs=(P(None, AXES), P(), P(), P(None, AXES)),
        check_vma=False,
    )
```

```python
import jax
import jax.numpy as jnp
from jax import lax
from jax.experimental import pallas as pl
from jax.experimental.pallas import tpu as pltpu
from jax.sharding import PartitionSpec as P

AXES = ("gx", "gy", "gz")
HIGHEST = lax.Precision.HIGHEST
F32 = jnp.float32
BF16 = jnp.bfloat16
CHUNKS = 4
OUT_CHUNK = 512
NEAR = 4
SMALL = 2e-2
MAGIC = 1.5 * 2.0**23


def round_int(x):
    return (x + MAGIC) - MAGIC


def two_sum(a, b):
    total = a + b
    part = total - a
    return total, (a - (total - part)) + (b - part)


def snap(x):
    c = x * (2.0**23 + 1.0)
    return c - (c - x)


def power_near(x):
    p = snap(jnp.maximum(x, 1e-30))
    return p, snap(1.0 / p)


def slices(hi, lo, count):
    digits = []
    for k in range(count):
        d = round_int(hi)
        digits.append(d)
        if k < count - 1:
            hi = (hi - d) * 256.0
            if lo is not None:
                lo = lo * 256.0
                new = hi + lo
                lo = lo - (new - hi)
                hi = new
    return digits


def nt(a, b, **kw):
    return lax.dot_general(a, b, (((1,), (1,)), ((), ())), preferred_element_type=F32, **kw)


def nn(a, b, **kw):
    return lax.dot_general(a, b, (((1,), (0,)), ((), ())), preferred_element_type=F32, **kw)


def iota(shape, axis):
    return lax.broadcasted_iota(jnp.int32, shape, axis)


def gram_kernel(core_ref, panel, trail, keep_ref, send_ref, pbuf, tbuf, ops, sems):
    n, rows = panel.shape
    t = trail.shape[0]
    width = rows // CHUNKS
    copies = []
    for k in range(CHUNKS):
        at = pl.ds(k * width, width)
        pair = (
            pltpu.make_async_copy(panel.at[:, at], pbuf.at[k], sems.at[0, k]),
            pltpu.make_async_copy(trail.at[:, at], tbuf.at[k], sems.at[1, k]),
        )
        copies.append(pair)
    for which in range(2):
        for pair in copies:
            pair[which].start()

    top = jnp.zeros((n, 128), F32)
    for k in range(CHUNKS):
        copies[k][0].wait()
        x = jnp.abs(pbuf[k])
        for q in range(0, width, 128):
            top = jnp.maximum(top, x[:, q : q + 128])
    p, inv = power_near(jnp.max(top, axis=1, keepdims=True))
    for k in range(CHUNKS):
        copies[k][1].wait()

    def split(k):
        a = pbuf[k] * (inv * 32.0)
        d1 = round_int(a)
        r1 = (a - d1) * 256.0
        d2 = round_int(r1)
        d3 = (r1 - d2) * 256.0
        c = tbuf[k]
        c1 = c.astype(BF16)
        rc = c - c1.astype(F32)
        c2 = rc.astype(BF16)
        c3 = rc - c2.astype(F32)
        at = 0
        for part in (c3, d1, d2, d3, c1, c2):
            ops[k, at : at + part.shape[0], :] = part.astype(BF16)
            at += part.shape[0]

    left, right = None, None
    split(0)
    for k in range(CHUNKS):
        if k + 1 < CHUNKS:
            split(k + 1)
        l = nt(ops[k, 0 : t + 2 * n, :], ops[k, t : t + 2 * n, :])
        r = nt(ops[k, t : t + 3 * n, :], ops[k, t + 2 * n :, :])
        left, right = (l, r) if left is None else (left + l, right + r)

    c3d1, left = left[:t, :n], left[t:, :]
    row = jnp.broadcast_to(p * (1.0 / 32.0), (n, n))
    col = row.T
    scale = row * col
    h, e = two_sum(left[:n, :n], (left[:n, n:] + left[n:, :n]) * 2.0**-8)
    e = e + (left[n:, n:] * 2.0**-16 + right[2 * n :, :n] * 2.0**-32)
    mix = right[:n, :n] * 2.0**-16 + right[n : 2 * n, :n] * 2.0**-24
    ac = right[2 * n :, n : n + t] * 2.0**-16 + right[n : 2 * n, n + t :] * 2.0**-8
    ac = ac + (right[n : 2 * n, n : n + t] * 2.0**-8 + right[:n, n + t :])
    ca = (c3d1 + (ac + right[:n, n : n + t]).T) * col[:t, :]

    core = core_ref[0]
    half = n // 2
    i, j = iota((half, n), 0), iota((half, n), 1)

    def fold(g):
        top, bottom = g[:half, :], g[half:, :]
        body = jnp.where((j >= half) & (i >= j - half), pltpu.roll(top, half, 1), bottom)
        diag = jnp.sum(jnp.where(i == j - half, bottom, 0.0), axis=0, keepdims=True)
        return body, jnp.broadcast_to(diag, (8, n))

    hi, lo = two_sum(h * scale, (e + (mix + mix.T)) * scale)
    hi_body, hi_diag = fold(hi)
    lo_body, lo_diag = fold(lo)
    q = half // 2
    tq = t // 2

    def put(ref, first):
        def pick(v, size):
            return jnp.where(first, v[:size, :], v[size:, :])

        ref[0:q, :] = pick(hi_body, q)
        ref[q : q + 8, :] = hi_diag
        ref[q + 8 : 2 * q + 8, :] = pick(lo_body, q)
        ref[2 * q + 8 : 2 * q + 16, :] = lo_diag
        ref[2 * q + 16 :, :] = pick(ca, tq)

    put(keep_ref, core == 0)
    put(send_ref, core == 1)


def local_gram(core, panel, trailing):
    n, rows = panel.shape
    t = trailing.shape[0]
    width = rows // CHUNKS
    out = jax.ShapeDtypeStruct((n // 2 + 16 + t // 2, n), F32)
    vmem, hbm = pl.BlockSpec(memory_space=pltpu.VMEM), pl.BlockSpec(memory_space=pltpu.HBM)
    return pl.pallas_call(
        gram_kernel,
        in_specs=[pl.BlockSpec(memory_space=pltpu.SMEM), hbm, hbm],
        out_specs=[vmem, vmem],
        out_shape=[out, out],
        scratch_shapes=[
            pltpu.VMEM((CHUNKS, n, width), F32),
            pltpu.VMEM((CHUNKS, t, width), F32),
            pltpu.VMEM((CHUNKS, 3 * (n + t), width), BF16),
            pltpu.SemaphoreType.DMA((2, CHUNKS)),
        ],
        compiler_params=pltpu.CompilerParams(vmem_limit_bytes=32 << 20),
        name="gram",
    )(core, panel, trailing)


def add_packed(words, *arrays):
    parts, errors = list(arrays), []
    while len(parts) > 1:
        pairs = []
        for a, b in zip(parts[::2], parts[1::2]):
            errors.append(two_sum(a[:words], b[:words])[1])
            pairs.append(a + b)
        parts = pairs
    error = errors[0] if len(errors) == 1 else (errors[0] + errors[1]) + errors[2]
    rest = parts[0].shape[0] - 2 * words
    return parts[0] + jnp.pad(error, ((words, rest), (0, 0)))


def exchange(value, mask):
    size = lax.axis_size(AXES)
    return lax.ppermute(value, AXES, [(s, s ^ mask) for s in range(size)])


def split3(x):
    x1 = x.astype(BF16)
    rest = x - x1.astype(F32)
    x2 = rest.astype(BF16)
    return x1, x2, (rest - x2.astype(F32)).astype(BF16)


def chol_inv(s):
    blocks = len(s)
    n = 8 * blocks
    rid, lid = iota((8, n), 0), iota((8, n), 1)
    s, w = list(s), [jnp.where(lid == rid + 8 * r, 1.0, 0.0) for r in range(blocks)]

    def spread(r, first):
        return [jnp.broadcast_to(s[r][:, first + k : first + k + 1], (8, n)) for k in range(8)]

    cols = {r: spread(r, 0) for r in (0, 1)}
    for r0 in range(blocks):
        first = 8 * r0
        near = range(r0, min(r0 + 3, blocks))
        for r in near:
            if r not in cols:
                cols[r] = spread(r, first)
        ahead = {r: spread(r, first + 8) for r in near if r > r0}
        edges, invs, srows, wrows, scales = {}, [], [], [], []
        inv_rows = jnp.zeros((8, n), F32)
        for k in range(8):
            pivot = cols[r0][k][k : k + 1, :]
            inv = 1.0 / pivot
            mult = {r: cols[r][k] * inv for r in near}
            mult[r0] = jnp.where(rid > k, mult[r0], 0.0)
            for later in range(k + 1, 8):
                edges[k, later] = edge = cols[r0][later][k : k + 1, :]
                for r in near:
                    cols[r][later] = cols[r][later] - mult[r] * edge
            if ahead:
                for q in range(8):
                    edge = cols[r0 + 1][k][q : q + 1, :]
                    for r in ahead:
                        ahead[r][q] = ahead[r][q] - mult[r] * edge
            srow, wrow = s[r0][k : k + 1, :], w[r0][k : k + 1, :]
            for r in near:
                s[r] = s[r] - mult[r] * srow
                w[r] = w[r] - mult[r] * wrow
            inv_rows = jnp.where(rid == k, inv, inv_rows)
            invs.append(inv)
            srows.append(srow)
            wrows.append(wrow)
            scales.append(lax.rsqrt(pivot))
        for r in range(r0 + 3, min(r0 + NEAR, blocks)):
            col = spread(r, first)
            for k in range(8):
                mult = col[k] * invs[k]
                for later in range(k + 1, 8):
                    col[later] = col[later] - mult * edges[k, later]
                s[r] = s[r] - mult * srows[k]
                w[r] = w[r] - mult * wrows[k]
        if r0 + NEAR < blocks:
            l1, l2, l3 = split3(s[r0] * inv_rows)
            r1, r2, r3 = split3(jnp.concatenate([s[r0], w[r0]], axis=1))

            def stack(*parts):
                return jnp.concatenate([p.astype(F32) for p in parts], axis=0).astype(BF16)

            left, right = stack(l1, l2, l1, l2, l1, l3), stack(r1, r2, r2, r1, r3, r1)
            update = lax.dot_general(left, right, (((0,), (0,)), ((), ())), preferred_element_type=F32)
            for r in range(r0 + NEAR, blocks):
                s[r] = s[r] - update[8 * r : 8 * r + 8, :n]
                w[r] = w[r] - update[8 * r : 8 * r + 8, n:]
        for k, d in enumerate(scales):
            w[r0] = jnp.where(rid == k, w[r0] * d, w[r0])
        cols = ahead
    return w


def apply_factors(wz, scale, panel, trailing, basis, updated, words, basis_buf, updated_buf, sems):
    n, rows = panel.shape
    w1, w2, w3 = split3(wz)
    for k, w in enumerate((w1, w2, w1, w2, w1, w3)):
        words[:, k * n : (k + 1) * n] = w
    copies = []
    for k in range(rows // OUT_CHUNK):
        at = pl.ds(k * OUT_CHUNK, OUT_CHUNK)
        a1, a2, a3 = split3(panel[:, at])
        out = nn(words[...], jnp.concatenate([a1, a2, a2, a1, a3, a1], axis=0))
        basis_buf[k] = out[:n, :] * scale
        updated_buf[k] = trailing[:, at] - out[n:, :]
        for copy in (
            pltpu.make_async_copy(basis_buf.at[k], basis.at[:, at], sems.at[0, k]),
            pltpu.make_async_copy(updated_buf.at[k], updated.at[:, at], sems.at[1, k]),
        ):
            copy.start()
            copies.append(copy)
    for copy in copies:
        copy.wait()


def factor_kernel(
    rows_all, core_ref, own_ref, other_ref, panel, trailing, basis, updated, upper, coup,
    upper_ref, coup_ref, small_sems, wcat, gcat, tcat, v_ref, panel_buf, trail_buf, in_sems, words, basis_buf, updated_buf, out_sems,
):
    loads = (
        pltpu.make_async_copy(panel, panel_buf, in_sems.at[0]),
        pltpu.make_async_copy(trailing, trail_buf, in_sems.at[1]),
    )
    for load in loads:
        load.start()
    n = upper_ref.shape[0]
    t = coup_ref.shape[0]
    half, q, tq = n // 2, n // 4, t // 2
    first = core_ref[0] == 0
    own, other = own_ref[...], other_ref[...]
    a, b = jnp.where(first, own, other), jnp.where(first, other, own)
    i, j = iota((n, n), 0), iota((n, n), 1)
    hi_, hj_ = iota((half, n), 0), iota((half, n), 1)

    def unfold(packed, diag_row):
        diag = jnp.broadcast_to(diag_row, (half, n))
        top = jnp.where((hj_ < half) & (hi_ >= hj_), pltpu.roll(packed, half, 1), 0.0)
        keep = jnp.where((hj_ < half) | (hi_ < hj_ - half), packed, 0.0)
        bottom = jnp.where(hi_ == hj_ - half, diag, keep)
        part = jnp.concatenate([top, bottom], axis=0)
        return jnp.where(i == j, part, part + part.T)

    def packed(start):
        return jnp.concatenate([a[start : start + q, :], b[start : start + q, :]], axis=0), a[start + q : start + q + 1, :]

    hi_body, hi_diag = packed(0)
    lo_body, lo_diag = packed(q + 8)
    ca = jnp.concatenate([a[2 * q + 16 :, :], b[2 * q + 16 :, :]], axis=0)
    hi_body, lo_body = two_sum(hi_body, lo_body)
    hi_diag, lo_diag = two_sum(hi_diag, lo_diag)
    g_hi, g_lo = unfold(hi_body, hi_diag), unfold(lo_body, lo_diag)
    w = jnp.concatenate(chol_inv([g_hi[8 * r : 8 * r + 8, :] for r in range(n // 8)]), axis=0)

    diag = jnp.sum(jnp.where(i == j, g_hi, 0.0), axis=0, keepdims=True)
    pc, inv_pc = power_near(jnp.sqrt(diag))
    ic = jnp.broadcast_to(inv_pc, (n, n))
    eq = ic * ic.T
    s_hi, s_lo = g_hi * eq, g_lo * eq
    w = w * jnp.broadcast_to(pc, (n, n))

    qr, inv_qr = power_near(jnp.max(jnp.abs(w), axis=1, keepdims=True))
    wd = slices(w * (inv_qr * 64.0), None, 3)
    qs = qr * (1.0 / 64.0)
    wt = (wd[0] + wd[1] * 2.0**-8 + wd[2] * 2.0**-16) * qs
    for k in range(3):
        wcat[:, k * n : (k + 1) * n] = wd[k].astype(BF16)
    gd = slices(s_hi * 32.0, s_lo * 32.0, 6)
    for k in range(6):
        gcat[(5 - k) * n : (6 - k) * n, :] = gd[k].astype(BF16)

    def weigh(parts):
        hi, lo = parts[0], None
        for k, part in enumerate(parts[1:]):
            hi, err = two_sum(hi, part * 2.0 ** (-8 * (k + 1)))
            lo = err if lo is None else lo + err
        return two_sum(hi, lo)

    def t_level(k):
        width = min(k + 1, 3) * n
        return nn(wcat[:, 0:width], gcat[(5 - k) * n : (5 - k) * n + width, :])

    t_hi, t_lo = weigh([t_level(k) for k in range(6)])
    tau, inv_tau = power_near(jnp.max(jnp.abs(t_hi), axis=1, keepdims=True))
    td = slices(t_hi * (inv_tau * 64.0), t_lo * (inv_tau * 64.0), 4)
    for k in range(4):
        tcat[:, (3 - k) * n : (4 - k) * n] = td[k].astype(BF16)

    def m_level(k):
        width = min(k + 1, 3) * n
        return nt(tcat[:, (3 - k) * n : (3 - k) * n + width], wcat[:, 0:width])

    m_hi, m_lo = weigh([m_level(k) for k in range(4)])
    qb = jnp.broadcast_to(qs, (n, n))
    scale = qb.T * (qb * (tau * (1.0 / 2048.0)))
    e = (m_hi * scale - jnp.where(i == j, 1.0, 0.0)) + m_lo * scale

    def phi(x):
        return jnp.where(i > j, x, jnp.where(i == j, 0.5 * x, 0.0))

    f = phi(e)
    size = jnp.sum(f * f)

    @pl.when(size <= SMALL * SMALL)
    def _():
        fb = f.astype(BF16)
        f2, square = -phi(nt(fb, fb)), nn(fb, fb)
        f2b = f2.astype(BF16)
        ab = jnp.concatenate([fb, f2b], axis=1)
        ba = jnp.concatenate([f2b, fb], axis=1)
        third = phi(nt(ab, ba)) + nn(ab, jnp.concatenate([(f2 - square).astype(BF16), fb], axis=0))
        v_ref[...] = (jnp.where(i == j, 1.0, 0.0) - f) + ((square - f2) + third)

    @pl.when(jnp.logical_not(size <= SMALL * SMALL))
    def _():
        lower = jnp.where(i >= j, e, 0.0)
        full = jnp.where(i == j, e + 1.0, lower + lower.T)
        blocks = chol_inv([full[8 * r : 8 * r + 8, :] for r in range(n // 8)])
        for r in range(n // 8):
            v_ref[8 * r : 8 * r + 8, :] = blocks[r]

    v = v_ref[...]
    y = nt(wt, ca * inv_pc, precision=HIGHEST)
    t_true = t_hi * (qs * (1.0 / 32.0)) * jnp.broadcast_to(pc, (n, n))
    wide = nn(v, jnp.concatenate([wt, t_true, y], axis=1), precision=HIGHEST)
    w_new = wide[:, :n] * ic
    root = jnp.sqrt(jnp.float32(rows_all))
    upper_ref[...] = jnp.where(i <= j, wide[:, n : 2 * n] * (1.0 / root), 0.0)
    coupling_t = wide[:, 2 * n :].T
    coup_ref[...] = coupling_t
    stores = (
        pltpu.make_async_copy(upper_ref, upper, small_sems.at[0]),
        pltpu.make_async_copy(coup_ref, coup, small_sems.at[1]),
    )
    for store in stores:
        store.start()
    wz = jnp.concatenate([w_new, nn(coupling_t, w_new, precision=HIGHEST)], axis=0)
    for load in loads:
        load.wait()
    apply_factors(wz, root, panel_buf, trail_buf, basis, updated, words, basis_buf, updated_buf, out_sems)
    for store in stores:
        store.wait()


def factor(core, own, other, panel, trailing, rows_all):
    n, rows = panel.shape
    t = trailing.shape[0]
    steps = rows // OUT_CHUNK
    vmem, hbm = pl.BlockSpec(memory_space=pltpu.VMEM), pl.BlockSpec(memory_space=pltpu.HBM)
    return pl.pallas_call(
        lambda *refs: factor_kernel(rows_all, *refs),
        in_specs=[pl.BlockSpec(memory_space=pltpu.SMEM), vmem, vmem, hbm, hbm],
        out_specs=[hbm] * 4,
        out_shape=[
            jax.ShapeDtypeStruct((n, rows), F32),
            jax.ShapeDtypeStruct((t, rows), F32),
            jax.ShapeDtypeStruct((n, n), F32),
            jax.ShapeDtypeStruct((t, n), F32),
        ],
        scratch_shapes=[
            pltpu.VMEM((n, n), F32),
            pltpu.VMEM((t, n), F32),
            pltpu.SemaphoreType.DMA((2,)),
            pltpu.VMEM((n, 3 * n), BF16),
            pltpu.VMEM((6 * n, n), BF16),
            pltpu.VMEM((n, 4 * n), BF16),
            pltpu.VMEM((n, n), F32),
            pltpu.VMEM((n, rows), F32),
            pltpu.VMEM((t, rows), F32),
            pltpu.SemaphoreType.DMA((2,)),
            pltpu.VMEM((n + t, 6 * n), BF16),
            pltpu.VMEM((steps, n, OUT_CHUNK), F32),
            pltpu.VMEM((steps, t, OUT_CHUNK), F32),
            pltpu.SemaphoreType.DMA((2, steps)),
        ],
        compiler_params=pltpu.CompilerParams(vmem_limit_bytes=48 << 20),
        name="factor",
    )(core, own, other, panel, trailing)


def shards(panel, trailing):
    n, t = panel.shape[0], trailing.shape[0]
    rows_all = panel.shape[1] * lax.axis_size(AXES)
    core = jnp.reshape(lax.axis_index("gy") % 2, (1,)).astype(jnp.int32)
    words = n // 4 + 8
    panel, trailing = (pltpu.with_memory_space_constraint(a, pltpu.HBM) for a in (panel, trailing))
    keep, send = local_gram(core, panel, trailing)
    total = add_packed(words, keep, exchange(send, 4))
    for masks in ((1, 3, 2), (8, 72, 64), (16, 48, 32)):
        near, wrap, far = (exchange(total, m) for m in masks)
        total = add_packed(words, total, wrap, near, far)
    other = exchange(total, 4)
    basis_t, updated, upper, coupling_t = factor(core, total, other, panel, trailing, rows_all)
    return basis_t, upper, coupling_t.T, updated


def solution(mesh):
    placed = (P(None, AXES), P(None, AXES))
    return jax.shard_map(
        shards,
        mesh=mesh,
        in_specs=placed,
        out_specs=(P(None, AXES), P(), P(), P(None, AXES)),
        check_vma=False,
    )
```
